512 devices in a mesh: space: 32 (over z, y_lo), chan: 16 (over x, y_hi, core).
Axes of the slice: x: 4, y: 8 (y_hi: 2, y_lo: 4; y = y_hi * 4 + y_lo), z: 8, core: 2. Of those that a mesh axis runs over, the one named last changes fastest.
Arguments:
- frames: bfloat16 [4, 48, 320, 512], P(None, None, 'space', 'chan'), may hold values from -120 to 120
- cache: bfloat16 [2, 48, 320, 512], P(None, None, 'space', 'chan'), may hold values from -6 to 6
- gamma: float32 [512], P('chan'), may hold values from 0.5 to 2
- beta: float32 [512], P('chan'), may hold values from -3 to 3
- kernel: bfloat16 [3, 3, 3, 512, 512], P(None, None, None, 'chan'), may hold values from -0.0546875 to 0.0546875
- bias: float32 [512], P('chan'), may hold values from -3 to 3
Outputs:
- output: bfloat16 [4, 48, 320, 512], P(None, None, 'space', 'chan')
The draws below stay inside these ranges and needn't reach their ends.
All inputs are finite; a program needn't handle non-finite values.
Results may differ from the reference program's by a relative error of at most 0.004.
Values may be sent and summed in bfloat16 or wider, within the bound.
A program may use at most 192 MiB of HBM per device.

```python
import math
import jax
import jax.numpy as jnp
from jax import lax

CH = 512
COUT = 512
GROUPS = 32
ROWS = 48
FRAMES = 4
CACHE = 2
WIDTH = 320


def draw_frames(key, part):
    key_offset, key_rough, key_base = jax.random.split(key, 3)
    full_shape = (FRAMES, ROWS, WIDTH, CH)
    position = jnp.arange(WIDTH, dtype=jnp.float32) / max(WIDTH - 1, 1)
    colscale = jnp.exp(math.log(3.0) * position)
    offset = jax.random.uniform(key_offset, (CH,), jnp.float32, 0.5, 1.5)
    roughness = jax.random.uniform(key_rough, full_shape, jnp.float32, 0.5, 2.0)
    pattern = jnp.clip(jax.random.normal(key_base, full_shape, jnp.float32), -6.0, 6.0)
    rowscale = jnp.ones((ROWS,), jnp.float32)
    ramp = jnp.exp(math.log(10.0) * (position - 0.5))
    level = offset[None, :] * ramp[:, None]
    values = level[None, None, :, :] + colscale[None, None, :, None] * rowscale[None, :, None, None] * roughness * pattern
    return values.astype(jnp.bfloat16)


def block_scale(stream_key, extent, cuts, least, top_value):
    level, own = 1.0, jax.random.fold_in(stream_key, 6)
    for axis_at, parts in cuts:
        draws = jnp.exp(jax.random.uniform(jax.random.fold_in(own, axis_at), (parts,), jnp.float32, least / len(cuts), top_value / len(cuts)))
        level = level * jnp.repeat(draws, extent[axis_at] // parts).reshape([-1 if axis == axis_at else 1 for axis in range(len(extent))])
    return level


def noise(stream_key, extent, scale, bound, shards=(), kind=jnp.bfloat16):
    entries = scale * jax.random.normal(stream_key, extent, jnp.float32)
    if shards:
        entries = entries * block_scale(stream_key, extent, shards, -0.22, 0.18)
    return jnp.clip(entries, -bound, bound).astype(kind)


def setup_inputs(seed: int = 0) -> dict:
    splits = jax.random.split(jax.random.key(seed), 7)
    return {
        "frames": draw_frames(jax.random.fold_in(splits[6], 71), 0),
        "cache": noise(splits[1], (CACHE, ROWS, WIDTH, CH), 1.0, 6.0, ((2, 32), (3, 16))),
        "gamma": jnp.clip(jnp.exp(math.log(2.0) - 1.3862944 * jax.random.uniform(splits[2], (CH,), jnp.float32) ** block_scale(splits[2], (CH,), ((0, 16),), -0.2, 0.2)), 0.5, 2.0),
        "beta": noise(splits[3], (CH,), 0.5, 3.0, ((0, 16),), jnp.float32),
        "kernel": noise(splits[4], (3, 3, 3, CH, COUT), (27 * CH) ** -0.5, 0.0546875, ((3, 16),)),
        "bias": noise(splits[5], (COUT,), 0.5, 3.0, ((0, 16),), jnp.float32),
    }


epsilon = 1e-06

def reference(frames, cache, gamma, beta, kernel, bias):
    group_size = CH // GROUPS
    values = frames.astype(jnp.float32).reshape(FRAMES, ROWS, WIDTH, GROUPS, group_size)
    group_mean = lax.optimization_barrier(jnp.mean(values, axis=(0, 1, 2, 4)))
    centred = values - group_mean[:, None]
    group_var = lax.optimization_barrier(jnp.mean(centred * centred, axis=(0, 1, 2, 4)))
    scaled = centred * lax.rsqrt(group_var + epsilon)[:, None]
    normed = scaled.reshape(FRAMES, ROWS, WIDTH, CH) * gamma + beta
    active = jax.nn.silu(normed).astype(jnp.bfloat16)
    joined = jnp.concatenate([cache, active], axis=0)
    padded = jnp.pad(joined, ((0, 0), (1, 1), (1, 1), (0, 0)))
    running = jnp.zeros((FRAMES * ROWS * WIDTH, COUT), jnp.float32)
    for depth in range(3):
        for row_tap in range(3):
            for col_tap in range(3):
                window = padded[depth:depth + FRAMES, row_tap:row_tap + ROWS, col_tap:col_tap + WIDTH, :]
                window = window.reshape(FRAMES * ROWS * WIDTH, CH).astype(jnp.float32)
                weights = kernel[depth, row_tap, col_tap].astype(jnp.float32)
                running = running + jnp.dot(window, weights, precision=lax.Precision.HIGHEST, preferred_element_type=jnp.float32)
    result = running + bias
    return result.astype(jnp.bfloat16).reshape(FRAMES, ROWS, WIDTH, COUT)
```

```python
import functools

import jax
import jax.numpy as jnp
from jax import lax
from jax.experimental import pallas as pl
from jax.experimental.pallas import tpu as pltpu
from jax.sharding import PartitionSpec as P

CH = 512
GROUPS = 32
MESH = pl.DeviceIdType.MESH

epsilon = 1e-06


def gather_kernel(n, x_ref, o_ref, buf, send_sem, recv_sem):
    me = lax.axis_index("space")
    ch = lax.axis_index("chan")
    barrier = pltpu.get_barrier_semaphore()

    def signal(k, carry):
        peer = lax.rem(me + k, n)
        pl.semaphore_signal(barrier, 1, device_id=(peer, ch), device_id_type=MESH)
        return carry

    lax.fori_loop(1, n, signal, 0)
    pl.semaphore_wait(barrier, n - 1)

    def copy_to(peer):
        return pltpu.make_async_remote_copy(
            src_ref=x_ref,
            dst_ref=buf.at[me],
            send_sem=send_sem.at[peer],
            recv_sem=recv_sem.at[me],
            device_id=(peer, ch),
            device_id_type=MESH,
        )

    def copy_from(peer):
        return pltpu.make_async_remote_copy(
            src_ref=x_ref,
            dst_ref=buf.at[peer],
            send_sem=send_sem.at[peer],
            recv_sem=recv_sem.at[peer],
            device_id=(peer, ch),
            device_id_type=MESH,
        )

    def start(k, carry):
        copy_to(lax.rem(me + k, n)).start()
        return carry

    lax.fori_loop(1, n, start, 0)

    def finish(k, carry):
        peer = lax.rem(me + k, n)
        copy_to(peer).wait_send()
        copy_from(peer).wait_recv()
        return carry

    lax.fori_loop(1, n, finish, 0)
    buf[me] = x_ref[...]
    o_ref[...] = buf[...]


def gather_space(tile):
    n = lax.axis_size("space")
    return pl.pallas_call(
        functools.partial(gather_kernel, n),
        out_shape=jax.ShapeDtypeStruct((n,) + tile.shape, tile.dtype),
        in_specs=[pl.BlockSpec(memory_space=pltpu.VMEM)],
        out_specs=pl.BlockSpec(memory_space=pltpu.VMEM),
        scratch_shapes=[
            pltpu.VMEM((n,) + tile.shape, tile.dtype),
            pltpu.SemaphoreType.DMA((n,)),
            pltpu.SemaphoreType.DMA((n,)),
        ],
        compiler_params=pltpu.CompilerParams(collective_id=0, has_side_effects=True),
    )(tile)


def edge_exchange(edges_last, edges_first, axis):
    peers = lax.axis_size(axis)
    up = [(i, (i + 1) % peers) for i in range(peers - 1)]
    down = [(j, i) for i, j in up]
    before = lax.ppermute(edges_last, axis, up)
    after = lax.ppermute(edges_first, axis, down)
    return before, after


def unfold_taps(source, row_count, col_count):
    return jnp.concatenate(
        [
            source[:, row_tap : row_tap + row_count, col_tap : col_tap + col_count, :]
            for row_tap in range(3)
            for col_tap in range(3)
        ],
        axis=3,
    )


def local(frames, cache, gamma, beta, kernel, bias):
    nframes, row_count, col_count, local_ch = frames.shape
    ncache = cache.shape[0]
    group_size = CH // GROUPS
    local_groups = local_ch // group_size
    nspace = lax.axis_size("space")
    me = lax.axis_index("space")
    local_members = float(nframes * row_count * col_count * group_size)

    raw = jnp.concatenate([cache, frames], axis=0)
    before, after = edge_exchange(raw[:, :, col_count - 1 :], raw[:, :, :1], "space")

    values = frames.astype(jnp.float32).reshape(
        nframes, row_count, col_count, local_groups, group_size
    )
    local_mean = jnp.sum(values, axis=(0, 1, 2, 4)) / local_members
    local_dev = values - local_mean[:, None]
    local_m2 = jnp.sum(local_dev * local_dev, axis=(0, 1, 2, 4))
    tile = jnp.zeros((8, 128), jnp.float32)
    tile = tile.at[0, :local_groups].set(local_mean).at[1, :local_groups].set(local_m2)
    gathered = gather_space(tile)
    means = gathered[:, 0, :local_groups]
    m2s = gathered[:, 1, :local_groups]
    group_mean = jnp.mean(means, axis=0)
    spread = jnp.sum(m2s, axis=0) + local_members * jnp.sum(
        (means - group_mean) ** 2, axis=0
    )
    group_var = spread / (local_members * nspace)
    inv = lax.rsqrt(group_var + epsilon)

    def activate(x):
        shape = x.shape
        v = x.astype(jnp.float32).reshape(shape[:-1] + (local_groups, group_size))
        scaled = (v - group_mean[:, None]) * inv[:, None]
        normed = scaled.reshape(shape) * gamma + beta
        return jax.nn.silu(normed).astype(jnp.bfloat16)

    active = activate(frames)
    joined = jnp.concatenate([cache, active], axis=0)
    left = jnp.concatenate([before[:ncache], activate(before[ncache:])], axis=0)
    right = jnp.concatenate([after[:ncache], activate(after[ncache:])], axis=0)
    left = jnp.where(me == 0, jnp.zeros_like(left), left)
    right = jnp.where(me == nspace - 1, jnp.zeros_like(right), right)
    bordered = jnp.concatenate([left, joined, right], axis=2)
    bordered = jnp.pad(bordered, ((0, 0), (1, 1), (0, 0), (0, 0)))
    cell_count = nframes * row_count * col_count
    columns_in = unfold_taps(bordered, row_count, col_count)
    tap_width = columns_in.shape[3]
    flat_kernel = kernel.reshape(3, tap_width, kernel.shape[4])
    running = jnp.zeros((bias.shape[0] * lax.axis_size("chan"), cell_count), jnp.float32)
    for depth in range(3):
        tap_weight = flat_kernel[depth]
        window = columns_in[depth : depth + nframes].reshape(cell_count, tap_width)
        running = running + lax.dot_general(
            tap_weight, window, (((0,), (1,)), ((), ())), preferred_element_type=jnp.float32
        )
    summed = lax.psum_scatter(running, "chan", scatter_dimension=0, tiled=True)
    result = summed.T + bias
    return result.astype(jnp.bfloat16).reshape(nframes, row_count, col_count, -1)


def solution(mesh):
    placed = (
        P(None, None, "space", "chan"),
        P(None, None, "space", "chan"),
        P("chan"),
        P("chan"),
        P(None, None, None, "chan", None),
        P("chan"),
    )
    return jax.shard_map(
        local, mesh=mesh, in_specs=placed, out_specs=P(None, None, "space", "chan"), check_vma=False
    )
```

```python
import functools

import jax
import jax.numpy as jnp
from jax import lax
from jax.experimental import pallas as pl
from jax.experimental.pallas import tpu as pltpu
from jax.sharding import PartitionSpec as P

CH = 512
GROUPS = 32
MESH = pl.DeviceIdType.MESH

epsilon = 1e-06


def gather_kernel(n, x_ref, o_ref, buf, send_sem, recv_sem):
    me = lax.axis_index("space")
    ch = lax.axis_index("chan")
    barrier = pltpu.get_barrier_semaphore()

    def signal(k, carry):
        peer = lax.rem(me + k, n)
        pl.semaphore_signal(barrier, 1, device_id=(peer, ch), device_id_type=MESH)
        return carry

    lax.fori_loop(1, n, signal, 0)
    pl.semaphore_wait(barrier, n - 1)

    def copy_to(peer):
        return pltpu.make_async_remote_copy(
            src_ref=x_ref,
            dst_ref=buf.at[me],
            send_sem=send_sem.at[peer],
            recv_sem=recv_sem.at[me],
            device_id=(peer, ch),
            device_id_type=MESH,
        )

    def copy_from(peer):
        return pltpu.make_async_remote_copy(
            src_ref=x_ref,
            dst_ref=buf.at[peer],
            send_sem=send_sem.at[peer],
            recv_sem=recv_sem.at[peer],
            device_id=(peer, ch),
            device_id_type=MESH,
        )

    def start(k, carry):
        copy_to(lax.rem(me + k, n)).start()
        return carry

    lax.fori_loop(1, n, start, 0)

    def finish(k, carry):
        peer = lax.rem(me + k, n)
        copy_to(peer).wait_send()
        copy_from(peer).wait_recv()
        return carry

    lax.fori_loop(1, n, finish, 0)
    buf[me] = x_ref[...]
    o_ref[...] = buf[...]


def gather_space(tile):
    n = lax.axis_size("space")
    return pl.pallas_call(
        functools.partial(gather_kernel, n),
        out_shape=jax.ShapeDtypeStruct((n,) + tile.shape, tile.dtype),
        in_specs=[pl.BlockSpec(memory_space=pltpu.VMEM)],
        out_specs=pl.BlockSpec(memory_space=pltpu.VMEM),
        scratch_shapes=[
            pltpu.VMEM((n,) + tile.shape, tile.dtype),
            pltpu.SemaphoreType.DMA((n,)),
            pltpu.SemaphoreType.DMA((n,)),
        ],
        compiler_params=pltpu.CompilerParams(collective_id=0, has_side_effects=True),
    )(tile)


def scatter_kernel(x_ref, o_ref, recv1, acc1, recv2, acc2, recv3, send_sem, recv_sem):
    sp = lax.axis_index("space")
    c = lax.axis_index("chan")
    core = c % 2
    yh = (c // 2) % 2
    xx = c // 4
    nx = x_ref.shape[1]

    def dev(x_, yh_, core_):
        return (sp, x_ * 4 + yh_ * 2 + core_)

    peers = [dev(xx, yh, 1 - core)]
    peers += [dev(lax.rem(xx + k, nx), yh, core) for k in range(1, nx)]
    peers += [dev(xx, 1 - yh, core)]
    barrier = pltpu.get_barrier_semaphore()
    for p in peers:
        pl.semaphore_signal(barrier, 1, device_id=p, device_id_type=MESH)
    pl.semaphore_wait(barrier, len(peers))

    first = pltpu.make_async_remote_copy(
        src_ref=x_ref.at[1 - core], dst_ref=recv1, send_sem=send_sem.at[0],
        recv_sem=recv_sem.at[0], device_id=peers[0], device_id_type=MESH)
    first.start()
    first.wait()

    sends = []
    for k in range(1, nx):
        dest = lax.rem(xx + k, nx)
        acc1[dest] = x_ref[core, dest] + recv1[dest]
        slot = nx - 1 - k
        cp = pltpu.make_async_remote_copy(
            src_ref=acc1.at[dest], dst_ref=recv2.at[slot], send_sem=send_sem.at[k],
            recv_sem=recv_sem.at[1 + slot], device_id=peers[k], device_id_type=MESH)
        cp.start()
        sends.append(cp)
    acc1[xx] = x_ref[core, xx] + recv1[xx]
    for slot in range(nx - 1):
        pltpu.make_async_remote_copy(
            src_ref=acc1.at[xx], dst_ref=recv2.at[slot], send_sem=send_sem.at[1 + slot],
            recv_sem=recv_sem.at[1 + slot], device_id=peers[0], device_id_type=MESH).wait_recv()
    other = 1 - yh
    total = acc1[xx, other]
    for slot in range(nx - 1):
        total = total + recv2[slot, other]
    acc2[other] = total
    last = pltpu.make_async_remote_copy(
        src_ref=acc2.at[other], dst_ref=recv3, send_sem=send_sem.at[nx],
        recv_sem=recv_sem.at[nx], device_id=peers[nx], device_id_type=MESH)
    last.start()
    total = acc1[xx, yh]
    for slot in range(nx - 1):
        total = total + recv2[slot, yh]
    for cp in sends:
        cp.wait_send()
    last.wait()
    o_ref[...] = total + recv3[...]


def scatter_chan(parts):
    ncore, nx, nyh, rows, cells = parts.shape
    f32 = jnp.float32
    return pl.pallas_call(
        scatter_kernel,
        out_shape=jax.ShapeDtypeStruct((rows, cells), f32),
        in_specs=[pl.BlockSpec(memory_space=pltpu.VMEM)],
        out_specs=pl.BlockSpec(memory_space=pltpu.VMEM),
        scratch_shapes=[
            pltpu.VMEM((nx, nyh, rows, cells), f32),
            pltpu.VMEM((nx, nyh, rows, cells), f32),
            pltpu.VMEM((nx - 1, nyh, rows, cells), f32),
            pltpu.VMEM((nyh, rows, cells), f32),
            pltpu.VMEM((rows, cells), f32),
            pltpu.SemaphoreType.DMA((nx + 1,)),
            pltpu.SemaphoreType.DMA((nx + 1,)),
        ],
        compiler_params=pltpu.CompilerParams(
            collective_id=1, has_side_effects=True, vmem_limit_bytes=48 * 1024 * 1024),
    )(parts)


def edge_exchange(edges_last, edges_first, axis):
    peers = lax.axis_size(axis)
    up = [(i, (i + 1) % peers) for i in range(peers - 1)]
    down = [(j, i) for i, j in up]
    before = lax.ppermute(edges_last, axis, up)
    after = lax.ppermute(edges_first, axis, down)
    return before, after


def unfold_taps(source, row_count, col_count):
    return jnp.concatenate(
        [
            source[:, row_tap : row_tap + row_count, col_tap : col_tap + col_count, :]
            for row_tap in range(3)
            for col_tap in range(3)
        ],
        axis=3,
    )


def local(frames, cache, gamma, beta, kernel, bias):
    nframes, row_count, col_count, local_ch = frames.shape
    ncache = cache.shape[0]
    group_size = CH // GROUPS
    local_groups = local_ch // group_size
    nspace = lax.axis_size("space")
    me = lax.axis_index("space")
    local_members = float(nframes * row_count * col_count * group_size)

    raw = jnp.concatenate([cache, frames], axis=0)
    before, after = edge_exchange(raw[:, :, col_count - 1 :], raw[:, :, :1], "space")

    values = frames.astype(jnp.float32).reshape(
        nframes, row_count, col_count, local_groups, group_size
    )
    local_mean = jnp.sum(values, axis=(0, 1, 2, 4)) / local_members
    local_dev = values - local_mean[:, None]
    local_m2 = jnp.sum(local_dev * local_dev, axis=(0, 1, 2, 4))
    tile = jnp.zeros((8, 128), jnp.float32)
    tile = tile.at[0, :local_groups].set(local_mean).at[1, :local_groups].set(local_m2)
    gathered = gather_space(tile)
    means = gathered[:, 0, :local_groups]
    m2s = gathered[:, 1, :local_groups]
    group_mean = jnp.mean(means, axis=0)
    spread = jnp.sum(m2s, axis=0) + local_members * jnp.sum(
        (means - group_mean) ** 2, axis=0
    )
    group_var = spread / (local_members * nspace)
    inv = lax.rsqrt(group_var + epsilon)

    def activate(x):
        shape = x.shape
        v = x.astype(jnp.float32).reshape(shape[:-1] + (local_groups, group_size))
        scaled = (v - group_mean[:, None]) * inv[:, None]
        normed = scaled.reshape(shape) * gamma + beta
        return jax.nn.silu(normed).astype(jnp.bfloat16)

    active = activate(frames)
    joined = jnp.concatenate([cache, active], axis=0)
    left = jnp.concatenate([before[:ncache], activate(before[ncache:])], axis=0)
    right = jnp.concatenate([after[:ncache], activate(after[ncache:])], axis=0)
    left = jnp.where(me == 0, jnp.zeros_like(left), left)
    right = jnp.where(me == nspace - 1, jnp.zeros_like(right), right)
    bordered = jnp.concatenate([left, joined, right], axis=2)
    bordered = jnp.pad(bordered, ((0, 0), (1, 1), (0, 0), (0, 0)))
    cell_count = nframes * row_count * col_count
    columns_in = unfold_taps(bordered, row_count, col_count)
    tap_width = columns_in.shape[3]
    nchan = lax.axis_size("chan")
    nx = nchan // 4
    perm_kernel = kernel.reshape(kernel.shape[:4] + (nx, 2, 2, local_ch))
    perm_kernel = perm_kernel.transpose(0, 1, 2, 3, 6, 4, 5, 7)
    flat_kernel = perm_kernel.reshape(3, tap_width, kernel.shape[4])
    running = jnp.zeros((bias.shape[0] * nchan, cell_count), jnp.float32)
    for depth in range(3):
        tap_weight = flat_kernel[depth]
        window = columns_in[depth : depth + nframes].reshape(cell_count, tap_width)
        running = running + lax.dot_general(
            tap_weight, window, (((0,), (1,)), ((), ())), preferred_element_type=jnp.float32
        )
    summed = scatter_chan(running.reshape(2, nx, 2, local_ch, cell_count))
    result = summed.T + bias
    return result.astype(jnp.bfloat16).reshape(nframes, row_count, col_count, -1)


def solution(mesh):
    placed = (
        P(None, None, "space", "chan"),
        P(None, None, "space", "chan"),
        P("chan"),
        P("chan"),
        P(None, None, None, "chan", None),
        P("chan"),
    )
    return jax.shard_map(
        local, mesh=mesh, in_specs=placed, out_specs=P(None, None, "space", "chan"), check_vma=False
    )
```

```python
import functools

import jax
import jax.numpy as jnp
from jax import lax
from jax.experimental import pallas as pl
from jax.experimental.pallas import tpu as pltpu
from jax.sharding import PartitionSpec as P

CH = 512
GROUPS = 32
MESH = pl.DeviceIdType.MESH

epsilon = 1e-06


def gather_kernel(n, x_ref, o_ref, buf, send_sem, recv_sem):
    me = lax.axis_index("space")
    ch = lax.axis_index("chan")
    barrier = pltpu.get_barrier_semaphore()

    def signal(k, carry):
        peer = lax.rem(me + k, n)
        pl.semaphore_signal(barrier, 1, device_id=(peer, ch), device_id_type=MESH)
        return carry

    lax.fori_loop(1, n, signal, 0)
    pl.semaphore_wait(barrier, n - 1)

    def copy_to(peer):
        return pltpu.make_async_remote_copy(
            src_ref=x_ref,
            dst_ref=buf.at[me],
            send_sem=send_sem.at[peer],
            recv_sem=recv_sem.at[me],
            device_id=(peer, ch),
            device_id_type=MESH,
        )

    def copy_from(peer):
        return pltpu.make_async_remote_copy(
            src_ref=x_ref,
            dst_ref=buf.at[peer],
            send_sem=send_sem.at[peer],
            recv_sem=recv_sem.at[peer],
            device_id=(peer, ch),
            device_id_type=MESH,
        )

    def start(k, carry):
        copy_to(lax.rem(me + k, n)).start()
        return carry

    lax.fori_loop(1, n, start, 0)

    def finish(k, carry):
        peer = lax.rem(me + k, n)
        copy_to(peer).wait_send()
        copy_from(peer).wait_recv()
        return carry

    lax.fori_loop(1, n, finish, 0)
    buf[me] = x_ref[...]
    o_ref[...] = buf[...]


def gather_space(tile):
    n = lax.axis_size("space")
    return pl.pallas_call(
        functools.partial(gather_kernel, n),
        out_shape=jax.ShapeDtypeStruct((n,) + tile.shape, tile.dtype),
        in_specs=[pl.BlockSpec(memory_space=pltpu.VMEM)],
        out_specs=pl.BlockSpec(memory_space=pltpu.VMEM),
        scratch_shapes=[
            pltpu.VMEM((n,) + tile.shape, tile.dtype),
            pltpu.SemaphoreType.DMA((n,)),
            pltpu.SemaphoreType.DMA((n,)),
        ],
        compiler_params=pltpu.CompilerParams(collective_id=0, has_side_effects=True),
    )(tile)


def scatter_kernel(x_ref, o_ref, recv1, acc1, recv2, acc2, recv3, send_sem, recv_sem):
    sp = lax.axis_index("space")
    c = lax.axis_index("chan")
    core = c % 2
    yh = (c // 2) % 2
    xx = c // 4
    nx = x_ref.shape[1]

    def dev(x_, yh_, core_):
        return (sp, x_ * 4 + yh_ * 2 + core_)

    peers = [dev(xx, yh, 1 - core)]
    peers += [dev(lax.rem(xx + k, nx), yh, core) for k in range(1, nx)]
    peers += [dev(xx, 1 - yh, core)]
    barrier = pltpu.get_barrier_semaphore()
    for p in peers:
        pl.semaphore_signal(barrier, 1, device_id=p, device_id_type=MESH)
    pl.semaphore_wait(barrier, len(peers))

    first = pltpu.make_async_remote_copy(
        src_ref=x_ref.at[1 - core], dst_ref=recv1, send_sem=send_sem.at[0],
        recv_sem=recv_sem.at[0], device_id=peers[0], device_id_type=MESH)
    first.start()
    first.wait()

    sends = []
    for k in range(1, nx):
        dest = lax.rem(xx + k, nx)
        acc1[dest] = x_ref[core, dest] + recv1[dest]
        slot = nx - 1 - k
        cp = pltpu.make_async_remote_copy(
            src_ref=acc1.at[dest], dst_ref=recv2.at[slot], send_sem=send_sem.at[k],
            recv_sem=recv_sem.at[1 + slot], device_id=peers[k], device_id_type=MESH)
        cp.start()
        sends.append(cp)
    acc1[xx] = x_ref[core, xx] + recv1[xx]
    for slot in range(nx - 1):
        pltpu.make_async_remote_copy(
            src_ref=acc1.at[xx], dst_ref=recv2.at[slot], send_sem=send_sem.at[1 + slot],
            recv_sem=recv_sem.at[1 + slot], device_id=peers[0], device_id_type=MESH).wait_recv()
    other = 1 - yh
    total = acc1[xx, other]
    for slot in range(nx - 1):
        total = total + recv2[slot, other]
    acc2[other] = total
    last = pltpu.make_async_remote_copy(
        src_ref=acc2.at[other], dst_ref=recv3, send_sem=send_sem.at[nx],
        recv_sem=recv_sem.at[nx], device_id=peers[nx], device_id_type=MESH)
    last.start()
    total = acc1[xx, yh]
    for slot in range(nx - 1):
        total = total + recv2[slot, yh]
    for cp in sends:
        cp.wait_send()
    last.wait()
    o_ref[...] = total + recv3[...]


def scatter_chan(parts):
    ncore, nx, nyh, rows, cells = parts.shape
    f32 = jnp.float32
    return pl.pallas_call(
        scatter_kernel,
        out_shape=jax.ShapeDtypeStruct((rows, cells), f32),
        in_specs=[pl.BlockSpec(memory_space=pltpu.VMEM)],
        out_specs=pl.BlockSpec(memory_space=pltpu.VMEM),
        scratch_shapes=[
            pltpu.VMEM((nx, nyh, rows, cells), f32),
            pltpu.VMEM((nx, nyh, rows, cells), f32),
            pltpu.VMEM((nx - 1, nyh, rows, cells), f32),
            pltpu.VMEM((nyh, rows, cells), f32),
            pltpu.VMEM((rows, cells), f32),
            pltpu.SemaphoreType.DMA((nx + 1,)),
            pltpu.SemaphoreType.DMA((nx + 1,)),
        ],
        compiler_params=pltpu.CompilerParams(
            collective_id=1, has_side_effects=True, vmem_limit_bytes=48 * 1024 * 1024),
    )(parts)


def edge_exchange(edges_last, edges_first, axis):
    peers = lax.axis_size(axis)
    up = [(i, (i + 1) % peers) for i in range(peers - 1)]
    down = [(j, i) for i, j in up]
    before = lax.ppermute(edges_last, axis, up)
    after = lax.ppermute(edges_first, axis, down)
    return before, after


def unfold_taps(source, row_count, col_count):
    return jnp.concatenate(
        [
            source[:, row_tap : row_tap + row_count, col_tap : col_tap + col_count, :]
            for row_tap in range(3)
            for col_tap in range(3)
        ],
        axis=3,
    )


def local(frames, cache, gamma, beta, kernel, bias):
    nframes, row_count, col_count, local_ch = frames.shape
    ncache = cache.shape[0]
    group_size = CH // GROUPS
    local_groups = local_ch // group_size
    nspace = lax.axis_size("space")
    me = lax.axis_index("space")
    local_members = float(nframes * row_count * col_count * group_size)

    raw = jnp.concatenate([cache, frames], axis=0)
    before, after = edge_exchange(raw[:, :, col_count - 1 :], raw[:, :, :1], "space")

    values = frames.astype(jnp.float32).reshape(
        nframes, row_count, col_count, local_groups, group_size
    )
    local_mean = jnp.sum(values, axis=(0, 1, 2, 4)) / local_members
    local_dev = values - local_mean[:, None]
    local_m2 = jnp.sum(local_dev * local_dev, axis=(0, 1, 2, 4))
    tile = jnp.zeros((8, 128), jnp.float32)
    tile = tile.at[0, :local_groups].set(local_mean).at[1, :local_groups].set(local_m2)
    gathered = gather_space(tile)
    means = gathered[:, 0, :local_groups]
    m2s = gathered[:, 1, :local_groups]
    group_mean = jnp.mean(means, axis=0)
    spread = jnp.sum(m2s, axis=0) + local_members * jnp.sum(
        (means - group_mean) ** 2, axis=0
    )
    group_var = spread / (local_members * nspace)
    inv = lax.rsqrt(group_var + epsilon)

    def activate(x):
        shape = x.shape
        v = x.astype(jnp.float32).reshape(shape[:-1] + (local_groups, group_size))
        scaled = (v - group_mean[:, None]) * inv[:, None]
        normed = scaled.reshape(shape) * gamma + beta
        return jax.nn.silu(normed).astype(jnp.bfloat16)

    active = activate(frames)
    joined = jnp.concatenate([cache, active], axis=0)
    left = jnp.concatenate([before[:ncache], activate(before[ncache:])], axis=0)
    right = jnp.concatenate([after[:ncache], activate(after[ncache:])], axis=0)
    left = jnp.where(me == 0, jnp.zeros_like(left), left)
    right = jnp.where(me == nspace - 1, jnp.zeros_like(right), right)
    bordered = jnp.concatenate([left, joined, right], axis=2)
    bordered = jnp.pad(bordered, ((0, 0), (1, 1), (0, 0), (0, 0)))
    cell_count = nframes * row_count * col_count
    nchan = lax.axis_size("chan")
    nx = nchan // 4
    perm_kernel = kernel.reshape(kernel.shape[:4] + (nx, 2, 2, local_ch))
    perm_kernel = perm_kernel.transpose(0, 1, 2, 3, 6, 4, 5, 7).reshape(kernel.shape)
    running = lax.conv_general_dilated(
        bordered[None],
        perm_kernel,
        window_strides=(1, 1, 1),
        padding="VALID",
        dimension_numbers=("NDHWC", "DHWIO", "CNDHW"),
        preferred_element_type=jnp.float32,
    )
    running = running.reshape(-1, cell_count)
    summed = scatter_chan(running.reshape(2, nx, 2, local_ch, cell_count))
    result = summed.T + bias
    return result.astype(jnp.bfloat16).reshape(nframes, row_count, col_count, -1)


def solution(mesh):
    placed = (
        P(None, None, "space", "chan"),
        P(None, None, "space", "chan"),
        P("chan"),
        P("chan"),
        P(None, None, None, "chan", None),
        P("chan"),
    )
    return jax.shard_map(
        local, mesh=mesh, in_specs=placed, out_specs=P(None, None, "space", "chan"), check_vma=False
    )
```

```python
import functools

import jax
import jax.numpy as jnp
from jax import lax
from jax.experimental import pallas as pl
from jax.experimental.pallas import tpu as pltpu
from jax.sharding import PartitionSpec as P

CH = 512
GROUPS = 32
MESH = pl.DeviceIdType.MESH

epsilon = 1e-06


def gather_kernel(n, x_ref, o_ref, buf, send_sem, recv_sem):
    me = lax.axis_index("space")
    ch = lax.axis_index("chan")
    barrier = pltpu.get_barrier_semaphore()

    def signal(k, carry):
        peer = lax.rem(me + k, n)
        pl.semaphore_signal(barrier, 1, device_id=(peer, ch), device_id_type=MESH)
        return carry

    lax.fori_loop(1, n, signal, 0)
    pl.semaphore_wait(barrier, n - 1)

    def copy_to(peer):
        return pltpu.make_async_remote_copy(
            src_ref=x_ref,
            dst_ref=buf.at[me],
            send_sem=send_sem.at[peer],
            recv_sem=recv_sem.at[me],
            device_id=(peer, ch),
            device_id_type=MESH,
        )

    def copy_from(peer):
        return pltpu.make_async_remote_copy(
            src_ref=x_ref,
            dst_ref=buf.at[peer],
            send_sem=send_sem.at[peer],
            recv_sem=recv_sem.at[peer],
            device_id=(peer, ch),
            device_id_type=MESH,
        )

    def start(k, carry):
        copy_to(lax.rem(me + k, n)).start()
        return carry

    lax.fori_loop(1, n, start, 0)

    def finish(k, carry):
        peer = lax.rem(me + k, n)
        copy_to(peer).wait_send()
        copy_from(peer).wait_recv()
        return carry

    lax.fori_loop(1, n, finish, 0)
    buf[me] = x_ref[...]
    o_ref[...] = buf[...]


def gather_space(tile):
    n = lax.axis_size("space")
    return pl.pallas_call(
        functools.partial(gather_kernel, n),
        out_shape=jax.ShapeDtypeStruct((n,) + tile.shape, tile.dtype),
        in_specs=[pl.BlockSpec(memory_space=pltpu.VMEM)],
        out_specs=pl.BlockSpec(memory_space=pltpu.VMEM),
        scratch_shapes=[
            pltpu.VMEM((n,) + tile.shape, tile.dtype),
            pltpu.SemaphoreType.DMA((n,)),
            pltpu.SemaphoreType.DMA((n,)),
        ],
        compiler_params=pltpu.CompilerParams(collective_id=0, has_side_effects=True),
    )(tile)


def scatter_kernel(x_ref, o_ref, recv1, acc1, recv2, acc2, recv3, send_sem, recv_sem):
    sp = lax.axis_index("space")
    c = lax.axis_index("chan")
    core = c % 2
    yh = (c // 2) % 2
    xx = c // 4
    nx, nyh = x_ref.shape[0], x_ref.shape[1]
    nfirst = nx * nyh

    def dev(x_, yh_, core_):
        return (sp, x_ * 4 + yh_ * 2 + core_)

    peers = [dev(xx, yh, 1 - core)]
    peers += [dev(lax.rem(xx + k, nx), yh, core) for k in range(1, nx)]
    peers += [dev(xx, 1 - yh, core)]
    barrier = pltpu.get_barrier_semaphore()
    for p in peers:
        pl.semaphore_signal(barrier, 1, device_id=p, device_id_type=MESH)
    pl.semaphore_wait(barrier, len(peers))

    firsts = []
    for i in range(nx):
        for j in range(nyh):
            cp = pltpu.make_async_remote_copy(
                src_ref=x_ref.at[i, j, 1 - core], dst_ref=recv1.at[i, j],
                send_sem=send_sem.at[i * nyh + j], recv_sem=recv_sem.at[i * nyh + j],
                device_id=peers[0], device_id_type=MESH)
            cp.start()
            firsts.append(cp)
    for cp in firsts:
        cp.wait()

    def fold_first(dest):
        for j in range(nyh):
            acc1[dest, j] = x_ref[dest, j, core] + recv1[dest, j]

    sends = []
    for k in range(1, nx):
        dest = lax.rem(xx + k, nx)
        fold_first(dest)
        slot = nx - 1 - k
        cp = pltpu.make_async_remote_copy(
            src_ref=acc1.at[dest], dst_ref=recv2.at[slot], send_sem=send_sem.at[nfirst + k - 1],
            recv_sem=recv_sem.at[nfirst + slot], device_id=peers[k], device_id_type=MESH)
        cp.start()
        sends.append(cp)
    fold_first(xx)
    for slot in range(nx - 1):
        pltpu.make_async_remote_copy(
            src_ref=acc1.at[xx], dst_ref=recv2.at[slot], send_sem=send_sem.at[nfirst + slot],
            recv_sem=recv_sem.at[nfirst + slot], device_id=peers[0], device_id_type=MESH).wait_recv()
    other = 1 - yh
    total = acc1[xx, other]
    for slot in range(nx - 1):
        total = total + recv2[slot, other]
    acc2[other] = total
    last_sem = nfirst + nx - 1
    last = pltpu.make_async_remote_copy(
        src_ref=acc2.at[other], dst_ref=recv3, send_sem=send_sem.at[last_sem],
        recv_sem=recv_sem.at[last_sem], device_id=peers[nx], device_id_type=MESH)
    last.start()
    total = acc1[xx, yh]
    for slot in range(nx - 1):
        total = total + recv2[slot, yh]
    for cp in sends:
        cp.wait_send()
    last.wait()
    o_ref[...] = total + recv3[...]


def scatter_chan(parts):
    nx, nyh, ncore, rows, cells = parts.shape
    f32 = jnp.float32
    return pl.pallas_call(
        scatter_kernel,
        out_shape=jax.ShapeDtypeStruct((rows, cells), f32),
        in_specs=[pl.BlockSpec(memory_space=pltpu.VMEM)],
        out_specs=pl.BlockSpec(memory_space=pltpu.VMEM),
        scratch_shapes=[
            pltpu.VMEM((nx, nyh, rows, cells), f32),
            pltpu.VMEM((nx, nyh, rows, cells), f32),
            pltpu.VMEM((nx - 1, nyh, rows, cells), f32),
            pltpu.VMEM((nyh, rows, cells), f32),
            pltpu.VMEM((rows, cells), f32),
            pltpu.SemaphoreType.DMA((nx * nyh + nx,)),
            pltpu.SemaphoreType.DMA((nx * nyh + nx,)),
        ],
        compiler_params=pltpu.CompilerParams(
            collective_id=1, has_side_effects=True, vmem_limit_bytes=48 * 1024 * 1024),
    )(parts)


def edge_exchange(edges_last, edges_first, axis):
    peers = lax.axis_size(axis)
    up = [(i, (i + 1) % peers) for i in range(peers - 1)]
    down = [(j, i) for i, j in up]
    before = lax.ppermute(edges_last, axis, up)
    after = lax.ppermute(edges_first, axis, down)
    return before, after


def unfold_taps(source, row_count, col_count):
    return jnp.concatenate(
        [
            source[:, row_tap : row_tap + row_count, col_tap : col_tap + col_count, :]
            for row_tap in range(3)
            for col_tap in range(3)
        ],
        axis=3,
    )


def local(frames, cache, gamma, beta, kernel, bias):
    nframes, row_count, col_count, local_ch = frames.shape
    ncache = cache.shape[0]
    group_size = CH // GROUPS
    local_groups = local_ch // group_size
    nspace = lax.axis_size("space")
    me = lax.axis_index("space")
    local_members = float(nframes * row_count * col_count * group_size)

    raw = jnp.concatenate([cache, frames], axis=0)
    before, after = edge_exchange(raw[:, :, col_count - 1 :], raw[:, :, :1], "space")

    values = frames.astype(jnp.float32).reshape(
        nframes, row_count, col_count, local_groups, group_size
    )
    local_mean = jnp.sum(values, axis=(0, 1, 2, 4)) / local_members
    local_dev = values - local_mean[:, None]
    local_m2 = jnp.sum(local_dev * local_dev, axis=(0, 1, 2, 4))
    tile = jnp.zeros((8, 128), jnp.float32)
    tile = tile.at[0, :local_groups].set(local_mean).at[1, :local_groups].set(local_m2)
    gathered = gather_space(tile)
    means = gathered[:, 0, :local_groups]
    m2s = gathered[:, 1, :local_groups]
    group_mean = jnp.mean(means, axis=0)
    spread = jnp.sum(m2s, axis=0) + local_members * jnp.sum(
        (means - group_mean) ** 2, axis=0
    )
    group_var = spread / (local_members * nspace)
    inv = lax.rsqrt(group_var + epsilon)

    def activate(x):
        shape = x.shape
        v = x.astype(jnp.float32).reshape(shape[:-1] + (local_groups, group_size))
        scaled = (v - group_mean[:, None]) * inv[:, None]
        normed = scaled.reshape(shape) * gamma + beta
        return jax.nn.silu(normed).astype(jnp.bfloat16)

    active = activate(frames)
    joined = jnp.concatenate([cache, active], axis=0)
    left = jnp.concatenate([before[:ncache], activate(before[ncache:])], axis=0)
    right = jnp.concatenate([after[:ncache], activate(after[ncache:])], axis=0)
    left = jnp.where(me == 0, jnp.zeros_like(left), left)
    right = jnp.where(me == nspace - 1, jnp.zeros_like(right), right)
    bordered = jnp.concatenate([left, joined, right], axis=2)
    bordered = jnp.pad(bordered, ((0, 0), (1, 1), (0, 0), (0, 0)))
    cell_count = nframes * row_count * col_count
    columns_in = unfold_taps(bordered, row_count, col_count)
    tap_width = columns_in.shape[3]
    nchan = lax.axis_size("chan")
    nx = nchan // 4
    flat_kernel = kernel.reshape(3, tap_width, kernel.shape[4])
    running = jnp.zeros((bias.shape[0] * nchan, cell_count), jnp.float32)
    for depth in range(3):
        tap_weight = flat_kernel[depth]
        window = columns_in[depth : depth + nframes].reshape(cell_count, tap_width)
        running = running + lax.dot_general(
            tap_weight, window, (((0,), (1,)), ((), ())), preferred_element_type=jnp.float32
        )
    summed = scatter_chan(running.reshape(nx, 2, 2, local_ch, cell_count))
    result = summed.T + bias
    return result.astype(jnp.bfloat16).reshape(nframes, row_count, col_count, -1)


def solution(mesh):
    placed = (
        P(None, None, "space", "chan"),
        P(None, None, "space", "chan"),
        P("chan"),
        P("chan"),
        P(None, None, None, "chan", None),
        P("chan"),
    )
    return jax.shard_map(
        local, mesh=mesh, in_specs=placed, out_specs=P(None, None, "space", "chan"), check_vma=False
    )
```

```python
import functools

import jax
import jax.numpy as jnp
from jax import lax
from jax.experimental import pallas as pl
from jax.experimental.pallas import tpu as pltpu
from jax.sharding import PartitionSpec as P

CH = 512
GROUPS = 32
MESH = pl.DeviceIdType.MESH

epsilon = 1e-06


def gather_kernel(n, x_ref, o_ref, buf, send_sem, recv_sem):
    me = lax.axis_index("space")
    ch = lax.axis_index("chan")
    barrier = pltpu.get_barrier_semaphore()

    def signal(k, carry):
        peer = lax.rem(me + k, n)
        pl.semaphore_signal(barrier, 1, device_id=(peer, ch), device_id_type=MESH)
        return carry

    lax.fori_loop(1, n, signal, 0)
    pl.semaphore_wait(barrier, n - 1)

    def copy_to(peer):
        return pltpu.make_async_remote_copy(
            src_ref=x_ref,
            dst_ref=buf.at[me],
            send_sem=send_sem.at[peer],
            recv_sem=recv_sem.at[me],
            device_id=(peer, ch),
            device_id_type=MESH,
        )

    def copy_from(peer):
        return pltpu.make_async_remote_copy(
            src_ref=x_ref,
            dst_ref=buf.at[peer],
            send_sem=send_sem.at[peer],
            recv_sem=recv_sem.at[peer],
            device_id=(peer, ch),
            device_id_type=MESH,
        )

    def start(k, carry):
        copy_to(lax.rem(me + k, n)).start()
        return carry

    lax.fori_loop(1, n, start, 0)

    def finish(k, carry):
        peer = lax.rem(me + k, n)
        copy_to(peer).wait_send()
        copy_from(peer).wait_recv()
        return carry

    lax.fori_loop(1, n, finish, 0)
    buf[me] = x_ref[...]
    o_ref[...] = buf[...]


def gather_space(tile):
    n = lax.axis_size("space")
    return pl.pallas_call(
        functools.partial(gather_kernel, n),
        out_shape=jax.ShapeDtypeStruct((n,) + tile.shape, tile.dtype),
        in_specs=[pl.BlockSpec(memory_space=pltpu.VMEM)],
        out_specs=pl.BlockSpec(memory_space=pltpu.VMEM),
        scratch_shapes=[
            pltpu.VMEM((n,) + tile.shape, tile.dtype),
            pltpu.SemaphoreType.DMA((n,)),
            pltpu.SemaphoreType.DMA((n,)),
        ],
        compiler_params=pltpu.CompilerParams(collective_id=0, has_side_effects=True),
    )(tile)


def scatter_kernel(x_ref, o_ref, recv1, acc1, own, recv2, acc2, recv3, send_sem, recv_sem):
    sp = lax.axis_index("space")
    c = lax.axis_index("chan")
    core = c % 2
    yh = (c // 2) % 2
    xx = c // 4
    nx, nyh = x_ref.shape[0], x_ref.shape[1]
    nfirst = nx * nyh

    def dev(x_, yh_, core_):
        return (sp, x_ * 4 + yh_ * 2 + core_)

    peers = [dev(xx, yh, 1 - core)]
    peers += [dev(lax.rem(xx + k, nx), yh, core) for k in range(1, nx)]
    peers += [dev(xx, 1 - yh, core)]
    barrier = pltpu.get_barrier_semaphore()
    for p in peers:
        pl.semaphore_signal(barrier, 1, device_id=p, device_id_type=MESH)
    pl.semaphore_wait(barrier, len(peers))

    firsts = []
    for i in range(nx):
        for j in range(nyh):
            cp = pltpu.make_async_remote_copy(
                src_ref=x_ref.at[i, j, 1 - core], dst_ref=recv1.at[i, j],
                send_sem=send_sem.at[i * nyh + j], recv_sem=recv_sem.at[i * nyh + j],
                device_id=peers[0], device_id_type=MESH)
            cp.start()
            firsts.append(cp)
    for cp in firsts:
        cp.wait()

    def fold_first(dest, dst):
        for j in range(nyh):
            dst[j] = (x_ref[dest, j, core] + recv1[dest, j]).astype(dst.dtype)

    sends = []
    for k in range(1, nx):
        dest = lax.rem(xx + k, nx)
        fold_first(dest, acc1.at[dest])
        slot = nx - 1 - k
        cp = pltpu.make_async_remote_copy(
            src_ref=acc1.at[dest], dst_ref=recv2.at[slot], send_sem=send_sem.at[nfirst + k - 1],
            recv_sem=recv_sem.at[nfirst + slot], device_id=peers[k], device_id_type=MESH)
        cp.start()
        sends.append(cp)
    fold_first(xx, own)
    for slot in range(nx - 1):
        pltpu.make_async_remote_copy(
            src_ref=acc1.at[xx], dst_ref=recv2.at[slot], send_sem=send_sem.at[nfirst + slot],
            recv_sem=recv_sem.at[nfirst + slot], device_id=peers[0], device_id_type=MESH).wait_recv()
    other = 1 - yh
    total = own[other]
    for slot in range(nx - 1):
        total = total + recv2[slot, other].astype(jnp.float32)
    acc2[...] = total.astype(acc2.dtype)
    last_sem = nfirst + nx - 1
    last = pltpu.make_async_remote_copy(
        src_ref=acc2, dst_ref=recv3, send_sem=send_sem.at[last_sem],
        recv_sem=recv_sem.at[last_sem], device_id=peers[nx], device_id_type=MESH)
    last.start()
    total = own[yh]
    for slot in range(nx - 1):
        total = total + recv2[slot, yh].astype(jnp.float32)
    for cp in sends:
        cp.wait_send()
    last.wait()
    o_ref[...] = total + recv3[...].astype(jnp.float32)


def scatter_chan(parts):
    nx, nyh, ncore, rows, cells = parts.shape
    f32, bf16 = jnp.float32, jnp.bfloat16
    return pl.pallas_call(
        scatter_kernel,
        out_shape=jax.ShapeDtypeStruct((rows, cells), f32),
        in_specs=[pl.BlockSpec(memory_space=pltpu.VMEM)],
        out_specs=pl.BlockSpec(memory_space=pltpu.VMEM),
        scratch_shapes=[
            pltpu.VMEM((nx, nyh, rows, cells), f32),
            pltpu.VMEM((nx, nyh, rows, cells), bf16),
            pltpu.VMEM((nyh, rows, cells), f32),
            pltpu.VMEM((nx - 1, nyh, rows, cells), bf16),
            pltpu.VMEM((rows, cells), bf16),
            pltpu.VMEM((rows, cells), bf16),
            pltpu.SemaphoreType.DMA((nx * nyh + nx,)),
            pltpu.SemaphoreType.DMA((nx * nyh + nx,)),
        ],
        compiler_params=pltpu.CompilerParams(
            collective_id=1, has_side_effects=True, vmem_limit_bytes=48 * 1024 * 1024),
    )(parts)


def edge_exchange(edges_last, edges_first, axis):
    peers = lax.axis_size(axis)
    up = [(i, (i + 1) % peers) for i in range(peers - 1)]
    down = [(j, i) for i, j in up]
    before = lax.ppermute(edges_last, axis, up)
    after = lax.ppermute(edges_first, axis, down)
    return before, after


def unfold_taps(source, row_count, col_count):
    return jnp.concatenate(
        [
            source[:, row_tap : row_tap + row_count, col_tap : col_tap + col_count, :]
            for row_tap in range(3)
            for col_tap in range(3)
        ],
        axis=3,
    )


def local(frames, cache, gamma, beta, kernel, bias):
    nframes, row_count, col_count, local_ch = frames.shape
    ncache = cache.shape[0]
    group_size = CH // GROUPS
    local_groups = local_ch // group_size
    nspace = lax.axis_size("space")
    me = lax.axis_index("space")
    local_members = float(nframes * row_count * col_count * group_size)

    raw = jnp.concatenate([cache, frames], axis=0)
    before, after = edge_exchange(raw[:, :, col_count - 1 :], raw[:, :, :1], "space")

    values = frames.astype(jnp.float32).reshape(
        nframes, row_count, col_count, local_groups, group_size
    )
    local_mean = jnp.sum(values, axis=(0, 1, 2, 4)) / local_members
    local_dev = values - local_mean[:, None]
    local_m2 = jnp.sum(local_dev * local_dev, axis=(0, 1, 2, 4))
    tile = jnp.zeros((8, 128), jnp.float32)
    tile = tile.at[0, :local_groups].set(local_mean).at[1, :local_groups].set(local_m2)
    gathered = gather_space(tile)
    means = gathered[:, 0, :local_groups]
    m2s = gathered[:, 1, :local_groups]
    group_mean = jnp.mean(means, axis=0)
    spread = jnp.sum(m2s, axis=0) + local_members * jnp.sum(
        (means - group_mean) ** 2, axis=0
    )
    group_var = spread / (local_members * nspace)
    inv = lax.rsqrt(group_var + epsilon)

    def activate(x):
        shape = x.shape
        v = x.astype(jnp.float32).reshape(shape[:-1] + (local_groups, group_size))
        scaled = (v - group_mean[:, None]) * inv[:, None]
        normed = scaled.reshape(shape) * gamma + beta
        return jax.nn.silu(normed).astype(jnp.bfloat16)

    active = activate(frames)
    joined = jnp.concatenate([cache, active], axis=0)
    left = jnp.concatenate([before[:ncache], activate(before[ncache:])], axis=0)
    right = jnp.concatenate([after[:ncache], activate(after[ncache:])], axis=0)
    left = jnp.where(me == 0, jnp.zeros_like(left), left)
    right = jnp.where(me == nspace - 1, jnp.zeros_like(right), right)
    bordered = jnp.concatenate([left, joined, right], axis=2)
    bordered = jnp.pad(bordered, ((0, 0), (1, 1), (0, 0), (0, 0)))
    cell_count = nframes * row_count * col_count
    columns_in = unfold_taps(bordered, row_count, col_count)
    tap_width = columns_in.shape[3]
    nchan = lax.axis_size("chan")
    nx = nchan // 4
    flat_kernel = kernel.reshape(3, tap_width, kernel.shape[4])
    running = jnp.zeros((bias.shape[0] * nchan, cell_count), jnp.float32)
    for depth in range(3):
        tap_weight = flat_kernel[depth]
        window = columns_in[depth : depth + nframes].reshape(cell_count, tap_width)
        running = running + lax.dot_general(
            tap_weight, window, (((0,), (1,)), ((), ())), preferred_element_type=jnp.float32
        )
    summed = scatter_chan(running.reshape(nx, 2, 2, local_ch, cell_count))
    result = summed.T + bias
    return result.astype(jnp.bfloat16).reshape(nframes, row_count, col_count, -1)


def solution(mesh):
    placed = (
        P(None, None, "space", "chan"),
        P(None, None, "space", "chan"),
        P("chan"),
        P("chan"),
        P(None, None, None, "chan", None),
        P("chan"),
    )
    return jax.shard_map(
        local, mesh=mesh, in_specs=placed, out_specs=P(None, None, "space", "chan"), check_vma=False
    )
```

```python
import functools

import jax
import jax.numpy as jnp
from jax import lax
from jax.experimental import pallas as pl
from jax.experimental.pallas import tpu as pltpu
from jax.sharding import PartitionSpec as P

CH = 512
GROUPS = 32
MESH = pl.DeviceIdType.MESH

epsilon = 1e-06


def gather_kernel(n, x_ref, o_ref, buf, send_sem, recv_sem):
    me = lax.axis_index("space")
    ch = lax.axis_index("chan")
    barrier = pltpu.get_barrier_semaphore()

    def signal(k, carry):
        peer = lax.rem(me + k, n)
        pl.semaphore_signal(barrier, 1, device_id=(peer, ch), device_id_type=MESH)
        return carry

    lax.fori_loop(1, n, signal, 0)
    pl.semaphore_wait(barrier, n - 1)

    def copy_to(peer):
        return pltpu.make_async_remote_copy(
            src_ref=x_ref,
            dst_ref=buf.at[me],
            send_sem=send_sem.at[peer],
            recv_sem=recv_sem.at[me],
            device_id=(peer, ch),
            device_id_type=MESH,
        )

    def copy_from(peer):
        return pltpu.make_async_remote_copy(
            src_ref=x_ref,
            dst_ref=buf.at[peer],
            send_sem=send_sem.at[peer],
            recv_sem=recv_sem.at[peer],
            device_id=(peer, ch),
            device_id_type=MESH,
        )

    def start(k, carry):
        copy_to(lax.rem(me + k, n)).start()
        return carry

    lax.fori_loop(1, n, start, 0)

    def finish(k, carry):
        peer = lax.rem(me + k, n)
        copy_to(peer).wait_send()
        copy_from(peer).wait_recv()
        return carry

    lax.fori_loop(1, n, finish, 0)
    buf[me] = x_ref[...]
    o_ref[...] = buf[...]


def gather_space(tile):
    n = lax.axis_size("space")
    return pl.pallas_call(
        functools.partial(gather_kernel, n),
        out_shape=jax.ShapeDtypeStruct((n,) + tile.shape, tile.dtype),
        in_specs=[pl.BlockSpec(memory_space=pltpu.VMEM)],
        out_specs=pl.BlockSpec(memory_space=pltpu.VMEM),
        scratch_shapes=[
            pltpu.VMEM((n,) + tile.shape, tile.dtype),
            pltpu.SemaphoreType.DMA((n,)),
            pltpu.SemaphoreType.DMA((n,)),
        ],
        compiler_params=pltpu.CompilerParams(collective_id=0, has_side_effects=True),
    )(tile)


def scatter_kernel(x_ref, o_ref, recv1, acc1, own, recv2, acc2, recv3, send_sem, recv_sem):
    sp = lax.axis_index("space")
    c = lax.axis_index("chan")
    core = c % 2
    yh = (c // 2) % 2
    xx = c // 4
    nx, nyh = x_ref.shape[0], x_ref.shape[1]
    nfirst = nx * nyh

    def dev(x_, yh_, core_):
        return (sp, x_ * 4 + yh_ * 2 + core_)

    peers = [dev(xx, yh, 1 - core)]
    peers += [dev(lax.rem(xx + k, nx), yh, core) for k in range(1, nx)]
    peers += [dev(xx, 1 - yh, core)]
    barrier = pltpu.get_barrier_semaphore()
    for p in peers:
        pl.semaphore_signal(barrier, 1, device_id=p, device_id_type=MESH)
    pl.semaphore_wait(barrier, len(peers))

    firsts = []
    for i in range(nx):
        for j in range(nyh):
            cp = pltpu.make_async_remote_copy(
                src_ref=x_ref.at[i, j, 1 - core], dst_ref=recv1.at[i, j],
                send_sem=send_sem.at[i * nyh + j], recv_sem=recv_sem.at[i * nyh + j],
                device_id=peers[0], device_id_type=MESH)
            cp.start()
            firsts.append(cp)
    for cp in firsts:
        cp.wait()

    def fold_first(dest, dst):
        for j in range(nyh):
            dst[j] = (x_ref[dest, j, core] + recv1[dest, j]).astype(dst.dtype)

    sends = []
    for k in range(1, nx):
        dest = lax.rem(xx + k, nx)
        fold_first(dest, acc1.at[dest])
        slot = nx - 1 - k
        cp = pltpu.make_async_remote_copy(
            src_ref=acc1.at[dest], dst_ref=recv2.at[slot], send_sem=send_sem.at[nfirst + k - 1],
            recv_sem=recv_sem.at[nfirst + slot], device_id=peers[k], device_id_type=MESH)
        cp.start()
        sends.append(cp)
    fold_first(xx, own)
    for slot in range(nx - 1):
        pltpu.make_async_remote_copy(
            src_ref=acc1.at[xx], dst_ref=recv2.at[slot], send_sem=send_sem.at[nfirst + slot],
            recv_sem=recv_sem.at[nfirst + slot], device_id=peers[0], device_id_type=MESH).wait_recv()
    other = 1 - yh
    total = own[other]
    for slot in range(nx - 1):
        total = total + recv2[slot, other].astype(jnp.float32)
    acc2[...] = total.astype(acc2.dtype)
    last_sem = nfirst + nx - 1
    last = pltpu.make_async_remote_copy(
        src_ref=acc2, dst_ref=recv3, send_sem=send_sem.at[last_sem],
        recv_sem=recv_sem.at[last_sem], device_id=peers[nx], device_id_type=MESH)
    last.start()
    total = own[yh]
    for slot in range(nx - 1):
        total = total + recv2[slot, yh].astype(jnp.float32)
    for cp in sends:
        cp.wait_send()
    last.wait()
    o_ref[...] = total + recv3[...].astype(jnp.float32)


def scatter_chan(parts):
    nx, nyh, ncore, rows, cells = parts.shape
    f32, bf16 = jnp.float32, jnp.bfloat16
    return pl.pallas_call(
        scatter_kernel,
        out_shape=jax.ShapeDtypeStruct((rows, cells), f32),
        in_specs=[pl.BlockSpec(memory_space=pltpu.VMEM)],
        out_specs=pl.BlockSpec(memory_space=pltpu.VMEM),
        scratch_shapes=[
            pltpu.VMEM((nx, nyh, rows, cells), f32),
            pltpu.VMEM((nx, nyh, rows, cells), bf16),
            pltpu.VMEM((nyh, rows, cells), f32),
            pltpu.VMEM((nx - 1, nyh, rows, cells), bf16),
            pltpu.VMEM((rows, cells), bf16),
            pltpu.VMEM((rows, cells), bf16),
            pltpu.SemaphoreType.DMA((nx * nyh + nx,)),
            pltpu.SemaphoreType.DMA((nx * nyh + nx,)),
        ],
        compiler_params=pltpu.CompilerParams(
            collective_id=1, has_side_effects=True, vmem_limit_bytes=48 * 1024 * 1024),
    )(parts)


def edge_exchange(edges_last, edges_first, axis):
    peers = lax.axis_size(axis)
    up = [(i, (i + 1) % peers) for i in range(peers - 1)]
    down = [(j, i) for i, j in up]
    before = lax.ppermute(edges_last, axis, up)
    after = lax.ppermute(edges_first, axis, down)
    return before, after


def local(frames, cache, gamma, beta, kernel, bias):
    nframes, row_count, col_count, local_ch = frames.shape
    ncache = cache.shape[0]
    group_size = CH // GROUPS
    local_groups = local_ch // group_size
    nspace = lax.axis_size("space")
    me = lax.axis_index("space")
    local_members = float(nframes * row_count * col_count * group_size)

    raw = jnp.concatenate([cache, frames], axis=0)
    before, after = edge_exchange(raw[:, :, col_count - 1 :], raw[:, :, :1], "space")

    values = frames.astype(jnp.float32).reshape(
        nframes, row_count, col_count, local_groups, group_size
    )
    local_mean = jnp.sum(values, axis=(0, 1, 2, 4)) / local_members
    local_dev = values - local_mean[:, None]
    local_m2 = jnp.sum(local_dev * local_dev, axis=(0, 1, 2, 4))
    tile = jnp.zeros((8, 128), jnp.float32)
    tile = tile.at[0, :local_groups].set(local_mean).at[1, :local_groups].set(local_m2)
    gathered = gather_space(tile)
    means = gathered[:, 0, :local_groups]
    m2s = gathered[:, 1, :local_groups]
    group_mean = jnp.mean(means, axis=0)
    spread = jnp.sum(m2s, axis=0) + local_members * jnp.sum(
        (means - group_mean) ** 2, axis=0
    )
    group_var = spread / (local_members * nspace)
    inv = lax.rsqrt(group_var + epsilon)

    def activate(x):
        shape = x.shape
        v = x.astype(jnp.float32).reshape(shape[:-1] + (local_groups, group_size))
        scaled = (v - group_mean[:, None]) * inv[:, None]
        normed = scaled.reshape(shape) * gamma + beta
        return jax.nn.silu(normed).astype(jnp.bfloat16)

    active = activate(frames)
    joined = jnp.concatenate([cache, active], axis=0)
    left = jnp.concatenate([before[:ncache], activate(before[ncache:])], axis=0)
    right = jnp.concatenate([after[:ncache], activate(after[ncache:])], axis=0)
    left = jnp.where(me == 0, jnp.zeros_like(left), left)
    right = jnp.where(me == nspace - 1, jnp.zeros_like(right), right)
    bordered = jnp.concatenate([left, joined, right], axis=2)
    bordered = jnp.pad(bordered, ((0, 0), (1, 1), (0, 0), (0, 0)))
    cell_count = nframes * row_count * col_count
    bordered = bordered.transpose(0, 2, 1, 3)
    columns_in = jnp.concatenate(
        [
            bordered[:, col_tap : col_tap + col_count, row_tap : row_tap + row_count, :]
            for row_tap in range(3)
            for col_tap in range(3)
        ],
        axis=3,
    )
    tap_width = columns_in.shape[3]
    nchan = lax.axis_size("chan")
    nx = nchan // 4
    flat_kernel = kernel.reshape(3, tap_width, kernel.shape[4])
    running = jnp.zeros((bias.shape[0] * nchan, cell_count), jnp.float32)
    plane = row_count * col_count
    flat_in = columns_in.reshape(columns_in.shape[0] * plane, tap_width)
    for depth in range(3):
        tap_weight = flat_kernel[depth]
        window = flat_in[depth * plane : depth * plane + cell_count]
        running = running + lax.dot_general(
            tap_weight, window, (((0,), (1,)), ((), ())), preferred_element_type=jnp.float32
        )
    summed = scatter_chan(running.reshape(nx, 2, 2, local_ch, cell_count))
    result = summed.T + bias
    result = result.astype(jnp.bfloat16).reshape(nframes, col_count, row_count, -1)
    return result.transpose(0, 2, 1, 3)


def solution(mesh):
    placed = (
        P(None, None, "space", "chan"),
        P(None, None, "space", "chan"),
        P("chan"),
        P("chan"),
        P(None, None, None, "chan", None),
        P("chan"),
    )
    return jax.shard_map(
        local, mesh=mesh, in_specs=placed, out_specs=P(None, None, "space", "chan"), check_vma=False
    )
```

```python
import functools

import jax
import jax.numpy as jnp
from jax import lax
from jax.experimental import pallas as pl
from jax.experimental.pallas import tpu as pltpu
from jax.experimental.layout import Layout, with_layout_constraint
from jax.sharding import PartitionSpec as P

CH = 512
GROUPS = 32
MESH = pl.DeviceIdType.MESH

epsilon = 1e-06


def gather_kernel(n, x_ref, o_ref, buf, send_sem, recv_sem):
    me = lax.axis_index("space")
    ch = lax.axis_index("chan")
    barrier = pltpu.get_barrier_semaphore()

    def signal(k, carry):
        peer = lax.rem(me + k, n)
        pl.semaphore_signal(barrier, 1, device_id=(peer, ch), device_id_type=MESH)
        return carry

    lax.fori_loop(1, n, signal, 0)
    pl.semaphore_wait(barrier, n - 1)

    def copy_to(peer):
        return pltpu.make_async_remote_copy(
            src_ref=x_ref,
            dst_ref=buf.at[me],
            send_sem=send_sem.at[peer],
            recv_sem=recv_sem.at[me],
            device_id=(peer, ch),
            device_id_type=MESH,
        )

    def copy_from(peer):
        return pltpu.make_async_remote_copy(
            src_ref=x_ref,
            dst_ref=buf.at[peer],
            send_sem=send_sem.at[peer],
            recv_sem=recv_sem.at[peer],
            device_id=(peer, ch),
            device_id_type=MESH,
        )

    def start(k, carry):
        copy_to(lax.rem(me + k, n)).start()
        return carry

    lax.fori_loop(1, n, start, 0)

    def finish(k, carry):
        peer = lax.rem(me + k, n)
        copy_to(peer).wait_send()
        copy_from(peer).wait_recv()
        return carry

    lax.fori_loop(1, n, finish, 0)
    buf[me] = x_ref[...]
    o_ref[...] = buf[...]


def gather_space(tile):
    n = lax.axis_size("space")
    return pl.pallas_call(
        functools.partial(gather_kernel, n),
        out_shape=jax.ShapeDtypeStruct((n,) + tile.shape, tile.dtype),
        in_specs=[pl.BlockSpec(memory_space=pltpu.VMEM)],
        out_specs=pl.BlockSpec(memory_space=pltpu.VMEM),
        scratch_shapes=[
            pltpu.VMEM((n,) + tile.shape, tile.dtype),
            pltpu.SemaphoreType.DMA((n,)),
            pltpu.SemaphoreType.DMA((n,)),
        ],
        compiler_params=pltpu.CompilerParams(collective_id=0, has_side_effects=True),
    )(tile)


def scatter_kernel(x_ref, o_ref, recv1, acc1, own, recv2, acc2, recv3, send_sem, recv_sem):
    sp = lax.axis_index("space")
    c = lax.axis_index("chan")
    core = c % 2
    yh = (c // 2) % 2
    xx = c // 4
    nx, nyh = x_ref.shape[0], x_ref.shape[1]
    nfirst = nx * nyh

    def dev(x_, yh_, core_):
        return (sp, x_ * 4 + yh_ * 2 + core_)

    peers = [dev(xx, yh, 1 - core)]
    peers += [dev(lax.rem(xx + k, nx), yh, core) for k in range(1, nx)]
    peers += [dev(xx, 1 - yh, core)]
    barrier = pltpu.get_barrier_semaphore()
    for p in peers:
        pl.semaphore_signal(barrier, 1, device_id=p, device_id_type=MESH)
    pl.semaphore_wait(barrier, len(peers))

    firsts = []
    for i in range(nx):
        for j in range(nyh):
            cp = pltpu.make_async_remote_copy(
                src_ref=x_ref.at[i, j, 1 - core], dst_ref=recv1.at[i, j],
                send_sem=send_sem.at[i * nyh + j], recv_sem=recv_sem.at[i * nyh + j],
                device_id=peers[0], device_id_type=MESH)
            cp.start()
            firsts.append(cp)
    for cp in firsts:
        cp.wait()

    def fold_first(dest, dst):
        for j in range(nyh):
            dst[j] = (x_ref[dest, j, core] + recv1[dest, j]).astype(dst.dtype)

    sends = []
    for k in range(1, nx):
        dest = lax.rem(xx + k, nx)
        fold_first(dest, acc1.at[dest])
        slot = nx - 1 - k
        cp = pltpu.make_async_remote_copy(
            src_ref=acc1.at[dest], dst_ref=recv2.at[slot], send_sem=send_sem.at[nfirst + k - 1],
            recv_sem=recv_sem.at[nfirst + slot], device_id=peers[k], device_id_type=MESH)
        cp.start()
        sends.append(cp)
    fold_first(xx, own)
    for slot in range(nx - 1):
        pltpu.make_async_remote_copy(
            src_ref=acc1.at[xx], dst_ref=recv2.at[slot], send_sem=send_sem.at[nfirst + slot],
            recv_sem=recv_sem.at[nfirst + slot], device_id=peers[0], device_id_type=MESH).wait_recv()
    other = 1 - yh
    total = own[other]
    for slot in range(nx - 1):
        total = total + recv2[slot, other].astype(jnp.float32)
    acc2[...] = total.astype(acc2.dtype)
    last_sem = nfirst + nx - 1
    last = pltpu.make_async_remote_copy(
        src_ref=acc2, dst_ref=recv3, send_sem=send_sem.at[last_sem],
        recv_sem=recv_sem.at[last_sem], device_id=peers[nx], device_id_type=MESH)
    last.start()
    total = own[yh]
    for slot in range(nx - 1):
        total = total + recv2[slot, yh].astype(jnp.float32)
    for cp in sends:
        cp.wait_send()
    last.wait()
    o_ref[...] = total + recv3[...].astype(jnp.float32)


def scatter_chan(parts):
    nx, nyh, ncore, rows, cells = parts.shape
    f32, bf16 = jnp.float32, jnp.bfloat16
    return pl.pallas_call(
        scatter_kernel,
        out_shape=jax.ShapeDtypeStruct((rows, cells), f32),
        in_specs=[pl.BlockSpec(memory_space=pltpu.VMEM)],
        out_specs=pl.BlockSpec(memory_space=pltpu.VMEM),
        scratch_shapes=[
            pltpu.VMEM((nx, nyh, rows, cells), f32),
            pltpu.VMEM((nx, nyh, rows, cells), bf16),
            pltpu.VMEM((nyh, rows, cells), f32),
            pltpu.VMEM((nx - 1, nyh, rows, cells), bf16),
            pltpu.VMEM((rows, cells), bf16),
            pltpu.VMEM((rows, cells), bf16),
            pltpu.SemaphoreType.DMA((nx * nyh + nx,)),
            pltpu.SemaphoreType.DMA((nx * nyh + nx,)),
        ],
        compiler_params=pltpu.CompilerParams(
            collective_id=1, has_side_effects=True, vmem_limit_bytes=48 * 1024 * 1024),
    )(parts)


def edge_exchange(edges_last, edges_first, axis):
    peers = lax.axis_size(axis)
    up = [(i, (i + 1) % peers) for i in range(peers - 1)]
    down = [(j, i) for i, j in up]
    before = lax.ppermute(edges_last, axis, up)
    after = lax.ppermute(edges_first, axis, down)
    return before, after


def local(frames, cache, gamma, beta, kernel, bias):
    nframes, row_count, col_count, local_ch = frames.shape
    ncache = cache.shape[0]
    group_size = CH // GROUPS
    local_groups = local_ch // group_size
    nspace = lax.axis_size("space")
    me = lax.axis_index("space")
    local_members = float(nframes * row_count * col_count * group_size)

    raw = jnp.concatenate([cache, frames], axis=0)
    before, after = edge_exchange(raw[:, :, col_count - 1 :], raw[:, :, :1], "space")

    values = frames.astype(jnp.float32).reshape(
        nframes, row_count, col_count, local_groups, group_size
    )
    local_mean = jnp.sum(values, axis=(0, 1, 2, 4)) / local_members
    local_dev = values - local_mean[:, None]
    local_m2 = jnp.sum(local_dev * local_dev, axis=(0, 1, 2, 4))
    tile = jnp.zeros((8, 128), jnp.float32)
    tile = tile.at[0, :local_groups].set(local_mean).at[1, :local_groups].set(local_m2)
    gathered = gather_space(tile)
    means = gathered[:, 0, :local_groups]
    m2s = gathered[:, 1, :local_groups]
    group_mean = jnp.mean(means, axis=0)
    spread = jnp.sum(m2s, axis=0) + local_members * jnp.sum(
        (means - group_mean) ** 2, axis=0
    )
    group_var = spread / (local_members * nspace)
    inv = lax.rsqrt(group_var + epsilon)

    def activate(x):
        shape = x.shape
        v = x.astype(jnp.float32).reshape(shape[:-1] + (local_groups, group_size))
        scaled = (v - group_mean[:, None]) * inv[:, None]
        normed = scaled.reshape(shape) * gamma + beta
        return jax.nn.silu(normed).astype(jnp.bfloat16)

    active = activate(frames)
    joined = jnp.concatenate([cache, active], axis=0)
    left = jnp.concatenate([before[:ncache], activate(before[ncache:])], axis=0)
    right = jnp.concatenate([after[:ncache], activate(after[ncache:])], axis=0)
    left = jnp.where(me == 0, jnp.zeros_like(left), left)
    right = jnp.where(me == nspace - 1, jnp.zeros_like(right), right)
    bordered = jnp.concatenate([left, joined, right], axis=2)
    bordered = jnp.pad(bordered, ((0, 0), (1, 1), (0, 0), (0, 0)))
    cell_count = nframes * row_count * col_count
    bordered = bordered.transpose(0, 2, 1, 3)
    columns_in = jnp.concatenate(
        [
            bordered[:, col_tap : col_tap + col_count, row_tap : row_tap + row_count, :]
            for row_tap in range(3)
            for col_tap in range(3)
        ],
        axis=3,
    )
    columns_in = with_layout_constraint(columns_in, Layout(major_to_minor=(0, 1, 2, 3)))
    tap_width = columns_in.shape[3]
    nchan = lax.axis_size("chan")
    nx = nchan // 4
    flat_kernel = kernel.reshape(3, tap_width, kernel.shape[4])
    running = jnp.zeros((bias.shape[0] * nchan, cell_count), jnp.float32)
    plane = row_count * col_count
    flat_in = columns_in.reshape(columns_in.shape[0] * plane, tap_width)
    for depth in range(3):
        tap_weight = flat_kernel[depth]
        window = flat_in[depth * plane : depth * plane + cell_count]
        running = running + lax.dot_general(
            tap_weight, window, (((0,), (1,)), ((), ())), preferred_element_type=jnp.float32
        )
    summed = scatter_chan(running.reshape(nx, 2, 2, local_ch, cell_count))
    result = summed.T + bias
    result = result.astype(jnp.bfloat16).reshape(nframes, col_count, row_count, -1)
    return result.transpose(0, 2, 1, 3)


def solution(mesh):
    placed = (
        P(None, None, "space", "chan"),
        P(None, None, "space", "chan"),
        P("chan"),
        P("chan"),
        P(None, None, None, "chan", None),
        P("chan"),
    )
    return jax.shard_map(
        local, mesh=mesh, in_specs=placed, out_specs=P(None, None, "space", "chan"), check_vma=False
    )
```

```python
import functools

import jax
import jax.numpy as jnp
from jax import lax
from jax.experimental import pallas as pl
from jax.experimental.pallas import tpu as pltpu
from jax.experimental.layout import Layout, with_layout_constraint
from jax.sharding import PartitionSpec as P

CH = 512
GROUPS = 32
MESH = pl.DeviceIdType.MESH

epsilon = 1e-06


def gather_kernel(n, x_ref, o_ref, buf, send_sem, recv_sem):
    me = lax.axis_index("space")
    ch = lax.axis_index("chan")
    barrier = pltpu.get_barrier_semaphore()

    def signal(k, carry):
        peer = lax.rem(me + k, n)
        pl.semaphore_signal(barrier, 1, device_id=(peer, ch), device_id_type=MESH)
        return carry

    lax.fori_loop(1, n, signal, 0)
    pl.semaphore_wait(barrier, n - 1)

    def copy_to(peer):
        return pltpu.make_async_remote_copy(
            src_ref=x_ref,
            dst_ref=buf.at[me],
            send_sem=send_sem.at[peer],
            recv_sem=recv_sem.at[me],
            device_id=(peer, ch),
            device_id_type=MESH,
        )

    def copy_from(peer):
        return pltpu.make_async_remote_copy(
            src_ref=x_ref,
            dst_ref=buf.at[peer],
            send_sem=send_sem.at[peer],
            recv_sem=recv_sem.at[peer],
            device_id=(peer, ch),
            device_id_type=MESH,
        )

    def start(k, carry):
        copy_to(lax.rem(me + k, n)).start()
        return carry

    lax.fori_loop(1, n, start, 0)

    def finish(k, carry):
        peer = lax.rem(me + k, n)
        copy_to(peer).wait_send()
        copy_from(peer).wait_recv()
        return carry

    lax.fori_loop(1, n, finish, 0)
    buf[me] = x_ref[...]
    o_ref[...] = buf[...]


def gather_space(tile):
    n = lax.axis_size("space")
    return pl.pallas_call(
        functools.partial(gather_kernel, n),
        out_shape=jax.ShapeDtypeStruct((n,) + tile.shape, tile.dtype),
        in_specs=[pl.BlockSpec(memory_space=pltpu.VMEM)],
        out_specs=pl.BlockSpec(memory_space=pltpu.VMEM),
        scratch_shapes=[
            pltpu.VMEM((n,) + tile.shape, tile.dtype),
            pltpu.SemaphoreType.DMA((n,)),
            pltpu.SemaphoreType.DMA((n,)),
        ],
        compiler_params=pltpu.CompilerParams(collective_id=0, has_side_effects=True),
    )(tile)


def scatter_kernel(nchunk, x_ref, o_ref, recv1, acc1, own, recv2, acc2, recv3,
                   sem1s, sem1r, sem2s, sem2r, sem3s, sem3r):
    sp = lax.axis_index("space")
    c = lax.axis_index("chan")
    core = c % 2
    yh = (c // 2) % 2
    xx = c // 4
    nx, nyh = x_ref.shape[0], x_ref.shape[1]
    width = x_ref.shape[-1] // nchunk
    f32, bf16 = jnp.float32, jnp.bfloat16

    def dev(x_, yh_, core_):
        return (sp, x_ * 4 + yh_ * 2 + core_)

    peers = [dev(xx, yh, 1 - core)]
    peers += [dev(lax.rem(xx + k, nx), yh, core) for k in range(1, nx)]
    peers += [dev(xx, 1 - yh, core)]
    barrier = pltpu.get_barrier_semaphore()
    for p in peers:
        pl.semaphore_signal(barrier, 1, device_id=p, device_id_type=MESH)
    pl.semaphore_wait(barrier, len(peers))

    def cols(q):
        return pl.ds(q * width, width)

    firsts = []
    for q in range(nchunk):
        for i in range(nx):
            for j in range(nyh):
                n = (q * nx + i) * nyh + j
                cp = pltpu.make_async_remote_copy(
                    src_ref=x_ref.at[i, j, 1 - core, :, cols(q)], dst_ref=recv1.at[q, i, j],
                    send_sem=sem1s.at[n], recv_sem=sem1r.at[n],
                    device_id=peers[0], device_id_type=MESH)
                cp.start()
                firsts.append(cp)

    def second(q):
        for cp in firsts[q * nx * nyh : (q + 1) * nx * nyh]:
            cp.wait()
        sends = []
        for k in range(1, nx):
            dest = lax.rem(xx + k, nx)
            for j in range(nyh):
                acc1[q, dest, j] = (x_ref[dest, j, core, :, cols(q)] + recv1[q, dest, j]).astype(bf16)
            slot = nx - 1 - k
            cp = pltpu.make_async_remote_copy(
                src_ref=acc1.at[q, dest], dst_ref=recv2.at[q, slot],
                send_sem=sem2s.at[q * (nx - 1) + k - 1], recv_sem=sem2r.at[q * (nx - 1) + slot],
                device_id=peers[k], device_id_type=MESH)
            cp.start()
            sends.append(cp)
        for j in range(nyh):
            own[q, j] = x_ref[xx, j, core, :, cols(q)] + recv1[q, xx, j]
        return sends

    def third(q):
        for slot in range(nx - 1):
            pltpu.make_async_remote_copy(
                src_ref=acc1.at[q, xx], dst_ref=recv2.at[q, slot],
                send_sem=sem2s.at[q * (nx - 1) + slot], recv_sem=sem2r.at[q * (nx - 1) + slot],
                device_id=peers[0], device_id_type=MESH).wait_recv()
        other = 1 - yh
        total = own[q, other]
        for slot in range(nx - 1):
            total = total + recv2[q, slot, other].astype(f32)
        acc2[q] = total.astype(bf16)
        cp = pltpu.make_async_remote_copy(
            src_ref=acc2.at[q], dst_ref=recv3.at[q], send_sem=sem3s.at[q],
            recv_sem=sem3r.at[q], device_id=peers[nx], device_id_type=MESH)
        cp.start()
        total = own[q, yh]
        for slot in range(nx - 1):
            total = total + recv2[q, slot, yh].astype(f32)
        own[q, yh] = total
        return cp

    seconds, lasts = [], []
    for q in range(nchunk):
        seconds.append(second(q))
        if q >= 1:
            lasts.append(third(q - 1))
    lasts.append(third(nchunk - 1))
    for sends in seconds:
        for cp in sends:
            cp.wait_send()
    for q, cp in enumerate(lasts):
        cp.wait()
        o_ref[:, cols(q)] = own[q, yh] + recv3[q].astype(f32)


def scatter_chan(parts, nchunk=3):
    nx, nyh, ncore, rows, cells = parts.shape
    width = cells // nchunk
    f32, bf16 = jnp.float32, jnp.bfloat16
    return pl.pallas_call(
        functools.partial(scatter_kernel, nchunk),
        out_shape=jax.ShapeDtypeStruct((rows, cells), f32),
        in_specs=[pl.BlockSpec(memory_space=pltpu.VMEM)],
        out_specs=pl.BlockSpec(memory_space=pltpu.VMEM),
        scratch_shapes=[
            pltpu.VMEM((nchunk, nx, nyh, rows, width), f32),
            pltpu.VMEM((nchunk, nx, nyh, rows, width), bf16),
            pltpu.VMEM((nchunk, nyh, rows, width), f32),
            pltpu.VMEM((nchunk, nx - 1, nyh, rows, width), bf16),
            pltpu.VMEM((nchunk, rows, width), bf16),
            pltpu.VMEM((nchunk, rows, width), bf16),
            pltpu.SemaphoreType.DMA((nchunk * nx * nyh,)),
            pltpu.SemaphoreType.DMA((nchunk * nx * nyh,)),
            pltpu.SemaphoreType.DMA((nchunk * (nx - 1),)),
            pltpu.SemaphoreType.DMA((nchunk * (nx - 1),)),
            pltpu.SemaphoreType.DMA((nchunk,)),
            pltpu.SemaphoreType.DMA((nchunk,)),
        ],
        compiler_params=pltpu.CompilerParams(
            collective_id=1, has_side_effects=True, vmem_limit_bytes=48 * 1024 * 1024),
    )(parts)


def edge_exchange(edges_last, edges_first, axis):
    peers = lax.axis_size(axis)
    up = [(i, (i + 1) % peers) for i in range(peers - 1)]
    down = [(j, i) for i, j in up]
    before = lax.ppermute(edges_last, axis, up)
    after = lax.ppermute(edges_first, axis, down)
    return before, after


def local(frames, cache, gamma, beta, kernel, bias):
    nframes, row_count, col_count, local_ch = frames.shape
    ncache = cache.shape[0]
    group_size = CH // GROUPS
    local_groups = local_ch // group_size
    nspace = lax.axis_size("space")
    me = lax.axis_index("space")
    local_members = float(nframes * row_count * col_count * group_size)

    raw = jnp.concatenate([cache, frames], axis=0)
    before, after = edge_exchange(raw[:, :, col_count - 1 :], raw[:, :, :1], "space")

    values = frames.astype(jnp.float32).reshape(
        nframes, row_count, col_count, local_groups, group_size
    )
    local_mean = jnp.sum(values, axis=(0, 1, 2, 4)) / local_members
    local_dev = values - local_mean[:, None]
    local_m2 = jnp.sum(local_dev * local_dev, axis=(0, 1, 2, 4))
    tile = jnp.zeros((8, 128), jnp.float32)
    tile = tile.at[0, :local_groups].set(local_mean).at[1, :local_groups].set(local_m2)
    gathered = gather_space(tile)
    means = gathered[:, 0, :local_groups]
    m2s = gathered[:, 1, :local_groups]
    group_mean = jnp.mean(means, axis=0)
    spread = jnp.sum(m2s, axis=0) + local_members * jnp.sum(
        (means - group_mean) ** 2, axis=0
    )
    group_var = spread / (local_members * nspace)
    inv = lax.rsqrt(group_var + epsilon)

    def activate(x):
        shape = x.shape
        v = x.astype(jnp.float32).reshape(shape[:-1] + (local_groups, group_size))
        scaled = (v - group_mean[:, None]) * inv[:, None]
        normed = scaled.reshape(shape) * gamma + beta
        return jax.nn.silu(normed).astype(jnp.bfloat16)

    active = activate(frames)
    joined = jnp.concatenate([cache, active], axis=0)
    left = jnp.concatenate([before[:ncache], activate(before[ncache:])], axis=0)
    right = jnp.concatenate([after[:ncache], activate(after[ncache:])], axis=0)
    left = jnp.where(me == 0, jnp.zeros_like(left), left)
    right = jnp.where(me == nspace - 1, jnp.zeros_like(right), right)
    bordered = jnp.concatenate([left, joined, right], axis=2)
    bordered = jnp.pad(bordered, ((0, 0), (1, 1), (0, 0), (0, 0)))
    cell_count = nframes * row_count * col_count
    bordered = bordered.transpose(0, 2, 1, 3)
    columns_in = jnp.concatenate(
        [
            bordered[:, col_tap : col_tap + col_count, row_tap : row_tap + row_count, :]
            for row_tap in range(3)
            for col_tap in range(3)
        ],
        axis=3,
    )
    columns_in = with_layout_constraint(columns_in, Layout(major_to_minor=(0, 1, 2, 3)))
    tap_width = columns_in.shape[3]
    nchan = lax.axis_size("chan")
    nx = nchan // 4
    flat_kernel = kernel.reshape(3, tap_width, kernel.shape[4])
    running = jnp.zeros((bias.shape[0] * nchan, cell_count), jnp.float32)
    plane = row_count * col_count
    flat_in = columns_in.reshape(columns_in.shape[0] * plane, tap_width)
    for depth in range(3):
        tap_weight = flat_kernel[depth]
        window = flat_in[depth * plane : depth * plane + cell_count]
        running = running + lax.dot_general(
            tap_weight, window, (((0,), (1,)), ((), ())), preferred_element_type=jnp.float32
        )
    summed = scatter_chan(running.reshape(nx, 2, 2, local_ch, cell_count))
    result = summed.T + bias
    result = result.astype(jnp.bfloat16).reshape(nframes, col_count, row_count, -1)
    return result.transpose(0, 2, 1, 3)


def solution(mesh):
    placed = (
        P(None, None, "space", "chan"),
        P(None, None, "space", "chan"),
        P("chan"),
        P("chan"),
        P(None, None, None, "chan", None),
        P("chan"),
    )
    return jax.shard_map(
        local, mesh=mesh, in_specs=placed, out_specs=P(None, None, "space", "chan"), check_vma=False
    )
```

```python
import functools

import jax
import jax.numpy as jnp
from jax import lax
from jax.experimental import pallas as pl
from jax.experimental.pallas import tpu as pltpu
from jax.experimental.layout import Layout, with_layout_constraint
from jax.sharding import PartitionSpec as P

CH = 512
GROUPS = 32
MESH = pl.DeviceIdType.MESH

epsilon = 1e-06


def gather_kernel(n, x_ref, o_ref, buf, send_sem, recv_sem):
    me = lax.axis_index("space")
    ch = lax.axis_index("chan")
    barrier = pltpu.get_barrier_semaphore()

    def signal(k, carry):
        peer = lax.rem(me + k, n)
        pl.semaphore_signal(barrier, 1, device_id=(peer, ch), device_id_type=MESH)
        return carry

    lax.fori_loop(1, n, signal, 0)
    pl.semaphore_wait(barrier, n - 1)

    def copy_to(peer):
        return pltpu.make_async_remote_copy(
            src_ref=x_ref,
            dst_ref=buf.at[me],
            send_sem=send_sem.at[peer],
            recv_sem=recv_sem.at[me],
            device_id=(peer, ch),
            device_id_type=MESH,
        )

    def copy_from(peer):
        return pltpu.make_async_remote_copy(
            src_ref=x_ref,
            dst_ref=buf.at[peer],
            send_sem=send_sem.at[peer],
            recv_sem=recv_sem.at[peer],
            device_id=(peer, ch),
            device_id_type=MESH,
        )

    def start(k, carry):
        copy_to(lax.rem(me + k, n)).start()
        return carry

    lax.fori_loop(1, n, start, 0)

    def finish(k, carry):
        peer = lax.rem(me + k, n)
        copy_to(peer).wait_send()
        copy_from(peer).wait_recv()
        return carry

    lax.fori_loop(1, n, finish, 0)
    buf[me] = x_ref[...]
    o_ref[...] = buf[...]


def gather_space(tile):
    n = lax.axis_size("space")
    return pl.pallas_call(
        functools.partial(gather_kernel, n),
        out_shape=jax.ShapeDtypeStruct((n,) + tile.shape, tile.dtype),
        in_specs=[pl.BlockSpec(memory_space=pltpu.VMEM)],
        out_specs=pl.BlockSpec(memory_space=pltpu.VMEM),
        scratch_shapes=[
            pltpu.VMEM((n,) + tile.shape, tile.dtype),
            pltpu.SemaphoreType.DMA((n,)),
            pltpu.SemaphoreType.DMA((n,)),
        ],
        compiler_params=pltpu.CompilerParams(collective_id=0, has_side_effects=True),
    )(tile)


def scatter_kernel(nchunk, x_ref, o_ref, recv1, acc1, own, recv2, acc2, recv3,
                   sem1s, sem1r, sem2s, sem2r, sem3s, sem3r):
    sp = lax.axis_index("space")
    c = lax.axis_index("chan")
    core = c % 2
    yh = (c // 2) % 2
    xx = c // 4
    nx, nyh = x_ref.shape[0], x_ref.shape[1]
    width = x_ref.shape[-1] // nchunk
    f32, bf16 = jnp.float32, jnp.bfloat16

    def dev(x_, yh_, core_):
        return (sp, x_ * 4 + yh_ * 2 + core_)

    peers = [dev(xx, yh, 1 - core)]
    peers += [dev(lax.rem(xx + k, nx), yh, core) for k in range(1, nx)]
    peers += [dev(xx, 1 - yh, core)]
    barrier = pltpu.get_barrier_semaphore()
    for p in peers:
        pl.semaphore_signal(barrier, 1, device_id=p, device_id_type=MESH)
    pl.semaphore_wait(barrier, len(peers))

    def cols(q):
        return pl.ds(q * width, width)

    firsts = []
    for q in range(nchunk):
        for i in range(nx):
            for j in range(nyh):
                n = (q * nx + i) * nyh + j
                cp = pltpu.make_async_remote_copy(
                    src_ref=x_ref.at[i, j, 1 - core, :, cols(q)], dst_ref=recv1.at[q, i, j],
                    send_sem=sem1s.at[n], recv_sem=sem1r.at[n],
                    device_id=peers[0], device_id_type=MESH)
                cp.start()
                firsts.append(cp)

    def second(q):
        for cp in firsts[q * nx * nyh : (q + 1) * nx * nyh]:
            cp.wait()
        sends = []
        for k in range(1, nx):
            dest = lax.rem(xx + k, nx)
            for j in range(nyh):
                acc1[q, dest, j] = (x_ref[dest, j, core, :, cols(q)] + recv1[q, dest, j]).astype(bf16)
            slot = nx - 1 - k
            cp = pltpu.make_async_remote_copy(
                src_ref=acc1.at[q, dest], dst_ref=recv2.at[q, slot],
                send_sem=sem2s.at[q * (nx - 1) + k - 1], recv_sem=sem2r.at[q * (nx - 1) + slot],
                device_id=peers[k], device_id_type=MESH)
            cp.start()
            sends.append(cp)
        for j in range(nyh):
            own[q, j] = x_ref[xx, j, core, :, cols(q)] + recv1[q, xx, j]
        return sends

    def third(q):
        for slot in range(nx - 1):
            pltpu.make_async_remote_copy(
                src_ref=acc1.at[q, xx], dst_ref=recv2.at[q, slot],
                send_sem=sem2s.at[q * (nx - 1) + slot], recv_sem=sem2r.at[q * (nx - 1) + slot],
                device_id=peers[0], device_id_type=MESH).wait_recv()
        other = 1 - yh
        total = own[q, other]
        for slot in range(nx - 1):
            total = total + recv2[q, slot, other].astype(f32)
        acc2[q] = total.astype(bf16)
        cp = pltpu.make_async_remote_copy(
            src_ref=acc2.at[q], dst_ref=recv3.at[q], send_sem=sem3s.at[q],
            recv_sem=sem3r.at[q], device_id=peers[nx], device_id_type=MESH)
        cp.start()
        total = own[q, yh]
        for slot in range(nx - 1):
            total = total + recv2[q, slot, yh].astype(f32)
        own[q, yh] = total
        return cp

    seconds, lasts = [], []
    for q in range(nchunk):
        seconds.append(second(q))
        if q >= 1:
            lasts.append(third(q - 1))
    lasts.append(third(nchunk - 1))
    for sends in seconds:
        for cp in sends:
            cp.wait_send()
    for q, cp in enumerate(lasts):
        cp.wait()
        o_ref[:, cols(q)] = own[q, yh] + recv3[q].astype(f32)


def scatter_chan(parts, nchunk=5):
    nx, nyh, ncore, rows, cells = parts.shape
    width = cells // nchunk
    f32, bf16 = jnp.float32, jnp.bfloat16
    return pl.pallas_call(
        functools.partial(scatter_kernel, nchunk),
        out_shape=jax.ShapeDtypeStruct((rows, cells), f32),
        in_specs=[pl.BlockSpec(memory_space=pltpu.VMEM)],
        out_specs=pl.BlockSpec(memory_space=pltpu.VMEM),
        scratch_shapes=[
            pltpu.VMEM((nchunk, nx, nyh, rows, width), f32),
            pltpu.VMEM((nchunk, nx, nyh, rows, width), bf16),
            pltpu.VMEM((nchunk, nyh, rows, width), f32),
            pltpu.VMEM((nchunk, nx - 1, nyh, rows, width), bf16),
            pltpu.VMEM((nchunk, rows, width), bf16),
            pltpu.VMEM((nchunk, rows, width), bf16),
            pltpu.SemaphoreType.DMA((nchunk * nx * nyh,)),
            pltpu.SemaphoreType.DMA((nchunk * nx * nyh,)),
            pltpu.SemaphoreType.DMA((nchunk * (nx - 1),)),
            pltpu.SemaphoreType.DMA((nchunk * (nx - 1),)),
            pltpu.SemaphoreType.DMA((nchunk,)),
            pltpu.SemaphoreType.DMA((nchunk,)),
        ],
        compiler_params=pltpu.CompilerParams(
            collective_id=1, has_side_effects=True, vmem_limit_bytes=48 * 1024 * 1024),
    )(parts)


def edge_exchange(edges_last, edges_first, axis):
    peers = lax.axis_size(axis)
    up = [(i, (i + 1) % peers) for i in range(peers - 1)]
    down = [(j, i) for i, j in up]
    before = lax.ppermute(edges_last, axis, up)
    after = lax.ppermute(edges_first, axis, down)
    return before, after


def local(frames, cache, gamma, beta, kernel, bias):
    nframes, row_count, col_count, local_ch = frames.shape
    ncache = cache.shape[0]
    group_size = CH // GROUPS
    local_groups = local_ch // group_size
    nspace = lax.axis_size("space")
    me = lax.axis_index("space")
    local_members = float(nframes * row_count * col_count * group_size)

    raw = jnp.concatenate([cache, frames], axis=0)
    before, after = edge_exchange(raw[:, :, col_count - 1 :], raw[:, :, :1], "space")

    values = frames.astype(jnp.float32).reshape(
        nframes, row_count, col_count, local_groups, group_size
    )
    local_mean = jnp.sum(values, axis=(0, 1, 2, 4)) / local_members
    local_dev = values - local_mean[:, None]
    local_m2 = jnp.sum(local_dev * local_dev, axis=(0, 1, 2, 4))
    tile = jnp.zeros((8, 128), jnp.float32)
    tile = tile.at[0, :local_groups].set(local_mean).at[1, :local_groups].set(local_m2)
    gathered = gather_space(tile)
    means = gathered[:, 0, :local_groups]
    m2s = gathered[:, 1, :local_groups]
    group_mean = jnp.mean(means, axis=0)
    spread = jnp.sum(m2s, axis=0) + local_members * jnp.sum(
        (means - group_mean) ** 2, axis=0
    )
    group_var = spread / (local_members * nspace)
    inv = lax.rsqrt(group_var + epsilon)

    def activate(x):
        shape = x.shape
        v = x.astype(jnp.float32).reshape(shape[:-1] + (local_groups, group_size))
        scaled = (v - group_mean[:, None]) * inv[:, None]
        normed = scaled.reshape(shape) * gamma + beta
        return jax.nn.silu(normed).astype(jnp.bfloat16)

    active = activate(frames)
    joined = jnp.concatenate([cache, active], axis=0)
    left = jnp.concatenate([before[:ncache], activate(before[ncache:])], axis=0)
    right = jnp.concatenate([after[:ncache], activate(after[ncache:])], axis=0)
    left = jnp.where(me == 0, jnp.zeros_like(left), left)
    right = jnp.where(me == nspace - 1, jnp.zeros_like(right), right)
    bordered = jnp.concatenate([left, joined, right], axis=2)
    bordered = jnp.pad(bordered, ((0, 0), (1, 1), (0, 0), (0, 0)))
    cell_count = nframes * row_count * col_count
    bordered = bordered.transpose(0, 2, 1, 3)
    columns_in = jnp.concatenate(
        [
            bordered[:, col_tap : col_tap + col_count, row_tap : row_tap + row_count, :]
            for row_tap in range(3)
            for col_tap in range(3)
        ],
        axis=3,
    )
    columns_in = with_layout_constraint(columns_in, Layout(major_to_minor=(0, 1, 2, 3)))
    tap_width = columns_in.shape[3]
    nchan = lax.axis_size("chan")
    nx = nchan // 4
    flat_kernel = kernel.reshape(3, tap_width, kernel.shape[4])
    running = jnp.zeros((bias.shape[0] * nchan, cell_count), jnp.float32)
    plane = row_count * col_count
    flat_in = columns_in.reshape(columns_in.shape[0] * plane, tap_width)
    for depth in range(3):
        tap_weight = flat_kernel[depth]
        window = flat_in[depth * plane : depth * plane + cell_count]
        running = running + lax.dot_general(
            tap_weight, window, (((0,), (1,)), ((), ())), preferred_element_type=jnp.float32
        )
    summed = scatter_chan(running.reshape(nx, 2, 2, local_ch, cell_count))
    result = summed.T + bias
    result = result.astype(jnp.bfloat16).reshape(nframes, col_count, row_count, -1)
    return result.transpose(0, 2, 1, 3)


def solution(mesh):
    placed = (
        P(None, None, "space", "chan"),
        P(None, None, "space", "chan"),
        P("chan"),
        P("chan"),
        P(None, None, None, "chan", None),
        P("chan"),
    )
    return jax.shard_map(
        local, mesh=mesh, in_specs=placed, out_specs=P(None, None, "space", "chan"), check_vma=False
    )
```

```python
import functools

import jax
import jax.numpy as jnp
from jax import lax
from jax.experimental import pallas as pl
from jax.experimental.pallas import tpu as pltpu
from jax.experimental.layout import Layout, with_layout_constraint
from jax.sharding import PartitionSpec as P

CH = 512
GROUPS = 32
MESH = pl.DeviceIdType.MESH

epsilon = 1e-06


def gather_kernel(n, x_ref, lo_ref, hi_ref, o_ref, left_ref, right_ref,
                  buf, left_buf, right_buf, send_sem, recv_sem, edge_send, edge_recv):
    me = lax.axis_index("space")
    ch = lax.axis_index("chan")
    right = lax.rem(me + 1, n)
    left = lax.rem(me + n - 1, n)
    barrier = pltpu.get_barrier_semaphore()

    def signal(k, carry):
        peer = lax.rem(me + k, n)
        pl.semaphore_signal(barrier, 1, device_id=(peer, ch), device_id_type=MESH)
        return carry

    lax.fori_loop(1, n, signal, 0)
    pl.semaphore_wait(barrier, n - 1)

    to_right = pltpu.make_async_remote_copy(
        src_ref=hi_ref, dst_ref=left_buf, send_sem=edge_send.at[0], recv_sem=edge_recv.at[0],
        device_id=(right, ch), device_id_type=MESH)
    to_left = pltpu.make_async_remote_copy(
        src_ref=lo_ref, dst_ref=right_buf, send_sem=edge_send.at[1], recv_sem=edge_recv.at[1],
        device_id=(left, ch), device_id_type=MESH)
    to_right.start()
    to_left.start()

    def copy_to(peer):
        return pltpu.make_async_remote_copy(
            src_ref=x_ref,
            dst_ref=buf.at[me],
            send_sem=send_sem.at[peer],
            recv_sem=recv_sem.at[me],
            device_id=(peer, ch),
            device_id_type=MESH,
        )

    def copy_from(peer):
        return pltpu.make_async_remote_copy(
            src_ref=x_ref,
            dst_ref=buf.at[peer],
            send_sem=send_sem.at[peer],
            recv_sem=recv_sem.at[peer],
            device_id=(peer, ch),
            device_id_type=MESH,
        )

    def start(k, carry):
        copy_to(lax.rem(me + k, n)).start()
        return carry

    lax.fori_loop(1, n, start, 0)

    def finish(k, carry):
        peer = lax.rem(me + k, n)
        copy_to(peer).wait_send()
        copy_from(peer).wait_recv()
        return carry

    lax.fori_loop(1, n, finish, 0)
    buf[me] = x_ref[...]
    o_ref[...] = buf[...]
    to_right.wait()
    to_left.wait()
    left_ref[...] = left_buf[...]
    right_ref[...] = right_buf[...]


def gather_space(tile, lo, hi):
    n = lax.axis_size("space")
    vmem = pl.BlockSpec(memory_space=pltpu.VMEM)
    return pl.pallas_call(
        functools.partial(gather_kernel, n),
        out_shape=(
            jax.ShapeDtypeStruct((n,) + tile.shape, tile.dtype),
            jax.ShapeDtypeStruct(hi.shape, hi.dtype),
            jax.ShapeDtypeStruct(lo.shape, lo.dtype),
        ),
        in_specs=[vmem, vmem, vmem],
        out_specs=(vmem, vmem, vmem),
        scratch_shapes=[
            pltpu.VMEM((n,) + tile.shape, tile.dtype),
            pltpu.VMEM(hi.shape, hi.dtype),
            pltpu.VMEM(lo.shape, lo.dtype),
            pltpu.SemaphoreType.DMA((n,)),
            pltpu.SemaphoreType.DMA((n,)),
            pltpu.SemaphoreType.DMA((2,)),
            pltpu.SemaphoreType.DMA((2,)),
        ],
        compiler_params=pltpu.CompilerParams(collective_id=0, has_side_effects=True),
    )(tile, lo, hi)


def scatter_kernel(nchunk, x_ref, o_ref, recv1, acc1, own, recv2, acc2, recv3,
                   sem1s, sem1r, sem2s, sem2r, sem3s, sem3r):
    sp = lax.axis_index("space")
    c = lax.axis_index("chan")
    core = c % 2
    yh = (c // 2) % 2
    xx = c // 4
    nx, nyh = x_ref.shape[0], x_ref.shape[1]
    width = x_ref.shape[-1] // nchunk
    f32, bf16 = jnp.float32, jnp.bfloat16

    def dev(x_, yh_, core_):
        return (sp, x_ * 4 + yh_ * 2 + core_)

    peers = [dev(xx, yh, 1 - core)]
    peers += [dev(lax.rem(xx + k, nx), yh, core) for k in range(1, nx)]
    peers += [dev(xx, 1 - yh, core)]
    barrier = pltpu.get_barrier_semaphore()
    for p in peers:
        pl.semaphore_signal(barrier, 1, device_id=p, device_id_type=MESH)
    pl.semaphore_wait(barrier, len(peers))

    def cols(q):
        return pl.ds(q * width, width)

    firsts = []
    for q in range(nchunk):
        for i in range(nx):
            for j in range(nyh):
                n = (q * nx + i) * nyh + j
                cp = pltpu.make_async_remote_copy(
                    src_ref=x_ref.at[i, j, 1 - core, :, cols(q)], dst_ref=recv1.at[q, i, j],
                    send_sem=sem1s.at[n], recv_sem=sem1r.at[n],
                    device_id=peers[0], device_id_type=MESH)
                cp.start()
                firsts.append(cp)

    def second(q):
        for cp in firsts[q * nx * nyh : (q + 1) * nx * nyh]:
            cp.wait()
        sends = []
        for k in range(1, nx):
            dest = lax.rem(xx + k, nx)
            for j in range(nyh):
                acc1[q, dest, j] = (x_ref[dest, j, core, :, cols(q)] + recv1[q, dest, j]).astype(bf16)
            slot = nx - 1 - k
            cp = pltpu.make_async_remote_copy(
                src_ref=acc1.at[q, dest], dst_ref=recv2.at[q, slot],
                send_sem=sem2s.at[q * (nx - 1) + k - 1], recv_sem=sem2r.at[q * (nx - 1) + slot],
                device_id=peers[k], device_id_type=MESH)
            cp.start()
            sends.append(cp)
        for j in range(nyh):
            own[q, j] = x_ref[xx, j, core, :, cols(q)] + recv1[q, xx, j]
        return sends

    def third(q):
        for slot in range(nx - 1):
            pltpu.make_async_remote_copy(
                src_ref=acc1.at[q, xx], dst_ref=recv2.at[q, slot],
                send_sem=sem2s.at[q * (nx - 1) + slot], recv_sem=sem2r.at[q * (nx - 1) + slot],
                device_id=peers[0], device_id_type=MESH).wait_recv()
        other = 1 - yh
        total = own[q, other]
        for slot in range(nx - 1):
            total = total + recv2[q, slot, other].astype(f32)
        acc2[q] = total.astype(bf16)
        cp = pltpu.make_async_remote_copy(
            src_ref=acc2.at[q], dst_ref=recv3.at[q], send_sem=sem3s.at[q],
            recv_sem=sem3r.at[q], device_id=peers[nx], device_id_type=MESH)
        cp.start()
        total = own[q, yh]
        for slot in range(nx - 1):
            total = total + recv2[q, slot, yh].astype(f32)
        own[q, yh] = total
        return cp

    seconds, lasts = [], []
    for q in range(nchunk):
        seconds.append(second(q))
        if q >= 1:
            lasts.append(third(q - 1))
    lasts.append(third(nchunk - 1))
    for sends in seconds:
        for cp in sends:
            cp.wait_send()
    for q, cp in enumerate(lasts):
        cp.wait()
        o_ref[:, cols(q)] = own[q, yh] + recv3[q].astype(f32)


def scatter_chan(parts, nchunk=3):
    nx, nyh, ncore, rows, cells = parts.shape
    width = cells // nchunk
    f32, bf16 = jnp.float32, jnp.bfloat16
    return pl.pallas_call(
        functools.partial(scatter_kernel, nchunk),
        out_shape=jax.ShapeDtypeStruct((rows, cells), f32),
        in_specs=[pl.BlockSpec(memory_space=pltpu.VMEM)],
        out_specs=pl.BlockSpec(memory_space=pltpu.VMEM),
        scratch_shapes=[
            pltpu.VMEM((nchunk, nx, nyh, rows, width), f32),
            pltpu.VMEM((nchunk, nx, nyh, rows, width), bf16),
            pltpu.VMEM((nchunk, nyh, rows, width), f32),
            pltpu.VMEM((nchunk, nx - 1, nyh, rows, width), bf16),
            pltpu.VMEM((nchunk, rows, width), bf16),
            pltpu.VMEM((nchunk, rows, width), bf16),
            pltpu.SemaphoreType.DMA((nchunk * nx * nyh,)),
            pltpu.SemaphoreType.DMA((nchunk * nx * nyh,)),
            pltpu.SemaphoreType.DMA((nchunk * (nx - 1),)),
            pltpu.SemaphoreType.DMA((nchunk * (nx - 1),)),
            pltpu.SemaphoreType.DMA((nchunk,)),
            pltpu.SemaphoreType.DMA((nchunk,)),
        ],
        compiler_params=pltpu.CompilerParams(
            collective_id=1, has_side_effects=True, vmem_limit_bytes=48 * 1024 * 1024),
    )(parts)


def local(frames, cache, gamma, beta, kernel, bias):
    nframes, row_count, col_count, local_ch = frames.shape
    ncache = cache.shape[0]
    group_size = CH // GROUPS
    local_groups = local_ch // group_size
    nspace = lax.axis_size("space")
    me = lax.axis_index("space")
    local_members = float(nframes * row_count * col_count * group_size)

    raw = jnp.concatenate([cache, frames], axis=0)

    values = frames.astype(jnp.float32).reshape(
        nframes, row_count, col_count, local_groups, group_size
    )
    local_mean = jnp.sum(values, axis=(0, 1, 2, 4)) / local_members
    local_dev = values - local_mean[:, None]
    local_m2 = jnp.sum(local_dev * local_dev, axis=(0, 1, 2, 4))
    tile = jnp.zeros((8, 128), jnp.float32)
    tile = tile.at[0, :local_groups].set(local_mean).at[1, :local_groups].set(local_m2)
    gathered, before, after = gather_space(tile, raw[:, :, 0], raw[:, :, col_count - 1])
    before = before[:, :, None]
    after = after[:, :, None]
    means = gathered[:, 0, :local_groups]
    m2s = gathered[:, 1, :local_groups]
    group_mean = jnp.mean(means, axis=0)
    spread = jnp.sum(m2s, axis=0) + local_members * jnp.sum(
        (means - group_mean) ** 2, axis=0
    )
    group_var = spread / (local_members * nspace)
    inv = lax.rsqrt(group_var + epsilon)

    def activate(x):
        shape = x.shape
        v = x.astype(jnp.float32).reshape(shape[:-1] + (local_groups, group_size))
        scaled = (v - group_mean[:, None]) * inv[:, None]
        normed = scaled.reshape(shape) * gamma + beta
        return jax.nn.silu(normed).astype(jnp.bfloat16)

    active = activate(frames)
    joined = jnp.concatenate([cache, active], axis=0)
    left = jnp.concatenate([before[:ncache], activate(before[ncache:])], axis=0)
    right = jnp.concatenate([after[:ncache], activate(after[ncache:])], axis=0)
    left = jnp.where(me == 0, jnp.zeros_like(left), left)
    right = jnp.where(me == nspace - 1, jnp.zeros_like(right), right)
    bordered = jnp.concatenate([left, joined, right], axis=2)
    bordered = jnp.pad(bordered, ((0, 0), (1, 1), (0, 0), (0, 0)))
    cell_count = nframes * row_count * col_count
    bordered = bordered.transpose(0, 2, 1, 3)
    columns_in = jnp.concatenate(
        [
            bordered[:, col_tap : col_tap + col_count, row_tap : row_tap + row_count, :]
            for row_tap in range(3)
            for col_tap in range(3)
        ],
        axis=3,
    )
    columns_in = with_layout_constraint(columns_in, Layout(major_to_minor=(0, 1, 2, 3)))
    tap_width = columns_in.shape[3]
    nchan = lax.axis_size("chan")
    nx = nchan // 4
    flat_kernel = kernel.reshape(3, tap_width, kernel.shape[4])
    running = jnp.zeros((bias.shape[0] * nchan, cell_count), jnp.float32)
    plane = row_count * col_count
    flat_in = columns_in.reshape(columns_in.shape[0] * plane, tap_width)
    for depth in range(3):
        tap_weight = flat_kernel[depth]
        window = flat_in[depth * plane : depth * plane + cell_count]
        running = running + lax.dot_general(
            tap_weight, window, (((0,), (1,)), ((), ())), preferred_element_type=jnp.float32
        )
    summed = scatter_chan(running.reshape(nx, 2, 2, local_ch, cell_count))
    result = summed.T + bias
    result = result.astype(jnp.bfloat16).reshape(nframes, col_count, row_count, -1)
    return result.transpose(0, 2, 1, 3)


def solution(mesh):
    placed = (
        P(None, None, "space", "chan"),
        P(None, None, "space", "chan"),
        P("chan"),
        P("chan"),
        P(None, None, None, "chan", None),
        P("chan"),
    )
    return jax.shard_map(
        local, mesh=mesh, in_specs=placed, out_specs=P(None, None, "space", "chan"), check_vma=False
    )
```

```python
import functools

import jax
import jax.numpy as jnp
from jax import lax
from jax.experimental import pallas as pl
from jax.experimental.pallas import tpu as pltpu
from jax.experimental.layout import Layout, with_layout_constraint
from jax.sharding import PartitionSpec as P

CH = 512
GROUPS = 32
MESH = pl.DeviceIdType.MESH

epsilon = 1e-06


def gather_kernel(n, nrow, x_ref, lo_ref, hi_ref, o_ref, left_ref, right_ref,
                  part, full, left_buf, right_buf, local_sem, a_send, a_recv, b_send, b_recv,
                  edge_send, edge_recv):
    me = lax.axis_index("space")
    ch = lax.axis_index("chan")
    ncol = n // nrow
    zz = me // nrow
    yy = me % nrow
    right = lax.rem(me + 1, n)
    left = lax.rem(me + n - 1, n)
    row_peers = [(zz * nrow + lax.rem(yy + k, nrow), lax.rem(yy + k, nrow)) for k in range(1, nrow)]
    col_peers = [(lax.rem(zz + k, ncol) * nrow + yy, lax.rem(zz + k, ncol)) for k in range(1, ncol)]
    barrier = pltpu.get_barrier_semaphore()
    for peer, _ in row_peers + col_peers:
        pl.semaphore_signal(barrier, 1, device_id=(peer, ch), device_id_type=MESH)
    for peer in (left, right):
        pl.semaphore_signal(barrier, 1, device_id=(peer, ch), device_id_type=MESH)
    pl.semaphore_wait(barrier, len(row_peers) + len(col_peers) + 2)

    to_right = pltpu.make_async_remote_copy(
        src_ref=hi_ref, dst_ref=left_buf, send_sem=edge_send.at[0], recv_sem=edge_recv.at[0],
        device_id=(right, ch), device_id_type=MESH)
    to_left = pltpu.make_async_remote_copy(
        src_ref=lo_ref, dst_ref=right_buf, send_sem=edge_send.at[1], recv_sem=edge_recv.at[1],
        device_id=(left, ch), device_id_type=MESH)
    to_right.start()
    to_left.start()

    sends = []
    for peer, slot in row_peers:
        cp = pltpu.make_async_remote_copy(
            src_ref=x_ref, dst_ref=part.at[yy], send_sem=a_send.at[slot], recv_sem=a_recv.at[yy],
            device_id=(peer, ch), device_id_type=MESH)
        cp.start()
        sends.append(cp)
    own = pltpu.make_async_copy(x_ref, part.at[yy], local_sem.at[0])
    own.start()
    for peer, slot in row_peers:
        pltpu.make_async_remote_copy(
            src_ref=x_ref, dst_ref=part.at[slot], send_sem=a_send.at[slot], recv_sem=a_recv.at[slot],
            device_id=(peer, ch), device_id_type=MESH).wait_recv()
    own.wait()
    for peer, slot in col_peers:
        cp = pltpu.make_async_remote_copy(
            src_ref=part, dst_ref=full.at[zz], send_sem=b_send.at[slot], recv_sem=b_recv.at[zz],
            device_id=(peer, ch), device_id_type=MESH)
        cp.start()
        sends.append(cp)
    own = pltpu.make_async_copy(part, full.at[zz], local_sem.at[1])
    own.start()
    for peer, slot in col_peers:
        pltpu.make_async_remote_copy(
            src_ref=part, dst_ref=full.at[slot], send_sem=b_send.at[slot], recv_sem=b_recv.at[slot],
            device_id=(peer, ch), device_id_type=MESH).wait_recv()
    own.wait()
    for cp in sends:
        cp.wait_send()
    o_ref[...] = full[...]
    to_right.wait()
    to_left.wait()
    left_ref[...] = left_buf[...]
    right_ref[...] = right_buf[...]


def gather_space(tile, lo, hi, nrow=4):
    n = lax.axis_size("space")
    ncol = n // nrow
    vmem = pl.BlockSpec(memory_space=pltpu.VMEM)
    gathered, before, after = pl.pallas_call(
        functools.partial(gather_kernel, n, nrow),
        out_shape=(
            jax.ShapeDtypeStruct((ncol, nrow) + tile.shape, tile.dtype),
            jax.ShapeDtypeStruct(hi.shape, hi.dtype),
            jax.ShapeDtypeStruct(lo.shape, lo.dtype),
        ),
        in_specs=[vmem, vmem, vmem],
        out_specs=(vmem, vmem, vmem),
        scratch_shapes=[
            pltpu.VMEM((nrow,) + tile.shape, tile.dtype),
            pltpu.VMEM((ncol, nrow) + tile.shape, tile.dtype),
            pltpu.VMEM(hi.shape, hi.dtype),
            pltpu.VMEM(lo.shape, lo.dtype),
            pltpu.SemaphoreType.DMA((2,)),
            pltpu.SemaphoreType.DMA((nrow,)),
            pltpu.SemaphoreType.DMA((nrow,)),
            pltpu.SemaphoreType.DMA((ncol,)),
            pltpu.SemaphoreType.DMA((ncol,)),
            pltpu.SemaphoreType.DMA((2,)),
            pltpu.SemaphoreType.DMA((2,)),
        ],
        compiler_params=pltpu.CompilerParams(collective_id=0, has_side_effects=True),
    )(tile, lo, hi)
    return gathered.reshape((n,) + tile.shape), before, after


def scatter_kernel(nchunk, x_ref, o_ref, recv1, acc1, own, recv2, acc2, recv3,
                   sem1s, sem1r, sem2s, sem2r, sem3s, sem3r):
    sp = lax.axis_index("space")
    c = lax.axis_index("chan")
    core = c % 2
    yh = (c // 2) % 2
    xx = c // 4
    nx, nyh = x_ref.shape[0], x_ref.shape[1]
    width = x_ref.shape[-1] // nchunk
    f32, bf16 = jnp.float32, jnp.bfloat16

    def dev(x_, yh_, core_):
        return (sp, x_ * 4 + yh_ * 2 + core_)

    peers = [dev(xx, yh, 1 - core)]
    peers += [dev(lax.rem(xx + k, nx), yh, core) for k in range(1, nx)]
    peers += [dev(xx, 1 - yh, core)]
    barrier = pltpu.get_barrier_semaphore()
    for p in peers:
        pl.semaphore_signal(barrier, 1, device_id=p, device_id_type=MESH)
    pl.semaphore_wait(barrier, len(peers))

    def cols(q):
        return pl.ds(q * width, width)

    firsts = []
    for q in range(nchunk):
        for i in range(nx):
            for j in range(nyh):
                n = (q * nx + i) * nyh + j
                cp = pltpu.make_async_remote_copy(
                    src_ref=x_ref.at[i, j, 1 - core, :, cols(q)], dst_ref=recv1.at[q, i, j],
                    send_sem=sem1s.at[n], recv_sem=sem1r.at[n],
                    device_id=peers[0], device_id_type=MESH)
                cp.start()
                firsts.append(cp)

    def second(q):
        for cp in firsts[q * nx * nyh : (q + 1) * nx * nyh]:
            cp.wait()
        sends = []
        for k in range(1, nx):
            dest = lax.rem(xx + k, nx)
            for j in range(nyh):
                acc1[q, dest, j] = (x_ref[dest, j, core, :, cols(q)] + recv1[q, dest, j]).astype(bf16)
            slot = nx - 1 - k
            cp = pltpu.make_async_remote_copy(
                src_ref=acc1.at[q, dest], dst_ref=recv2.at[q, slot],
                send_sem=sem2s.at[q * (nx - 1) + k - 1], recv_sem=sem2r.at[q * (nx - 1) + slot],
                device_id=peers[k], device_id_type=MESH)
            cp.start()
            sends.append(cp)
        for j in range(nyh):
            own[q, j] = x_ref[xx, j, core, :, cols(q)] + recv1[q, xx, j]
        return sends

    def third(q):
        for slot in range(nx - 1):
            pltpu.make_async_remote_copy(
                src_ref=acc1.at[q, xx], dst_ref=recv2.at[q, slot],
                send_sem=sem2s.at[q * (nx - 1) + slot], recv_sem=sem2r.at[q * (nx - 1) + slot],
                device_id=peers[0], device_id_type=MESH).wait_recv()
        other = 1 - yh
        total = own[q, other]
        for slot in range(nx - 1):
            total = total + recv2[q, slot, other].astype(f32)
        acc2[q] = total.astype(bf16)
        cp = pltpu.make_async_remote_copy(
            src_ref=acc2.at[q], dst_ref=recv3.at[q], send_sem=sem3s.at[q],
            recv_sem=sem3r.at[q], device_id=peers[nx], device_id_type=MESH)
        cp.start()
        total = own[q, yh]
        for slot in range(nx - 1):
            total = total + recv2[q, slot, yh].astype(f32)
        own[q, yh] = total
        return cp

    seconds, lasts = [], []
    for q in range(nchunk):
        seconds.append(second(q))
        if q >= 1:
            lasts.append(third(q - 1))
    lasts.append(third(nchunk - 1))
    for sends in seconds:
        for cp in sends:
            cp.wait_send()
    for q, cp in enumerate(lasts):
        cp.wait()
        o_ref[:, cols(q)] = own[q, yh] + recv3[q].astype(f32)


def scatter_chan(parts, nchunk=3):
    nx, nyh, ncore, rows, cells = parts.shape
    width = cells // nchunk
    f32, bf16 = jnp.float32, jnp.bfloat16
    return pl.pallas_call(
        functools.partial(scatter_kernel, nchunk),
        out_shape=jax.ShapeDtypeStruct((rows, cells), f32),
        in_specs=[pl.BlockSpec(memory_space=pltpu.VMEM)],
        out_specs=pl.BlockSpec(memory_space=pltpu.VMEM),
        scratch_shapes=[
            pltpu.VMEM((nchunk, nx, nyh, rows, width), f32),
            pltpu.VMEM((nchunk, nx, nyh, rows, width), bf16),
            pltpu.VMEM((nchunk, nyh, rows, width), f32),
            pltpu.VMEM((nchunk, nx - 1, nyh, rows, width), bf16),
            pltpu.VMEM((nchunk, rows, width), bf16),
            pltpu.VMEM((nchunk, rows, width), bf16),
            pltpu.SemaphoreType.DMA((nchunk * nx * nyh,)),
            pltpu.SemaphoreType.DMA((nchunk * nx * nyh,)),
            pltpu.SemaphoreType.DMA((nchunk * (nx - 1),)),
            pltpu.SemaphoreType.DMA((nchunk * (nx - 1),)),
            pltpu.SemaphoreType.DMA((nchunk,)),
            pltpu.SemaphoreType.DMA((nchunk,)),
        ],
        compiler_params=pltpu.CompilerParams(
            collective_id=1, has_side_effects=True, vmem_limit_bytes=48 * 1024 * 1024),
    )(parts)


def local(frames, cache, gamma, beta, kernel, bias):
    nframes, row_count, col_count, local_ch = frames.shape
    ncache = cache.shape[0]
    group_size = CH // GROUPS
    local_groups = local_ch // group_size
    nspace = lax.axis_size("space")
    me = lax.axis_index("space")
    local_members = float(nframes * row_count * col_count * group_size)

    raw = jnp.concatenate([cache, frames], axis=0)

    values = frames.astype(jnp.float32).reshape(
        nframes, row_count, col_count, local_groups, group_size
    )
    local_mean = jnp.sum(values, axis=(0, 1, 2, 4)) / local_members
    local_dev = values - local_mean[:, None]
    local_m2 = jnp.sum(local_dev * local_dev, axis=(0, 1, 2, 4))
    tile = jnp.zeros((8, 128), jnp.float32)
    tile = tile.at[0, :local_groups].set(local_mean).at[1, :local_groups].set(local_m2)
    gathered, before, after = gather_space(tile, raw[:, :, 0], raw[:, :, col_count - 1])
    before = before[:, :, None]
    after = after[:, :, None]
    means = gathered[:, 0, :local_groups]
    m2s = gathered[:, 1, :local_groups]
    group_mean = jnp.mean(means, axis=0)
    spread = jnp.sum(m2s, axis=0) + local_members * jnp.sum(
        (means - group_mean) ** 2, axis=0
    )
    group_var = spread / (local_members * nspace)
    inv = lax.rsqrt(group_var + epsilon)

    def activate(x):
        shape = x.shape
        v = x.astype(jnp.float32).reshape(shape[:-1] + (local_groups, group_size))
        scaled = (v - group_mean[:, None]) * inv[:, None]
        normed = scaled.reshape(shape) * gamma + beta
        return jax.nn.silu(normed).astype(jnp.bfloat16)

    active = activate(frames)
    joined = jnp.concatenate([cache, active], axis=0)
    left = jnp.concatenate([before[:ncache], activate(before[ncache:])], axis=0)
    right = jnp.concatenate([after[:ncache], activate(after[ncache:])], axis=0)
    left = jnp.where(me == 0, jnp.zeros_like(left), left)
    right = jnp.where(me == nspace - 1, jnp.zeros_like(right), right)
    bordered = jnp.concatenate([left, joined, right], axis=2)
    bordered = jnp.pad(bordered, ((0, 0), (1, 1), (0, 0), (0, 0)))
    cell_count = nframes * row_count * col_count
    bordered = bordered.transpose(0, 2, 1, 3)
    columns_in = jnp.concatenate(
        [
            bordered[:, col_tap : col_tap + col_count, row_tap : row_tap + row_count, :]
            for row_tap in range(3)
            for col_tap in range(3)
        ],
        axis=3,
    )
    columns_in = with_layout_constraint(columns_in, Layout(major_to_minor=(0, 1, 2, 3)))
    tap_width = columns_in.shape[3]
    nchan = lax.axis_size("chan")
    nx = nchan // 4
    flat_kernel = kernel.reshape(3, tap_width, kernel.shape[4])
    running = jnp.zeros((bias.shape[0] * nchan, cell_count), jnp.float32)
    plane = row_count * col_count
    flat_in = columns_in.reshape(columns_in.shape[0] * plane, tap_width)
    for depth in range(3):
        tap_weight = flat_kernel[depth]
        window = flat_in[depth * plane : depth * plane + cell_count]
        running = running + lax.dot_general(
            tap_weight, window, (((0,), (1,)), ((), ())), preferred_element_type=jnp.float32
        )
    summed = scatter_chan(running.reshape(nx, 2, 2, local_ch, cell_count))
    result = summed.T + bias
    result = result.astype(jnp.bfloat16).reshape(nframes, col_count, row_count, -1)
    return result.transpose(0, 2, 1, 3)


def solution(mesh):
    placed = (
        P(None, None, "space", "chan"),
        P(None, None, "space", "chan"),
        P("chan"),
        P("chan"),
        P(None, None, None, "chan", None),
        P("chan"),
    )
    return jax.shard_map(
        local, mesh=mesh, in_specs=placed, out_specs=P(None, None, "space", "chan"), check_vma=False
    )
```

```python
import functools

import jax
import jax.numpy as jnp
from jax import lax
from jax.experimental import pallas as pl
from jax.experimental.pallas import tpu as pltpu
from jax.experimental.layout import Layout, with_layout_constraint
from jax.sharding import PartitionSpec as P

CH = 512
GROUPS = 32
MESH = pl.DeviceIdType.MESH

epsilon = 1e-06


def gather_kernel(n, x_ref, lo_ref, hi_ref, o_ref, left_ref, right_ref,
                  buf, left_buf, right_buf, send_sem, recv_sem, edge_send, edge_recv):
    me = lax.axis_index("space")
    ch = lax.axis_index("chan")
    right = lax.rem(me + 1, n)
    left = lax.rem(me + n - 1, n)
    barrier = pltpu.get_barrier_semaphore()

    def signal(k, carry):
        peer = lax.rem(me + k, n)
        pl.semaphore_signal(barrier, 1, device_id=(peer, ch), device_id_type=MESH)
        return carry

    lax.fori_loop(1, n, signal, 0)
    pl.semaphore_wait(barrier, n - 1)

    to_right = pltpu.make_async_remote_copy(
        src_ref=hi_ref, dst_ref=left_buf, send_sem=edge_send.at[0], recv_sem=edge_recv.at[0],
        device_id=(right, ch), device_id_type=MESH)
    to_left = pltpu.make_async_remote_copy(
        src_ref=lo_ref, dst_ref=right_buf, send_sem=edge_send.at[1], recv_sem=edge_recv.at[1],
        device_id=(left, ch), device_id_type=MESH)
    to_right.start()
    to_left.start()

    def copy_to(peer):
        return pltpu.make_async_remote_copy(
            src_ref=x_ref,
            dst_ref=buf.at[me],
            send_sem=send_sem.at[peer],
            recv_sem=recv_sem.at[me],
            device_id=(peer, ch),
            device_id_type=MESH,
        )

    def copy_from(peer):
        return pltpu.make_async_remote_copy(
            src_ref=x_ref,
            dst_ref=buf.at[peer],
            send_sem=send_sem.at[peer],
            recv_sem=recv_sem.at[peer],
            device_id=(peer, ch),
            device_id_type=MESH,
        )

    def start(k, carry):
        copy_to(lax.rem(me + k, n)).start()
        return carry

    lax.fori_loop(1, n, start, 0)

    def finish(k, carry):
        peer = lax.rem(me + k, n)
        copy_to(peer).wait_send()
        copy_from(peer).wait_recv()
        return carry

    lax.fori_loop(1, n, finish, 0)
    buf[me] = x_ref[...]
    o_ref[...] = buf[...]
    to_right.wait()
    to_left.wait()
    left_ref[...] = left_buf[...]
    right_ref[...] = right_buf[...]


def gather_space(tile, lo, hi):
    n = lax.axis_size("space")
    vmem = pl.BlockSpec(memory_space=pltpu.VMEM)
    return pl.pallas_call(
        functools.partial(gather_kernel, n),
        out_shape=(
            jax.ShapeDtypeStruct((n,) + tile.shape, tile.dtype),
            jax.ShapeDtypeStruct(hi.shape, hi.dtype),
            jax.ShapeDtypeStruct(lo.shape, lo.dtype),
        ),
        in_specs=[vmem, vmem, vmem],
        out_specs=(vmem, vmem, vmem),
        scratch_shapes=[
            pltpu.VMEM((n,) + tile.shape, tile.dtype),
            pltpu.VMEM(hi.shape, hi.dtype),
            pltpu.VMEM(lo.shape, lo.dtype),
            pltpu.SemaphoreType.DMA((n,)),
            pltpu.SemaphoreType.DMA((n,)),
            pltpu.SemaphoreType.DMA((2,)),
            pltpu.SemaphoreType.DMA((2,)),
        ],
        compiler_params=pltpu.CompilerParams(collective_id=0, has_side_effects=True),
    )(tile, lo, hi)


def scatter_kernel(nchunk, x_ref, o_ref, half, recv1, acc1, own, recv2, acc2, recv3,
                   sem1s, sem1r, sem2s, sem2r, sem3s, sem3r):
    sp = lax.axis_index("space")
    c = lax.axis_index("chan")
    core = c % 2
    yh = (c // 2) % 2
    xx = c // 4
    nx, nyh = x_ref.shape[0], x_ref.shape[1]
    width = x_ref.shape[-1] // nchunk
    f32, bf16 = jnp.float32, jnp.bfloat16

    def dev(x_, yh_, core_):
        return (sp, x_ * 4 + yh_ * 2 + core_)

    peers = [dev(xx, yh, 1 - core)]
    peers += [dev(lax.rem(xx + k, nx), yh, core) for k in range(1, nx)]
    peers += [dev(xx, 1 - yh, core)]
    barrier = pltpu.get_barrier_semaphore()
    for p in peers:
        pl.semaphore_signal(barrier, 1, device_id=p, device_id_type=MESH)
    pl.semaphore_wait(barrier, len(peers))

    def cols(q):
        return pl.ds(q * width, width)

    firsts = []
    for q in range(nchunk):
        for i in range(nx):
            for j in range(nyh):
                n = (q * nx + i) * nyh + j
                half[q, i, j] = x_ref[i, j, 1 - core, :, cols(q)].astype(bf16)
                cp = pltpu.make_async_remote_copy(
                    src_ref=half.at[q, i, j], dst_ref=recv1.at[q, i, j],
                    send_sem=sem1s.at[n], recv_sem=sem1r.at[n],
                    device_id=peers[0], device_id_type=MESH)
                cp.start()
                firsts.append(cp)

    def second(q):
        for cp in firsts[q * nx * nyh : (q + 1) * nx * nyh]:
            cp.wait()
        sends = []
        for k in range(1, nx):
            dest = lax.rem(xx + k, nx)
            for j in range(nyh):
                acc1[q, dest, j] = (
                    x_ref[dest, j, core, :, cols(q)] + recv1[q, dest, j].astype(f32)
                ).astype(bf16)
            slot = nx - 1 - k
            cp = pltpu.make_async_remote_copy(
                src_ref=acc1.at[q, dest], dst_ref=recv2.at[q, slot],
                send_sem=sem2s.at[q * (nx - 1) + k - 1], recv_sem=sem2r.at[q * (nx - 1) + slot],
                device_id=peers[k], device_id_type=MESH)
            cp.start()
            sends.append(cp)
        for j in range(nyh):
            own[q, j] = x_ref[xx, j, core, :, cols(q)] + recv1[q, xx, j].astype(f32)
        return sends

    def third(q):
        for slot in range(nx - 1):
            pltpu.make_async_remote_copy(
                src_ref=acc1.at[q, xx], dst_ref=recv2.at[q, slot],
                send_sem=sem2s.at[q * (nx - 1) + slot], recv_sem=sem2r.at[q * (nx - 1) + slot],
                device_id=peers[0], device_id_type=MESH).wait_recv()
        other = 1 - yh
        total = own[q, other]
        for slot in range(nx - 1):
            total = total + recv2[q, slot, other].astype(f32)
        acc2[q] = total.astype(bf16)
        cp = pltpu.make_async_remote_copy(
            src_ref=acc2.at[q], dst_ref=recv3.at[q], send_sem=sem3s.at[q],
            recv_sem=sem3r.at[q], device_id=peers[nx], device_id_type=MESH)
        cp.start()
        total = own[q, yh]
        for slot in range(nx - 1):
            total = total + recv2[q, slot, yh].astype(f32)
        own[q, yh] = total
        return cp

    seconds, lasts = [], []
    for q in range(nchunk):
        seconds.append(second(q))
        if q >= 1:
            lasts.append(third(q - 1))
    lasts.append(third(nchunk - 1))
    for sends in seconds:
        for cp in sends:
            cp.wait_send()
    for q, cp in enumerate(lasts):
        cp.wait()
        o_ref[:, cols(q)] = own[q, yh] + recv3[q].astype(f32)


def scatter_chan(parts, nchunk=3):
    nx, nyh, ncore, rows, cells = parts.shape
    width = cells // nchunk
    f32, bf16 = jnp.float32, jnp.bfloat16
    return pl.pallas_call(
        functools.partial(scatter_kernel, nchunk),
        out_shape=jax.ShapeDtypeStruct((rows, cells), f32),
        in_specs=[pl.BlockSpec(memory_space=pltpu.VMEM)],
        out_specs=pl.BlockSpec(memory_space=pltpu.VMEM),
        scratch_shapes=[
            pltpu.VMEM((nchunk, nx, nyh, rows, width), bf16),
            pltpu.VMEM((nchunk, nx, nyh, rows, width), bf16),
            pltpu.VMEM((nchunk, nx, nyh, rows, width), bf16),
            pltpu.VMEM((nchunk, nyh, rows, width), f32),
            pltpu.VMEM((nchunk, nx - 1, nyh, rows, width), bf16),
            pltpu.VMEM((nchunk, rows, width), bf16),
            pltpu.VMEM((nchunk, rows, width), bf16),
            pltpu.SemaphoreType.DMA((nchunk * nx * nyh,)),
            pltpu.SemaphoreType.DMA((nchunk * nx * nyh,)),
            pltpu.SemaphoreType.DMA((nchunk * (nx - 1),)),
            pltpu.SemaphoreType.DMA((nchunk * (nx - 1),)),
            pltpu.SemaphoreType.DMA((nchunk,)),
            pltpu.SemaphoreType.DMA((nchunk,)),
        ],
        compiler_params=pltpu.CompilerParams(
            collective_id=1, has_side_effects=True, vmem_limit_bytes=48 * 1024 * 1024),
    )(parts)


def local(frames, cache, gamma, beta, kernel, bias):
    nframes, row_count, col_count, local_ch = frames.shape
    ncache = cache.shape[0]
    group_size = CH // GROUPS
    local_groups = local_ch // group_size
    nspace = lax.axis_size("space")
    me = lax.axis_index("space")
    local_members = float(nframes * row_count * col_count * group_size)

    raw = jnp.concatenate([cache, frames], axis=0)

    values = frames.astype(jnp.float32).reshape(
        nframes, row_count, col_count, local_groups, group_size
    )
    local_mean = jnp.sum(values, axis=(0, 1, 2, 4)) / local_members
    local_dev = values - local_mean[:, None]
    local_m2 = jnp.sum(local_dev * local_dev, axis=(0, 1, 2, 4))
    tile = jnp.zeros((8, 128), jnp.float32)
    tile = tile.at[0, :local_groups].set(local_mean).at[1, :local_groups].set(local_m2)
    gathered, before, after = gather_space(tile, raw[:, :, 0], raw[:, :, col_count - 1])
    before = before[:, :, None]
    after = after[:, :, None]
    means = gathered[:, 0, :local_groups]
    m2s = gathered[:, 1, :local_groups]
    group_mean = jnp.mean(means, axis=0)
    spread = jnp.sum(m2s, axis=0) + local_members * jnp.sum(
        (means - group_mean) ** 2, axis=0
    )
    group_var = spread / (local_members * nspace)
    inv = lax.rsqrt(group_var + epsilon)

    def activate(x):
        shape = x.shape
        v = x.astype(jnp.float32).reshape(shape[:-1] + (local_groups, group_size))
        scaled = (v - group_mean[:, None]) * inv[:, None]
        normed = scaled.reshape(shape) * gamma + beta
        return jax.nn.silu(normed).astype(jnp.bfloat16)

    active = activate(frames)
    joined = jnp.concatenate([cache, active], axis=0)
    left = jnp.concatenate([before[:ncache], activate(before[ncache:])], axis=0)
    right = jnp.concatenate([after[:ncache], activate(after[ncache:])], axis=0)
    left = jnp.where(me == 0, jnp.zeros_like(left), left)
    right = jnp.where(me == nspace - 1, jnp.zeros_like(right), right)
    bordered = jnp.concatenate([left, joined, right], axis=2)
    bordered = jnp.pad(bordered, ((0, 0), (1, 1), (0, 0), (0, 0)))
    cell_count = nframes * row_count * col_count
    bordered = bordered.transpose(0, 2, 1, 3)
    columns_in = jnp.concatenate(
        [
            bordered[:, col_tap : col_tap + col_count, row_tap : row_tap + row_count, :]
            for row_tap in range(3)
            for col_tap in range(3)
        ],
        axis=3,
    )
    columns_in = with_layout_constraint(columns_in, Layout(major_to_minor=(0, 1, 2, 3)))
    tap_width = columns_in.shape[3]
    nchan = lax.axis_size("chan")
    nx = nchan // 4
    flat_kernel = kernel.reshape(3, tap_width, kernel.shape[4])
    running = jnp.zeros((bias.shape[0] * nchan, cell_count), jnp.float32)
    plane = row_count * col_count
    flat_in = columns_in.reshape(columns_in.shape[0] * plane, tap_width)
    for depth in range(3):
        tap_weight = flat_kernel[depth]
        window = flat_in[depth * plane : depth * plane + cell_count]
        running = running + lax.dot_general(
            tap_weight, window, (((0,), (1,)), ((), ())), preferred_element_type=jnp.float32
        )
    summed = scatter_chan(running.reshape(nx, 2, 2, local_ch, cell_count))
    result = summed.T + bias
    result = result.astype(jnp.bfloat16).reshape(nframes, col_count, row_count, -1)
    return result.transpose(0, 2, 1, 3)


def solution(mesh):
    placed = (
        P(None, None, "space", "chan"),
        P(None, None, "space", "chan"),
        P("chan"),
        P("chan"),
        P(None, None, None, "chan", None),
        P("chan"),
    )
    return jax.shard_map(
        local, mesh=mesh, in_specs=placed, out_specs=P(None, None, "space", "chan"), check_vma=False
    )
```

```python
import functools

import jax
import jax.numpy as jnp
from jax import lax
from jax.experimental import pallas as pl
from jax.experimental.pallas import tpu as pltpu
from jax.experimental.layout import Layout, with_layout_constraint
from jax.sharding import PartitionSpec as P

CH = 512
GROUPS = 32
MESH = pl.DeviceIdType.MESH

epsilon = 1e-06


def gather_kernel(n, x_ref, lo_ref, hi_ref, o_ref, left_ref, right_ref,
                  buf, left_buf, right_buf, send_sem, recv_sem, edge_send, edge_recv):
    me = lax.axis_index("space")
    ch = lax.axis_index("chan")
    right = lax.rem(me + 1, n)
    left = lax.rem(me + n - 1, n)
    barrier = pltpu.get_barrier_semaphore()

    def signal(k, carry):
        peer = lax.rem(me + k, n)
        pl.semaphore_signal(barrier, 1, device_id=(peer, ch), device_id_type=MESH)
        return carry

    lax.fori_loop(1, n, signal, 0)
    pl.semaphore_wait(barrier, n - 1)

    to_right = pltpu.make_async_remote_copy(
        src_ref=hi_ref, dst_ref=left_buf, send_sem=edge_send.at[0], recv_sem=edge_recv.at[0],
        device_id=(right, ch), device_id_type=MESH)
    to_left = pltpu.make_async_remote_copy(
        src_ref=lo_ref, dst_ref=right_buf, send_sem=edge_send.at[1], recv_sem=edge_recv.at[1],
        device_id=(left, ch), device_id_type=MESH)
    to_right.start()
    to_left.start()

    def copy_to(peer):
        return pltpu.make_async_remote_copy(
            src_ref=x_ref,
            dst_ref=buf.at[me],
            send_sem=send_sem.at[peer],
            recv_sem=recv_sem.at[me],
            device_id=(peer, ch),
            device_id_type=MESH,
        )

    def copy_from(peer):
        return pltpu.make_async_remote_copy(
            src_ref=x_ref,
            dst_ref=buf.at[peer],
            send_sem=send_sem.at[peer],
            recv_sem=recv_sem.at[peer],
            device_id=(peer, ch),
            device_id_type=MESH,
        )

    def start(k, carry):
        copy_to(lax.rem(me + k, n)).start()
        return carry

    lax.fori_loop(1, n, start, 0)

    def finish(k, carry):
        peer = lax.rem(me + k, n)
        copy_to(peer).wait_send()
        copy_from(peer).wait_recv()
        return carry

    lax.fori_loop(1, n, finish, 0)
    buf[me] = x_ref[...]
    o_ref[...] = buf[...]
    to_right.wait()
    to_left.wait()
    left_ref[...] = left_buf[...]
    right_ref[...] = right_buf[...]


def gather_space(tile, lo, hi):
    n = lax.axis_size("space")
    vmem = pl.BlockSpec(memory_space=pltpu.VMEM)
    return pl.pallas_call(
        functools.partial(gather_kernel, n),
        out_shape=(
            jax.ShapeDtypeStruct((n,) + tile.shape, tile.dtype),
            jax.ShapeDtypeStruct(hi.shape, hi.dtype),
            jax.ShapeDtypeStruct(lo.shape, lo.dtype),
        ),
        in_specs=[vmem, vmem, vmem],
        out_specs=(vmem, vmem, vmem),
        scratch_shapes=[
            pltpu.VMEM((n,) + tile.shape, tile.dtype),
            pltpu.VMEM(hi.shape, hi.dtype),
            pltpu.VMEM(lo.shape, lo.dtype),
            pltpu.SemaphoreType.DMA((n,)),
            pltpu.SemaphoreType.DMA((n,)),
            pltpu.SemaphoreType.DMA((2,)),
            pltpu.SemaphoreType.DMA((2,)),
        ],
        compiler_params=pltpu.CompilerParams(collective_id=0, has_side_effects=True),
    )(tile, lo, hi)


def scatter_kernel(nchunk, x_ref, o_ref, recv1, acc1, own, recv2, relay, acc2, recv3,
                   sem1s, sem1r, sem2s, sem2r, sem3s, sem3r):
    sp = lax.axis_index("space")
    c = lax.axis_index("chan")
    core = c % 2
    yh = (c // 2) % 2
    xx = c // 4
    nx, nyh = x_ref.shape[0], x_ref.shape[1]
    width = x_ref.shape[-1] // nchunk
    f32, bf16 = jnp.float32, jnp.bfloat16

    def dev(x_, yh_, core_):
        return (sp, x_ * 4 + yh_ * 2 + core_)

    peers = [dev(xx, yh, 1 - core)]
    peers += [dev(lax.rem(xx + k, nx), yh, core) for k in range(1, nx)]
    peers += [dev(xx, 1 - yh, core)]
    barrier = pltpu.get_barrier_semaphore()
    for p in peers:
        pl.semaphore_signal(barrier, 1, device_id=p, device_id_type=MESH)
    pl.semaphore_wait(barrier, len(peers))

    def cols(q):
        return pl.ds(q * width, width)

    firsts = []
    for q in range(nchunk):
        for i in range(nx):
            for j in range(nyh):
                n = (q * nx + i) * nyh + j
                cp = pltpu.make_async_remote_copy(
                    src_ref=x_ref.at[i, j, 1 - core, :, cols(q)], dst_ref=recv1.at[q, i, j],
                    send_sem=sem1s.at[n], recv_sem=sem1r.at[n],
                    device_id=peers[0], device_id_type=MESH)
                cp.start()
                firsts.append(cp)

    east = lax.rem(xx + 1, nx)
    west = lax.rem(xx + nx - 1, nx)
    across = lax.rem(xx + 2, nx)

    def rcopy(src, dst, q, n, peer):
        return pltpu.make_async_remote_copy(
            src_ref=src, dst_ref=dst, send_sem=sem2s.at[q * 6 + n], recv_sem=sem2r.at[q * 6 + n],
            device_id=peer, device_id_type=MESH)

    def second(q):
        for cp in firsts[q * nx * nyh : (q + 1) * nx * nyh]:
            cp.wait()
        for dest in (east, west, across):
            for j in range(nyh):
                acc1[q, dest, j] = (x_ref[dest, j, core, :, cols(q)] + recv1[q, dest, j]).astype(bf16)
        sends = [
            rcopy(acc1.at[q, east], recv2.at[q, 0], q, 0, peers[1]),
            rcopy(acc1.at[q, west], recv2.at[q, 1], q, 1, peers[3]),
            rcopy(acc1.at[q, across, 0], relay.at[q, 0], q, 2, peers[1]),
            rcopy(acc1.at[q, across, 1], relay.at[q, 1], q, 3, peers[3]),
        ]
        for cp in sends:
            cp.start()
        for j in range(nyh):
            own[q, j] = x_ref[xx, j, core, :, cols(q)] + recv1[q, xx, j]
        rcopy(acc1.at[q, across, 0], relay.at[q, 0], q, 2, peers[1]).wait_recv()
        fwd = rcopy(relay.at[q, 0], recv2.at[q, 2, 0], q, 4, peers[1])
        fwd.start()
        sends.append(fwd)
        rcopy(acc1.at[q, across, 1], relay.at[q, 1], q, 3, peers[3]).wait_recv()
        fwd = rcopy(relay.at[q, 1], recv2.at[q, 2, 1], q, 5, peers[3])
        fwd.start()
        sends.append(fwd)
        return sends

    def third(q):
        rcopy(acc1.at[q, east], recv2.at[q, 0], q, 0, peers[1]).wait_recv()
        rcopy(acc1.at[q, west], recv2.at[q, 1], q, 1, peers[3]).wait_recv()
        rcopy(relay.at[q, 0], recv2.at[q, 2, 0], q, 4, peers[1]).wait_recv()
        rcopy(relay.at[q, 1], recv2.at[q, 2, 1], q, 5, peers[3]).wait_recv()
        other = 1 - yh
        total = own[q, other]
        for slot in range(nx - 1):
            total = total + recv2[q, slot, other].astype(f32)
        acc2[q] = total.astype(bf16)
        cp = pltpu.make_async_remote_copy(
            src_ref=acc2.at[q], dst_ref=recv3.at[q], send_sem=sem3s.at[q],
            recv_sem=sem3r.at[q], device_id=peers[nx], device_id_type=MESH)
        cp.start()
        total = own[q, yh]
        for slot in range(nx - 1):
            total = total + recv2[q, slot, yh].astype(f32)
        own[q, yh] = total
        return cp

    seconds, lasts = [], []
    for q in range(nchunk):
        seconds.append(second(q))
        if q >= 1:
            lasts.append(third(q - 1))
    lasts.append(third(nchunk - 1))
    for sends in seconds:
        for cp in sends:
            cp.wait_send()
    for q, cp in enumerate(lasts):
        cp.wait()
        o_ref[:, cols(q)] = own[q, yh] + recv3[q].astype(f32)


def scatter_chan(parts, nchunk=3):
    nx, nyh, ncore, rows, cells = parts.shape
    width = cells // nchunk
    f32, bf16 = jnp.float32, jnp.bfloat16
    return pl.pallas_call(
        functools.partial(scatter_kernel, nchunk),
        out_shape=jax.ShapeDtypeStruct((rows, cells), f32),
        in_specs=[pl.BlockSpec(memory_space=pltpu.VMEM)],
        out_specs=pl.BlockSpec(memory_space=pltpu.VMEM),
        scratch_shapes=[
            pltpu.VMEM((nchunk, nx, nyh, rows, width), f32),
            pltpu.VMEM((nchunk, nx, nyh, rows, width), bf16),
            pltpu.VMEM((nchunk, nyh, rows, width), f32),
            pltpu.VMEM((nchunk, nx - 1, nyh, rows, width), bf16),
            pltpu.VMEM((nchunk, nyh, rows, width), bf16),
            pltpu.VMEM((nchunk, rows, width), bf16),
            pltpu.VMEM((nchunk, rows, width), bf16),
            pltpu.SemaphoreType.DMA((nchunk * nx * nyh,)),
            pltpu.SemaphoreType.DMA((nchunk * nx * nyh,)),
            pltpu.SemaphoreType.DMA((nchunk * 6,)),
            pltpu.SemaphoreType.DMA((nchunk * 6,)),
            pltpu.SemaphoreType.DMA((nchunk,)),
            pltpu.SemaphoreType.DMA((nchunk,)),
        ],
        compiler_params=pltpu.CompilerParams(
            collective_id=1, has_side_effects=True, vmem_limit_bytes=48 * 1024 * 1024),
    )(parts)


def local(frames, cache, gamma, beta, kernel, bias):
    nframes, row_count, col_count, local_ch = frames.shape
    ncache = cache.shape[0]
    group_size = CH // GROUPS
    local_groups = local_ch // group_size
    nspace = lax.axis_size("space")
    me = lax.axis_index("space")
    local_members = float(nframes * row_count * col_count * group_size)

    raw = jnp.concatenate([cache, frames], axis=0)

    values = frames.astype(jnp.float32).reshape(
        nframes, row_count, col_count, local_groups, group_size
    )
    local_mean = jnp.sum(values, axis=(0, 1, 2, 4)) / local_members
    local_dev = values - local_mean[:, None]
    local_m2 = jnp.sum(local_dev * local_dev, axis=(0, 1, 2, 4))
    tile = jnp.zeros((8, 128), jnp.float32)
    tile = tile.at[0, :local_groups].set(local_mean).at[1, :local_groups].set(local_m2)
    gathered, before, after = gather_space(tile, raw[:, :, 0], raw[:, :, col_count - 1])
    before = before[:, :, None]
    after = after[:, :, None]
    means = gathered[:, 0, :local_groups]
    m2s = gathered[:, 1, :local_groups]
    group_mean = jnp.mean(means, axis=0)
    spread = jnp.sum(m2s, axis=0) + local_members * jnp.sum(
        (means - group_mean) ** 2, axis=0
    )
    group_var = spread / (local_members * nspace)
    inv = lax.rsqrt(group_var + epsilon)

    def activate(x):
        shape = x.shape
        v = x.astype(jnp.float32).reshape(shape[:-1] + (local_groups, group_size))
        scaled = (v - group_mean[:, None]) * inv[:, None]
        normed = scaled.reshape(shape) * gamma + beta
        return jax.nn.silu(normed).astype(jnp.bfloat16)

    active = activate(frames)
    joined = jnp.concatenate([cache, active], axis=0)
    left = jnp.concatenate([before[:ncache], activate(before[ncache:])], axis=0)
    right = jnp.concatenate([after[:ncache], activate(after[ncache:])], axis=0)
    left = jnp.where(me == 0, jnp.zeros_like(left), left)
    right = jnp.where(me == nspace - 1, jnp.zeros_like(right), right)
    bordered = jnp.concatenate([left, joined, right], axis=2)
    bordered = jnp.pad(bordered, ((0, 0), (1, 1), (0, 0), (0, 0)))
    cell_count = nframes * row_count * col_count
    bordered = bordered.transpose(0, 2, 1, 3)
    columns_in = jnp.concatenate(
        [
            bordered[:, col_tap : col_tap + col_count, row_tap : row_tap + row_count, :]
            for row_tap in range(3)
            for col_tap in range(3)
        ],
        axis=3,
    )
    columns_in = with_layout_constraint(columns_in, Layout(major_to_minor=(0, 1, 2, 3)))
    tap_width = columns_in.shape[3]
    nchan = lax.axis_size("chan")
    nx = nchan // 4
    flat_kernel = kernel.reshape(3, tap_width, kernel.shape[4])
    running = jnp.zeros((bias.shape[0] * nchan, cell_count), jnp.float32)
    plane = row_count * col_count
    flat_in = columns_in.reshape(columns_in.shape[0] * plane, tap_width)
    for depth in range(3):
        tap_weight = flat_kernel[depth]
        window = flat_in[depth * plane : depth * plane + cell_count]
        running = running + lax.dot_general(
            tap_weight, window, (((0,), (1,)), ((), ())), preferred_element_type=jnp.float32
        )
    summed = scatter_chan(running.reshape(nx, 2, 2, local_ch, cell_count))
    result = summed.T + bias
    result = result.astype(jnp.bfloat16).reshape(nframes, col_count, row_count, -1)
    return result.transpose(0, 2, 1, 3)


def solution(mesh):
    placed = (
        P(None, None, "space", "chan"),
        P(None, None, "space", "chan"),
        P("chan"),
        P("chan"),
        P(None, None, None, "chan", None),
        P("chan"),
    )
    return jax.shard_map(
        local, mesh=mesh, in_specs=placed, out_specs=P(None, None, "space", "chan"), check_vma=False
    )
```

```python
import functools

import jax
import jax.numpy as jnp
from jax import lax
from jax.experimental import pallas as pl
from jax.experimental.pallas import tpu as pltpu
from jax.experimental.layout import Layout, with_layout_constraint
from jax.sharding import PartitionSpec as P

CH = 512
GROUPS = 32
MESH = pl.DeviceIdType.MESH

epsilon = 1e-06


def gather_kernel(n, x_ref, lo_ref, hi_ref, o_ref, left_ref, right_ref,
                  buf, left_buf, right_buf, send_sem, recv_sem, edge_send, edge_recv):
    me = lax.axis_index("space")
    ch = lax.axis_index("chan")
    right = lax.rem(me + 1, n)
    left = lax.rem(me + n - 1, n)
    barrier = pltpu.get_barrier_semaphore()

    def signal(k, carry):
        peer = lax.rem(me + k, n)
        pl.semaphore_signal(barrier, 1, device_id=(peer, ch), device_id_type=MESH)
        return carry

    lax.fori_loop(1, n, signal, 0)
    pl.semaphore_wait(barrier, n - 1)

    to_right = pltpu.make_async_remote_copy(
        src_ref=hi_ref, dst_ref=left_buf, send_sem=edge_send.at[0], recv_sem=edge_recv.at[0],
        device_id=(right, ch), device_id_type=MESH)
    to_left = pltpu.make_async_remote_copy(
        src_ref=lo_ref, dst_ref=right_buf, send_sem=edge_send.at[1], recv_sem=edge_recv.at[1],
        device_id=(left, ch), device_id_type=MESH)
    to_right.start()
    to_left.start()

    def copy_to(peer):
        return pltpu.make_async_remote_copy(
            src_ref=x_ref,
            dst_ref=buf.at[me],
            send_sem=send_sem.at[peer],
            recv_sem=recv_sem.at[me],
            device_id=(peer, ch),
            device_id_type=MESH,
        )

    def copy_from(peer):
        return pltpu.make_async_remote_copy(
            src_ref=x_ref,
            dst_ref=buf.at[peer],
            send_sem=send_sem.at[peer],
            recv_sem=recv_sem.at[peer],
            device_id=(peer, ch),
            device_id_type=MESH,
        )

    def start(k, carry):
        copy_to(lax.rem(me + k, n)).start()
        return carry

    lax.fori_loop(1, n, start, 0)

    def finish(k, carry):
        peer = lax.rem(me + k, n)
        copy_to(peer).wait_send()
        copy_from(peer).wait_recv()
        return carry

    lax.fori_loop(1, n, finish, 0)
    buf[me] = x_ref[...]
    o_ref[...] = buf[...]
    to_right.wait()
    to_left.wait()
    left_ref[...] = left_buf[...]
    right_ref[...] = right_buf[...]


def gather_space(tile, lo, hi):
    n = lax.axis_size("space")
    vmem = pl.BlockSpec(memory_space=pltpu.VMEM)
    return pl.pallas_call(
        functools.partial(gather_kernel, n),
        out_shape=(
            jax.ShapeDtypeStruct((n,) + tile.shape, tile.dtype),
            jax.ShapeDtypeStruct(hi.shape, hi.dtype),
            jax.ShapeDtypeStruct(lo.shape, lo.dtype),
        ),
        in_specs=[vmem, vmem, vmem],
        out_specs=(vmem, vmem, vmem),
        scratch_shapes=[
            pltpu.VMEM((n,) + tile.shape, tile.dtype),
            pltpu.VMEM(hi.shape, hi.dtype),
            pltpu.VMEM(lo.shape, lo.dtype),
            pltpu.SemaphoreType.DMA((n,)),
            pltpu.SemaphoreType.DMA((n,)),
            pltpu.SemaphoreType.DMA((2,)),
            pltpu.SemaphoreType.DMA((2,)),
        ],
        compiler_params=pltpu.CompilerParams(collective_id=0, has_side_effects=True),
    )(tile, lo, hi)


def scatter_kernel(nchunk, x_ref, o_ref, recv1, acc1, own, recv2, acc2, recv3,
                   sem1s, sem1r, sem2s, sem2r, sem3s, sem3r):
    sp = lax.axis_index("space")
    c = lax.axis_index("chan")
    core = c % 2
    yh = (c // 2) % 2
    xx = c // 4
    nx, nyh = x_ref.shape[0], x_ref.shape[1]
    width = x_ref.shape[-1] // nchunk
    f32, bf16 = jnp.float32, jnp.bfloat16

    def dev(x_, yh_, core_):
        return (sp, x_ * 4 + yh_ * 2 + core_)

    peers = [dev(xx, yh, 1 - core)]
    peers += [dev(lax.rem(xx + k, nx), yh, core) for k in range(1, nx)]
    peers += [dev(xx, 1 - yh, core)]
    barrier = pltpu.get_barrier_semaphore()
    for p in peers:
        pl.semaphore_signal(barrier, 1, device_id=p, device_id_type=MESH)
    pl.semaphore_wait(barrier, len(peers))

    def cols(q):
        return pl.ds(q * width, width)

    firsts = []
    for q in range(nchunk):
        for i in range(nx):
            for j in range(nyh):
                n = (q * nx + i) * nyh + j
                cp = pltpu.make_async_remote_copy(
                    src_ref=x_ref.at[i, j, 1 - core, :, cols(q)], dst_ref=recv1.at[q, i, j],
                    send_sem=sem1s.at[n], recv_sem=sem1r.at[n],
                    device_id=peers[0], device_id_type=MESH)
                cp.start()
                firsts.append(cp)

    def second(q):
        for cp in firsts[q * nx * nyh : (q + 1) * nx * nyh]:
            cp.wait()
        sends = []
        for k in range(1, nx):
            dest = lax.rem(xx + k, nx)
            for j in range(nyh):
                acc1[q, dest, j] = (x_ref[dest, j, core, :, cols(q)] + recv1[q, dest, j]).astype(bf16)
            slot = nx - 1 - k
            cp = pltpu.make_async_remote_copy(
                src_ref=acc1.at[q, dest], dst_ref=recv2.at[q, slot],
                send_sem=sem2s.at[q * (nx - 1) + k - 1], recv_sem=sem2r.at[q * (nx - 1) + slot],
                device_id=peers[k], device_id_type=MESH)
            cp.start()
            sends.append(cp)
        for j in range(nyh):
            own[q, j] = x_ref[xx, j, core, :, cols(q)] + recv1[q, xx, j]
        return sends

    def third(q):
        for slot in range(nx - 1):
            pltpu.make_async_remote_copy(
                src_ref=acc1.at[q, xx], dst_ref=recv2.at[q, slot],
                send_sem=sem2s.at[q * (nx - 1) + slot], recv_sem=sem2r.at[q * (nx - 1) + slot],
                device_id=peers[0], device_id_type=MESH).wait_recv()
        other = 1 - yh
        total = own[q, other]
        for slot in range(nx - 1):
            total = total + recv2[q, slot, other].astype(f32)
        acc2[q] = total.astype(bf16)
        cp = pltpu.make_async_remote_copy(
            src_ref=acc2.at[q], dst_ref=recv3.at[q], send_sem=sem3s.at[q],
            recv_sem=sem3r.at[q], device_id=peers[nx], device_id_type=MESH)
        cp.start()
        total = own[q, yh]
        for slot in range(nx - 1):
            total = total + recv2[q, slot, yh].astype(f32)
        own[q, yh] = total
        return cp

    seconds, lasts = [], []
    for q in range(nchunk):
        seconds.append(second(q))
        if q >= 1:
            lasts.append(third(q - 1))
    lasts.append(third(nchunk - 1))
    for sends in seconds:
        for cp in sends:
            cp.wait_send()
    for q, cp in enumerate(lasts):
        cp.wait()
        o_ref[:, cols(q)] = own[q, yh] + recv3[q].astype(f32)


def scatter_chan(parts, nchunk=3):
    nx, nyh, ncore, rows, cells = parts.shape
    width = cells // nchunk
    f32, bf16 = jnp.float32, jnp.bfloat16
    return pl.pallas_call(
        functools.partial(scatter_kernel, nchunk),
        out_shape=jax.ShapeDtypeStruct((rows, cells), f32),
        in_specs=[pl.BlockSpec(memory_space=pltpu.VMEM)],
        out_specs=pl.BlockSpec(memory_space=pltpu.VMEM),
        scratch_shapes=[
            pltpu.VMEM((nchunk, nx, nyh, rows, width), f32),
            pltpu.VMEM((nchunk, nx, nyh, rows, width), bf16),
            pltpu.VMEM((nchunk, nyh, rows, width), f32),
            pltpu.VMEM((nchunk, nx - 1, nyh, rows, width), bf16),
            pltpu.VMEM((nchunk, rows, width), bf16),
            pltpu.VMEM((nchunk, rows, width), bf16),
            pltpu.SemaphoreType.DMA((nchunk * nx * nyh,)),
            pltpu.SemaphoreType.DMA((nchunk * nx * nyh,)),
            pltpu.SemaphoreType.DMA((nchunk * (nx - 1),)),
            pltpu.SemaphoreType.DMA((nchunk * (nx - 1),)),
            pltpu.SemaphoreType.DMA((nchunk,)),
            pltpu.SemaphoreType.DMA((nchunk,)),
        ],
        compiler_params=pltpu.CompilerParams(
            collective_id=1, has_side_effects=True, vmem_limit_bytes=48 * 1024 * 1024),
    )(parts)


def local(frames, cache, gamma, beta, kernel, bias):
    nframes, row_count, col_count, local_ch = frames.shape
    ncache = cache.shape[0]
    group_size = CH // GROUPS
    local_groups = local_ch // group_size
    nspace = lax.axis_size("space")
    me = lax.axis_index("space")
    local_members = float(nframes * row_count * col_count * group_size)

    raw = jnp.concatenate([cache, frames], axis=0)

    values = frames.astype(jnp.float32).reshape(
        nframes, row_count, col_count, local_groups, group_size
    )
    local_mean = jnp.sum(values, axis=(0, 1, 2, 4)) / local_members
    local_dev = values - local_mean[:, None]
    local_m2 = jnp.sum(local_dev * local_dev, axis=(0, 1, 2, 4))
    tile = jnp.zeros((8, 128), jnp.float32)
    tile = tile.at[0, :local_groups].set(local_mean).at[1, :local_groups].set(local_m2)
    gathered, before, after = gather_space(tile, raw[:, :, 0], raw[:, :, col_count - 1])
    before = before[:, :, None]
    after = after[:, :, None]
    means = gathered[:, 0, :local_groups]
    m2s = gathered[:, 1, :local_groups]
    group_mean = jnp.mean(means, axis=0)
    spread = jnp.sum(m2s, axis=0) + local_members * jnp.sum(
        (means - group_mean) ** 2, axis=0
    )
    group_var = spread / (local_members * nspace)
    inv = lax.rsqrt(group_var + epsilon)

    def activate(x):
        shape = x.shape
        v = x.astype(jnp.float32).reshape(shape[:-1] + (local_groups, group_size))
        scaled = (v - group_mean[:, None]) * inv[:, None]
        normed = scaled.reshape(shape) * gamma + beta
        return jax.nn.silu(normed).astype(jnp.bfloat16)

    active = activate(frames)
    joined = jnp.concatenate([cache, active], axis=0)
    left = jnp.concatenate([before[:ncache], activate(before[ncache:])], axis=0)
    right = jnp.concatenate([after[:ncache], activate(after[ncache:])], axis=0)
    left = jnp.where(me == 0, jnp.zeros_like(left), left)
    right = jnp.where(me == nspace - 1, jnp.zeros_like(right), right)
    bordered = jnp.concatenate([left, joined, right], axis=2)
    bordered = jnp.pad(bordered, ((0, 0), (1, 1), (0, 0), (0, 0)))
    cell_count = nframes * row_count * col_count
    bordered = bordered.transpose(0, 2, 1, 3)
    rows_in = jnp.concatenate(
        [bordered[:, :, row_tap : row_tap + row_count, :] for row_tap in range(3)], axis=3
    )
    rows_in = with_layout_constraint(rows_in, Layout(major_to_minor=(0, 1, 2, 3)))
    tap_width = rows_in.shape[3]
    nchan = lax.axis_size("chan")
    nx = nchan // 4
    running = jnp.zeros((bias.shape[0] * nchan, cell_count), jnp.float32)
    for depth in range(3):
        for col_tap in range(3):
            tap_weight = kernel[depth, :, col_tap].reshape(tap_width, kernel.shape[4])
            window = rows_in[depth : depth + nframes, col_tap : col_tap + col_count]
            window = window.reshape(cell_count, tap_width)
            running = running + lax.dot_general(
                tap_weight, window, (((0,), (1,)), ((), ())), preferred_element_type=jnp.float32
            )
    summed = scatter_chan(running.reshape(nx, 2, 2, local_ch, cell_count))
    result = summed.T + bias
    result = result.astype(jnp.bfloat16).reshape(nframes, col_count, row_count, -1)
    return result.transpose(0, 2, 1, 3)


def solution(mesh):
    placed = (
        P(None, None, "space", "chan"),
        P(None, None, "space", "chan"),
        P("chan"),
        P("chan"),
        P(None, None, None, "chan", None),
        P("chan"),
    )
    return jax.shard_map(
        local, mesh=mesh, in_specs=placed, out_specs=P(None, None, "space", "chan"), check_vma=False
    )
```

```python
import functools

import jax
import jax.numpy as jnp
from jax import lax
from jax.experimental import pallas as pl
from jax.experimental.pallas import tpu as pltpu
from jax.experimental.layout import Layout, with_layout_constraint
from jax.sharding import PartitionSpec as P

CH = 512
GROUPS = 32
MESH = pl.DeviceIdType.MESH

epsilon = 1e-06


def gather_kernel(n, x_ref, lo_ref, hi_ref, o_ref, left_ref, right_ref,
                  buf, left_buf, right_buf, send_sem, recv_sem, edge_send, edge_recv):
    me = lax.axis_index("space")
    ch = lax.axis_index("chan")
    right = lax.rem(me + 1, n)
    left = lax.rem(me + n - 1, n)
    barrier = pltpu.get_barrier_semaphore()

    def signal(k, carry):
        peer = lax.rem(me + k, n)
        pl.semaphore_signal(barrier, 1, device_id=(peer, ch), device_id_type=MESH)
        return carry

    lax.fori_loop(1, n, signal, 0)
    pl.semaphore_wait(barrier, n - 1)

    to_right = pltpu.make_async_remote_copy(
        src_ref=hi_ref, dst_ref=left_buf, send_sem=edge_send.at[0], recv_sem=edge_recv.at[0],
        device_id=(right, ch), device_id_type=MESH)
    to_left = pltpu.make_async_remote_copy(
        src_ref=lo_ref, dst_ref=right_buf, send_sem=edge_send.at[1], recv_sem=edge_recv.at[1],
        device_id=(left, ch), device_id_type=MESH)
    to_right.start()
    to_left.start()

    def copy_to(peer):
        return pltpu.make_async_remote_copy(
            src_ref=x_ref,
            dst_ref=buf.at[me],
            send_sem=send_sem.at[peer],
            recv_sem=recv_sem.at[me],
            device_id=(peer, ch),
            device_id_type=MESH,
        )

    def copy_from(peer):
        return pltpu.make_async_remote_copy(
            src_ref=x_ref,
            dst_ref=buf.at[peer],
            send_sem=send_sem.at[peer],
            recv_sem=recv_sem.at[peer],
            device_id=(peer, ch),
            device_id_type=MESH,
        )

    def start(k, carry):
        copy_to(lax.rem(me + k, n)).start()
        return carry

    lax.fori_loop(1, n, start, 0)

    def finish(k, carry):
        peer = lax.rem(me + k, n)
        copy_to(peer).wait_send()
        copy_from(peer).wait_recv()
        return carry

    lax.fori_loop(1, n, finish, 0)
    buf[me] = x_ref[...]
    o_ref[...] = buf[...]
    to_right.wait()
    to_left.wait()
    left_ref[...] = left_buf[...]
    right_ref[...] = right_buf[...]


def gather_space(tile, lo, hi):
    n = lax.axis_size("space")
    vmem = pl.BlockSpec(memory_space=pltpu.VMEM)
    return pl.pallas_call(
        functools.partial(gather_kernel, n),
        out_shape=(
            jax.ShapeDtypeStruct((n,) + tile.shape, tile.dtype),
            jax.ShapeDtypeStruct(hi.shape, hi.dtype),
            jax.ShapeDtypeStruct(lo.shape, lo.dtype),
        ),
        in_specs=[vmem, vmem, vmem],
        out_specs=(vmem, vmem, vmem),
        scratch_shapes=[
            pltpu.VMEM((n,) + tile.shape, tile.dtype),
            pltpu.VMEM(hi.shape, hi.dtype),
            pltpu.VMEM(lo.shape, lo.dtype),
            pltpu.SemaphoreType.DMA((n,)),
            pltpu.SemaphoreType.DMA((n,)),
            pltpu.SemaphoreType.DMA((2,)),
            pltpu.SemaphoreType.DMA((2,)),
        ],
        compiler_params=pltpu.CompilerParams(collective_id=0, has_side_effects=True),
    )(tile, lo, hi)


def scatter_kernel(nchunk, x_ref, o_ref, recv1, acc1, own, recv2, acc2, recv3,
                   sem1s, sem1r, sem2s, sem2r, sem3s, sem3r):
    sp = lax.axis_index("space")
    c = lax.axis_index("chan")
    core = c % 2
    yh = (c // 2) % 2
    xx = c // 4
    nx, nyh = x_ref.shape[0], x_ref.shape[1]
    width = x_ref.shape[-1] // nchunk
    f32, bf16 = jnp.float32, jnp.bfloat16

    def dev(x_, yh_, core_):
        return (sp, x_ * 4 + yh_ * 2 + core_)

    peers = [dev(xx, yh, 1 - core)]
    peers += [dev(lax.rem(xx + k, nx), yh, core) for k in range(1, nx)]
    peers += [dev(xx, 1 - yh, core)]
    barrier = pltpu.get_barrier_semaphore()
    for p in peers:
        pl.semaphore_signal(barrier, 1, device_id=p, device_id_type=MESH)
    pl.semaphore_wait(barrier, len(peers))

    def cols(q):
        return pl.ds(q * width, width)

    firsts = []
    for q in range(nchunk):
        for i in range(nx):
            for j in range(nyh):
                n = (q * nx + i) * nyh + j
                cp = pltpu.make_async_remote_copy(
                    src_ref=x_ref.at[i, j, 1 - core, :, cols(q)], dst_ref=recv1.at[q, i, j],
                    send_sem=sem1s.at[n], recv_sem=sem1r.at[n],
                    device_id=peers[0], device_id_type=MESH)
                cp.start()
                firsts.append(cp)

    def second(q):
        for cp in firsts[q * nx * nyh : (q + 1) * nx * nyh]:
            cp.wait()
        sends = []
        for k in range(1, nx):
            dest = lax.rem(xx + k, nx)
            for j in range(nyh):
                acc1[q, dest, j] = (x_ref[dest, j, core, :, cols(q)] + recv1[q, dest, j]).astype(bf16)
            slot = nx - 1 - k
            cp = pltpu.make_async_remote_copy(
                src_ref=acc1.at[q, dest], dst_ref=recv2.at[q, slot],
                send_sem=sem2s.at[q * (nx - 1) + k - 1], recv_sem=sem2r.at[q * (nx - 1) + slot],
                device_id=peers[k], device_id_type=MESH)
            cp.start()
            sends.append(cp)
        for j in range(nyh):
            own[q, j] = x_ref[xx, j, core, :, cols(q)] + recv1[q, xx, j]
        return sends

    def third(q):
        for slot in range(nx - 1):
            pltpu.make_async_remote_copy(
                src_ref=acc1.at[q, xx], dst_ref=recv2.at[q, slot],
                send_sem=sem2s.at[q * (nx - 1) + slot], recv_sem=sem2r.at[q * (nx - 1) + slot],
                device_id=peers[0], device_id_type=MESH).wait_recv()
        other = 1 - yh
        total = own[q, other]
        for slot in range(nx - 1):
            total = total + recv2[q, slot, other].astype(f32)
        acc2[q] = total.astype(bf16)
        cp = pltpu.make_async_remote_copy(
            src_ref=acc2.at[q], dst_ref=recv3.at[q], send_sem=sem3s.at[q],
            recv_sem=sem3r.at[q], device_id=peers[nx], device_id_type=MESH)
        cp.start()
        total = own[q, yh]
        for slot in range(nx - 1):
            total = total + recv2[q, slot, yh].astype(f32)
        own[q, yh] = total
        return cp

    seconds, lasts = [], []
    for q in range(nchunk):
        seconds.append(second(q))
        if q >= 1:
            lasts.append(third(q - 1))
    lasts.append(third(nchunk - 1))
    for sends in seconds:
        for cp in sends:
            cp.wait_send()
    for q, cp in enumerate(lasts):
        cp.wait()
        o_ref[:, cols(q)] = own[q, yh] + recv3[q].astype(f32)


def scatter_chan(parts, nchunk=3):
    nx, nyh, ncore, rows, cells = parts.shape
    width = cells // nchunk
    f32, bf16 = jnp.float32, jnp.bfloat16
    return pl.pallas_call(
        functools.partial(scatter_kernel, nchunk),
        out_shape=jax.ShapeDtypeStruct((rows, cells), f32),
        in_specs=[pl.BlockSpec(memory_space=pltpu.VMEM)],
        out_specs=pl.BlockSpec(memory_space=pltpu.VMEM),
        scratch_shapes=[
            pltpu.VMEM((nchunk, nx, nyh, rows, width), f32),
            pltpu.VMEM((nchunk, nx, nyh, rows, width), bf16),
            pltpu.VMEM((nchunk, nyh, rows, width), f32),
            pltpu.VMEM((nchunk, nx - 1, nyh, rows, width), bf16),
            pltpu.VMEM((nchunk, rows, width), bf16),
            pltpu.VMEM((nchunk, rows, width), bf16),
            pltpu.SemaphoreType.DMA((nchunk * nx * nyh,)),
            pltpu.SemaphoreType.DMA((nchunk * nx * nyh,)),
            pltpu.SemaphoreType.DMA((nchunk * (nx - 1),)),
            pltpu.SemaphoreType.DMA((nchunk * (nx - 1),)),
            pltpu.SemaphoreType.DMA((nchunk,)),
            pltpu.SemaphoreType.DMA((nchunk,)),
        ],
        compiler_params=pltpu.CompilerParams(
            collective_id=1, has_side_effects=True, vmem_limit_bytes=48 * 1024 * 1024),
    )(parts)


def local(frames, cache, gamma, beta, kernel, bias):
    nframes, row_count, col_count, local_ch = frames.shape
    ncache = cache.shape[0]
    group_size = CH // GROUPS
    local_groups = local_ch // group_size
    nspace = lax.axis_size("space")
    me = lax.axis_index("space")
    local_members = float(nframes * row_count * col_count * group_size)

    raw = jnp.concatenate([cache, frames], axis=0)

    values = frames.astype(jnp.float32).reshape(
        nframes, row_count, col_count, local_groups, group_size
    )
    local_mean = jnp.sum(values, axis=(0, 1, 2, 4)) / local_members
    local_dev = values - local_mean[:, None]
    local_m2 = jnp.sum(local_dev * local_dev, axis=(0, 1, 2, 4))
    tile = jnp.zeros((8, 128), jnp.float32)
    tile = tile.at[0, :local_groups].set(local_mean).at[1, :local_groups].set(local_m2)
    gathered, before, after = gather_space(tile, raw[:, :, 0], raw[:, :, col_count - 1])
    before = before[:, :, None]
    after = after[:, :, None]
    means = gathered[:, 0, :local_groups]
    m2s = gathered[:, 1, :local_groups]
    group_mean = jnp.mean(means, axis=0)
    spread = jnp.sum(m2s, axis=0) + local_members * jnp.sum(
        (means - group_mean) ** 2, axis=0
    )
    group_var = spread / (local_members * nspace)
    inv = lax.rsqrt(group_var + epsilon)

    def activate(x):
        shape = x.shape
        v = x.astype(jnp.float32).reshape(shape[:-1] + (local_groups, group_size))
        scaled = (v - group_mean[:, None]) * inv[:, None]
        normed = scaled.reshape(shape) * gamma + beta
        return jax.nn.silu(normed).astype(jnp.bfloat16)

    active = activate(frames)
    joined = jnp.concatenate([cache, active], axis=0)
    left = jnp.concatenate([before[:ncache], activate(before[ncache:])], axis=0)
    right = jnp.concatenate([after[:ncache], activate(after[ncache:])], axis=0)
    left = jnp.where(me == 0, jnp.zeros_like(left), left)
    right = jnp.where(me == nspace - 1, jnp.zeros_like(right), right)
    bordered = jnp.concatenate([left, joined, right], axis=2)
    bordered = jnp.pad(bordered, ((0, 0), (1, 1), (0, 0), (0, 0)))
    cell_count = nframes * row_count * col_count
    bordered = bordered.transpose(0, 2, 1, 3)
    rows_in = jnp.concatenate(
        [bordered[:, :, row_tap : row_tap + row_count, :] for row_tap in range(3)], axis=3
    )
    rows_in = with_layout_constraint(rows_in, Layout(major_to_minor=(0, 1, 2, 3)))
    columns_in = jnp.concatenate(
        [rows_in[:, col_tap : col_tap + col_count] for col_tap in range(3)], axis=3
    )
    columns_in = with_layout_constraint(columns_in, Layout(major_to_minor=(0, 1, 2, 3)))
    tap_width = columns_in.shape[3]
    nchan = lax.axis_size("chan")
    nx = nchan // 4
    flat_kernel = kernel.transpose(0, 2, 1, 3, 4).reshape(3, tap_width, kernel.shape[4])
    running = jnp.zeros((bias.shape[0] * nchan, cell_count), jnp.float32)
    plane = row_count * col_count
    flat_in = columns_in.reshape(columns_in.shape[0] * plane, tap_width)
    for depth in range(3):
        tap_weight = flat_kernel[depth]
        window = flat_in[depth * plane : depth * plane + cell_count]
        running = running + lax.dot_general(
            tap_weight, window, (((0,), (1,)), ((), ())), preferred_element_type=jnp.float32
        )
    summed = scatter_chan(running.reshape(nx, 2, 2, local_ch, cell_count))
    result = summed.T + bias
    result = result.astype(jnp.bfloat16).reshape(nframes, col_count, row_count, -1)
    return result.transpose(0, 2, 1, 3)


def solution(mesh):
    placed = (
        P(None, None, "space", "chan"),
        P(None, None, "space", "chan"),
        P("chan"),
        P("chan"),
        P(None, None, None, "chan", None),
        P("chan"),
    )
    return jax.shard_map(
        local, mesh=mesh, in_specs=placed, out_specs=P(None, None, "space", "chan"), check_vma=False
    )
```

```python
import functools

import jax
import jax.numpy as jnp
from jax import lax
from jax.experimental import pallas as pl
from jax.experimental.pallas import tpu as pltpu
from jax.experimental.layout import Layout, with_layout_constraint
from jax.sharding import PartitionSpec as P

CH = 512
GROUPS = 32
MESH = pl.DeviceIdType.MESH

epsilon = 1e-06


def gather_kernel(n, x_ref, lo_ref, hi_ref, o_ref, left_ref, right_ref,
                  buf, left_buf, right_buf, send_sem, recv_sem, edge_send, edge_recv):
    me = lax.axis_index("space")
    ch = lax.axis_index("chan")
    right = lax.rem(me + 1, n)
    left = lax.rem(me + n - 1, n)
    barrier = pltpu.get_barrier_semaphore()

    def signal(k, carry):
        peer = lax.rem(me + k, n)
        pl.semaphore_signal(barrier, 1, device_id=(peer, ch), device_id_type=MESH)
        return carry

    lax.fori_loop(1, n, signal, 0)
    pl.semaphore_wait(barrier, n - 1)

    to_right = pltpu.make_async_remote_copy(
        src_ref=hi_ref, dst_ref=left_buf, send_sem=edge_send.at[0], recv_sem=edge_recv.at[0],
        device_id=(right, ch), device_id_type=MESH)
    to_left = pltpu.make_async_remote_copy(
        src_ref=lo_ref, dst_ref=right_buf, send_sem=edge_send.at[1], recv_sem=edge_recv.at[1],
        device_id=(left, ch), device_id_type=MESH)
    to_right.start()
    to_left.start()

    def copy_to(peer):
        return pltpu.make_async_remote_copy(
            src_ref=x_ref,
            dst_ref=buf.at[me],
            send_sem=send_sem.at[peer],
            recv_sem=recv_sem.at[me],
            device_id=(peer, ch),
            device_id_type=MESH,
        )

    def copy_from(peer):
        return pltpu.make_async_remote_copy(
            src_ref=x_ref,
            dst_ref=buf.at[peer],
            send_sem=send_sem.at[peer],
            recv_sem=recv_sem.at[peer],
            device_id=(peer, ch),
            device_id_type=MESH,
        )

    def start(k, carry):
        copy_to(lax.rem(me + k, n)).start()
        return carry

    lax.fori_loop(1, n, start, 0)

    def finish(k, carry):
        peer = lax.rem(me + k, n)
        copy_to(peer).wait_send()
        copy_from(peer).wait_recv()
        return carry

    lax.fori_loop(1, n, finish, 0)
    buf[me] = x_ref[...]
    o_ref[...] = buf[...]
    to_right.wait()
    to_left.wait()
    left_ref[...] = left_buf[...]
    right_ref[...] = right_buf[...]


def gather_space(tile, lo, hi):
    n = lax.axis_size("space")
    vmem = pl.BlockSpec(memory_space=pltpu.VMEM)
    return pl.pallas_call(
        functools.partial(gather_kernel, n),
        out_shape=(
            jax.ShapeDtypeStruct((n,) + tile.shape, tile.dtype),
            jax.ShapeDtypeStruct(hi.shape, hi.dtype),
            jax.ShapeDtypeStruct(lo.shape, lo.dtype),
        ),
        in_specs=[vmem, vmem, vmem],
        out_specs=(vmem, vmem, vmem),
        scratch_shapes=[
            pltpu.VMEM((n,) + tile.shape, tile.dtype),
            pltpu.VMEM(hi.shape, hi.dtype),
            pltpu.VMEM(lo.shape, lo.dtype),
            pltpu.SemaphoreType.DMA((n,)),
            pltpu.SemaphoreType.DMA((n,)),
            pltpu.SemaphoreType.DMA((2,)),
            pltpu.SemaphoreType.DMA((2,)),
        ],
        compiler_params=pltpu.CompilerParams(collective_id=0, has_side_effects=True),
    )(tile, lo, hi)


def scatter_kernel(nchunk, x_ref, o_ref, recv1, acc1, own, recv2, acc2, recv3,
                   sem1s, sem1r, sem2s, sem2r, sem3s, sem3r):
    sp = lax.axis_index("space")
    c = lax.axis_index("chan")
    core = c % 2
    yh = (c // 2) % 2
    xx = c // 4
    nx, nyh = x_ref.shape[0], x_ref.shape[1]
    width = x_ref.shape[-1] // nchunk
    f32, bf16 = jnp.float32, jnp.bfloat16

    def dev(x_, yh_, core_):
        return (sp, x_ * 4 + yh_ * 2 + core_)

    peers = [dev(xx, yh, 1 - core)]
    peers += [dev(lax.rem(xx + k, nx), yh, core) for k in range(1, nx)]
    peers += [dev(xx, 1 - yh, core)]
    barrier = pltpu.get_barrier_semaphore()
    for p in peers:
        pl.semaphore_signal(barrier, 1, device_id=p, device_id_type=MESH)
    pl.semaphore_wait(barrier, len(peers))

    def cols(q):
        return pl.ds(q * width, width)

    firsts = []
    for q in range(nchunk):
        for i in range(nx):
            for j in range(nyh):
                n = (q * nx + i) * nyh + j
                cp = pltpu.make_async_remote_copy(
                    src_ref=x_ref.at[i, j, 1 - core, :, cols(q)], dst_ref=recv1.at[q, i, j],
                    send_sem=sem1s.at[n], recv_sem=sem1r.at[n],
                    device_id=peers[0], device_id_type=MESH)
                cp.start()
                firsts.append(cp)

    def second(q):
        for cp in firsts[q * nx * nyh : (q + 1) * nx * nyh]:
            cp.wait()
        sends = []
        for k in range(1, nx):
            dest = lax.rem(xx + k, nx)
            for j in range(nyh):
                acc1[q, dest, j] = (x_ref[dest, j, core, :, cols(q)] + recv1[q, dest, j]).astype(bf16)
            slot = nx - 1 - k
            cp = pltpu.make_async_remote_copy(
                src_ref=acc1.at[q, dest], dst_ref=recv2.at[q, slot],
                send_sem=sem2s.at[q * (nx - 1) + k - 1], recv_sem=sem2r.at[q * (nx - 1) + slot],
                device_id=peers[k], device_id_type=MESH)
            cp.start()
            sends.append(cp)
        for j in range(nyh):
            own[q, j] = x_ref[xx, j, core, :, cols(q)] + recv1[q, xx, j]
        return sends

    def third(q):
        for slot in range(nx - 1):
            pltpu.make_async_remote_copy(
                src_ref=acc1.at[q, xx], dst_ref=recv2.at[q, slot],
                send_sem=sem2s.at[q * (nx - 1) + slot], recv_sem=sem2r.at[q * (nx - 1) + slot],
                device_id=peers[0], device_id_type=MESH).wait_recv()
        other = 1 - yh
        total = own[q, other]
        for slot in range(nx - 1):
            total = total + recv2[q, slot, other].astype(f32)
        acc2[q] = total.astype(bf16)
        cp = pltpu.make_async_remote_copy(
            src_ref=acc2.at[q], dst_ref=recv3.at[q], send_sem=sem3s.at[q],
            recv_sem=sem3r.at[q], device_id=peers[nx], device_id_type=MESH)
        cp.start()
        total = own[q, yh]
        for slot in range(nx - 1):
            total = total + recv2[q, slot, yh].astype(f32)
        own[q, yh] = total
        return cp

    seconds, lasts = [], []
    for q in range(nchunk):
        seconds.append(second(q))
        if q >= 1:
            lasts.append(third(q - 1))
    lasts.append(third(nchunk - 1))
    for sends in seconds:
        for cp in sends:
            cp.wait_send()
    for q, cp in enumerate(lasts):
        cp.wait()
        o_ref[:, cols(q)] = own[q, yh] + recv3[q].astype(f32)


def scatter_chan(parts, nchunk=3):
    nx, nyh, ncore, rows, cells = parts.shape
    width = cells // nchunk
    f32, bf16 = jnp.float32, jnp.bfloat16
    return pl.pallas_call(
        functools.partial(scatter_kernel, nchunk),
        out_shape=jax.ShapeDtypeStruct((rows, cells), f32),
        in_specs=[pl.BlockSpec(memory_space=pltpu.VMEM)],
        out_specs=pl.BlockSpec(memory_space=pltpu.VMEM),
        scratch_shapes=[
            pltpu.VMEM((nchunk, nx, nyh, rows, width), f32),
            pltpu.VMEM((nchunk, nx, nyh, rows, width), bf16),
            pltpu.VMEM((nchunk, nyh, rows, width), f32),
            pltpu.VMEM((nchunk, nx - 1, nyh, rows, width), bf16),
            pltpu.VMEM((nchunk, rows, width), bf16),
            pltpu.VMEM((nchunk, rows, width), bf16),
            pltpu.SemaphoreType.DMA((nchunk * nx * nyh,)),
            pltpu.SemaphoreType.DMA((nchunk * nx * nyh,)),
            pltpu.SemaphoreType.DMA((nchunk * (nx - 1),)),
            pltpu.SemaphoreType.DMA((nchunk * (nx - 1),)),
            pltpu.SemaphoreType.DMA((nchunk,)),
            pltpu.SemaphoreType.DMA((nchunk,)),
        ],
        compiler_params=pltpu.CompilerParams(
            collective_id=1, has_side_effects=True, vmem_limit_bytes=48 * 1024 * 1024),
    )(parts)


def local(frames, cache, gamma, beta, kernel, bias):
    nframes, row_count, col_count, local_ch = frames.shape
    ncache = cache.shape[0]
    group_size = CH // GROUPS
    local_groups = local_ch // group_size
    nspace = lax.axis_size("space")
    me = lax.axis_index("space")
    local_members = float(nframes * row_count * col_count * group_size)


    def edge(col):
        return jnp.concatenate([cache[:, :, col], frames[:, :, col]], axis=0).transpose(0, 2, 1)

    values = frames.astype(jnp.float32).reshape(
        nframes, row_count, col_count, local_groups, group_size
    )
    local_mean = jnp.sum(values, axis=(0, 1, 2, 4)) / local_members
    local_dev = values - local_mean[:, None]
    local_m2 = jnp.sum(local_dev * local_dev, axis=(0, 1, 2, 4))
    tile = jnp.zeros((8, 128), jnp.float32)
    tile = tile.at[0, :local_groups].set(local_mean).at[1, :local_groups].set(local_m2)
    gathered, before, after = gather_space(tile, edge(0), edge(col_count - 1))
    before = before.transpose(0, 2, 1)[:, :, None]
    after = after.transpose(0, 2, 1)[:, :, None]
    means = gathered[:, 0, :local_groups]
    m2s = gathered[:, 1, :local_groups]
    group_mean = jnp.mean(means, axis=0)
    spread = jnp.sum(m2s, axis=0) + local_members * jnp.sum(
        (means - group_mean) ** 2, axis=0
    )
    group_var = spread / (local_members * nspace)
    inv = lax.rsqrt(group_var + epsilon)

    def activate(x):
        shape = x.shape
        v = x.astype(jnp.float32).reshape(shape[:-1] + (local_groups, group_size))
        scaled = (v - group_mean[:, None]) * inv[:, None]
        normed = scaled.reshape(shape) * gamma + beta
        return jax.nn.silu(normed).astype(jnp.bfloat16)

    active = activate(frames)
    joined = jnp.concatenate([cache, active], axis=0)
    left = jnp.concatenate([before[:ncache], activate(before[ncache:])], axis=0)
    right = jnp.concatenate([after[:ncache], activate(after[ncache:])], axis=0)
    left = jnp.where(me == 0, jnp.zeros_like(left), left)
    right = jnp.where(me == nspace - 1, jnp.zeros_like(right), right)
    bordered = jnp.concatenate([left, joined, right], axis=2)
    bordered = jnp.pad(bordered, ((0, 0), (1, 1), (0, 0), (0, 0)))
    cell_count = nframes * row_count * col_count
    bordered = bordered.transpose(0, 2, 1, 3)
    rows_in = jnp.concatenate(
        [bordered[:, :, row_tap : row_tap + row_count, :] for row_tap in range(3)], axis=3
    )
    rows_in = with_layout_constraint(rows_in, Layout(major_to_minor=(0, 1, 2, 3)))
    columns_in = jnp.concatenate(
        [rows_in[:, col_tap : col_tap + col_count] for col_tap in range(3)], axis=3
    )
    columns_in = with_layout_constraint(columns_in, Layout(major_to_minor=(0, 1, 2, 3)))
    tap_width = columns_in.shape[3]
    nchan = lax.axis_size("chan")
    nx = nchan // 4
    flat_kernel = kernel.transpose(0, 2, 1, 3, 4).reshape(3, tap_width, kernel.shape[4])
    running = jnp.zeros((bias.shape[0] * nchan, cell_count), jnp.float32)
    plane = row_count * col_count
    flat_in = columns_in.reshape(columns_in.shape[0] * plane, tap_width)
    for depth in range(3):
        tap_weight = flat_kernel[depth]
        window = flat_in[depth * plane : depth * plane + cell_count]
        running = running + lax.dot_general(
            tap_weight, window, (((0,), (1,)), ((), ())), preferred_element_type=jnp.float32
        )
    summed = scatter_chan(running.reshape(nx, 2, 2, local_ch, cell_count))
    result = summed.T + bias
    result = result.astype(jnp.bfloat16).reshape(nframes, col_count, row_count, -1)
    return result.transpose(0, 2, 1, 3)


def solution(mesh):
    placed = (
        P(None, None, "space", "chan"),
        P(None, None, "space", "chan"),
        P("chan"),
        P("chan"),
        P(None, None, None, "chan", None),
        P("chan"),
    )
    return jax.shard_map(
        local, mesh=mesh, in_specs=placed, out_specs=P(None, None, "space", "chan"), check_vma=False
    )
```

```python
import functools

import jax
import jax.numpy as jnp
from jax import lax
from jax.experimental import pallas as pl
from jax.experimental.pallas import tpu as pltpu
from jax.experimental.layout import Layout, with_layout_constraint
from jax.sharding import PartitionSpec as P

CH = 512
GROUPS = 32
MESH = pl.DeviceIdType.MESH

epsilon = 1e-06


def gather_kernel(n, x_ref, cache_ref, frames_ref, o_ref, left_ref, right_ref,
                  buf, left_buf, right_buf, send_sem, recv_sem, edge_send, edge_recv):
    me = lax.axis_index("space")
    ch = lax.axis_index("chan")
    right = lax.rem(me + 1, n)
    left = lax.rem(me + n - 1, n)
    barrier = pltpu.get_barrier_semaphore()

    def signal(k, carry):
        peer = lax.rem(me + k, n)
        pl.semaphore_signal(barrier, 1, device_id=(peer, ch), device_id_type=MESH)
        return carry

    lax.fori_loop(1, n, signal, 0)
    pl.semaphore_wait(barrier, n - 1)

    ncache = cache_ref.shape[0]
    last = cache_ref.shape[1] - 1
    edges = []
    for k, (src, lo_row) in enumerate(((cache_ref, 0), (frames_ref, ncache))):
        rows = pl.ds(lo_row, src.shape[0])
        edges.append(pltpu.make_async_remote_copy(
            src_ref=src.at[:, last], dst_ref=left_buf.at[rows], send_sem=edge_send.at[k],
            recv_sem=edge_recv.at[k], device_id=(right, ch), device_id_type=MESH))
        edges.append(pltpu.make_async_remote_copy(
            src_ref=src.at[:, 0], dst_ref=right_buf.at[rows], send_sem=edge_send.at[2 + k],
            recv_sem=edge_recv.at[2 + k], device_id=(left, ch), device_id_type=MESH))
    for cp in edges:
        cp.start()

    def copy_to(peer):
        return pltpu.make_async_remote_copy(
            src_ref=x_ref,
            dst_ref=buf.at[me],
            send_sem=send_sem.at[peer],
            recv_sem=recv_sem.at[me],
            device_id=(peer, ch),
            device_id_type=MESH,
        )

    def copy_from(peer):
        return pltpu.make_async_remote_copy(
            src_ref=x_ref,
            dst_ref=buf.at[peer],
            send_sem=send_sem.at[peer],
            recv_sem=recv_sem.at[peer],
            device_id=(peer, ch),
            device_id_type=MESH,
        )

    def start(k, carry):
        copy_to(lax.rem(me + k, n)).start()
        return carry

    lax.fori_loop(1, n, start, 0)

    def finish(k, carry):
        peer = lax.rem(me + k, n)
        copy_to(peer).wait_send()
        copy_from(peer).wait_recv()
        return carry

    lax.fori_loop(1, n, finish, 0)
    buf[me] = x_ref[...]
    o_ref[...] = buf[...]
    for cp in edges:
        cp.wait()
    left_ref[...] = left_buf[...]
    right_ref[...] = right_buf[...]


def gather_space(tile, cache_t, frames_t):
    n = lax.axis_size("space")
    vmem = pl.BlockSpec(memory_space=pltpu.VMEM)
    hbm = pl.BlockSpec(memory_space=pl.ANY)
    edge = (cache_t.shape[0] + frames_t.shape[0],) + cache_t.shape[2:]
    return pl.pallas_call(
        functools.partial(gather_kernel, n),
        out_shape=(
            jax.ShapeDtypeStruct((n,) + tile.shape, tile.dtype),
            jax.ShapeDtypeStruct(edge, cache_t.dtype),
            jax.ShapeDtypeStruct(edge, cache_t.dtype),
        ),
        in_specs=[vmem, hbm, hbm],
        out_specs=(vmem, vmem, vmem),
        scratch_shapes=[
            pltpu.VMEM((n,) + tile.shape, tile.dtype),
            pltpu.VMEM(edge, cache_t.dtype),
            pltpu.VMEM(edge, cache_t.dtype),
            pltpu.SemaphoreType.DMA((n,)),
            pltpu.SemaphoreType.DMA((n,)),
            pltpu.SemaphoreType.DMA((4,)),
            pltpu.SemaphoreType.DMA((4,)),
        ],
        compiler_params=pltpu.CompilerParams(collective_id=0, has_side_effects=True),
    )(tile, cache_t, frames_t)


def scatter_kernel(nchunk, x_ref, o_ref, recv1, acc1, own, recv2, acc2, recv3,
                   sem1s, sem1r, sem2s, sem2r, sem3s, sem3r):
    sp = lax.axis_index("space")
    c = lax.axis_index("chan")
    core = c % 2
    yh = (c // 2) % 2
    xx = c // 4
    nx, nyh = x_ref.shape[0], x_ref.shape[1]
    width = x_ref.shape[-1] // nchunk
    f32, bf16 = jnp.float32, jnp.bfloat16

    def dev(x_, yh_, core_):
        return (sp, x_ * 4 + yh_ * 2 + core_)

    peers = [dev(xx, yh, 1 - core)]
    peers += [dev(lax.rem(xx + k, nx), yh, core) for k in range(1, nx)]
    peers += [dev(xx, 1 - yh, core)]
    barrier = pltpu.get_barrier_semaphore()
    for p in peers:
        pl.semaphore_signal(barrier, 1, device_id=p, device_id_type=MESH)
    pl.semaphore_wait(barrier, len(peers))

    def cols(q):
        return pl.ds(q * width, width)

    firsts = []
    for q in range(nchunk):
        for i in range(nx):
            for j in range(nyh):
                n = (q * nx + i) * nyh + j
                cp = pltpu.make_async_remote_copy(
                    src_ref=x_ref.at[i, j, 1 - core, :, cols(q)], dst_ref=recv1.at[q, i, j],
                    send_sem=sem1s.at[n], recv_sem=sem1r.at[n],
                    device_id=peers[0], device_id_type=MESH)
                cp.start()
                firsts.append(cp)

    def second(q):
        for cp in firsts[q * nx * nyh : (q + 1) * nx * nyh]:
            cp.wait()
        sends = []
        for k in range(1, nx):
            dest = lax.rem(xx + k, nx)
            for j in range(nyh):
                acc1[q, dest, j] = (x_ref[dest, j, core, :, cols(q)] + recv1[q, dest, j]).astype(bf16)
            slot = nx - 1 - k
            cp = pltpu.make_async_remote_copy(
                src_ref=acc1.at[q, dest], dst_ref=recv2.at[q, slot],
                send_sem=sem2s.at[q * (nx - 1) + k - 1], recv_sem=sem2r.at[q * (nx - 1) + slot],
                device_id=peers[k], device_id_type=MESH)
            cp.start()
            sends.append(cp)
        for j in range(nyh):
            own[q, j] = x_ref[xx, j, core, :, cols(q)] + recv1[q, xx, j]
        return sends

    def third(q):
        for slot in range(nx - 1):
            pltpu.make_async_remote_copy(
                src_ref=acc1.at[q, xx], dst_ref=recv2.at[q, slot],
                send_sem=sem2s.at[q * (nx - 1) + slot], recv_sem=sem2r.at[q * (nx - 1) + slot],
                device_id=peers[0], device_id_type=MESH).wait_recv()
        other = 1 - yh
        total = own[q, other]
        for slot in range(nx - 1):
            total = total + recv2[q, slot, other].astype(f32)
        acc2[q] = total.astype(bf16)
        cp = pltpu.make_async_remote_copy(
            src_ref=acc2.at[q], dst_ref=recv3.at[q], send_sem=sem3s.at[q],
            recv_sem=sem3r.at[q], device_id=peers[nx], device_id_type=MESH)
        cp.start()
        total = own[q, yh]
        for slot in range(nx - 1):
            total = total + recv2[q, slot, yh].astype(f32)
        own[q, yh] = total
        return cp

    seconds, lasts = [], []
    for q in range(nchunk):
        seconds.append(second(q))
        if q >= 1:
            lasts.append(third(q - 1))
    lasts.append(third(nchunk - 1))
    for sends in seconds:
        for cp in sends:
            cp.wait_send()
    for q, cp in enumerate(lasts):
        cp.wait()
        o_ref[:, cols(q)] = own[q, yh] + recv3[q].astype(f32)


def scatter_chan(parts, nchunk=3):
    nx, nyh, ncore, rows, cells = parts.shape
    width = cells // nchunk
    f32, bf16 = jnp.float32, jnp.bfloat16
    return pl.pallas_call(
        functools.partial(scatter_kernel, nchunk),
        out_shape=jax.ShapeDtypeStruct((rows, cells), f32),
        in_specs=[pl.BlockSpec(memory_space=pltpu.VMEM)],
        out_specs=pl.BlockSpec(memory_space=pltpu.VMEM),
        scratch_shapes=[
            pltpu.VMEM((nchunk, nx, nyh, rows, width), f32),
            pltpu.VMEM((nchunk, nx, nyh, rows, width), bf16),
            pltpu.VMEM((nchunk, nyh, rows, width), f32),
            pltpu.VMEM((nchunk, nx - 1, nyh, rows, width), bf16),
            pltpu.VMEM((nchunk, rows, width), bf16),
            pltpu.VMEM((nchunk, rows, width), bf16),
            pltpu.SemaphoreType.DMA((nchunk * nx * nyh,)),
            pltpu.SemaphoreType.DMA((nchunk * nx * nyh,)),
            pltpu.SemaphoreType.DMA((nchunk * (nx - 1),)),
            pltpu.SemaphoreType.DMA((nchunk * (nx - 1),)),
            pltpu.SemaphoreType.DMA((nchunk,)),
            pltpu.SemaphoreType.DMA((nchunk,)),
        ],
        compiler_params=pltpu.CompilerParams(
            collective_id=1, has_side_effects=True, vmem_limit_bytes=48 * 1024 * 1024),
    )(parts)


def local(frames, cache, gamma, beta, kernel, bias):
    nframes, row_count, col_count, local_ch = frames.shape
    ncache = cache.shape[0]
    group_size = CH // GROUPS
    local_groups = local_ch // group_size
    nspace = lax.axis_size("space")
    me = lax.axis_index("space")
    local_members = float(nframes * row_count * col_count * group_size)


    values = frames.astype(jnp.float32).reshape(
        nframes, row_count, col_count, local_groups, group_size
    )
    local_mean = jnp.sum(values, axis=(0, 1, 2, 4)) / local_members
    local_dev = values - local_mean[:, None]
    local_m2 = jnp.sum(local_dev * local_dev, axis=(0, 1, 2, 4))
    tile = jnp.zeros((8, 128), jnp.float32)
    tile = tile.at[0, :local_groups].set(local_mean).at[1, :local_groups].set(local_m2)
    gathered, before, after = gather_space(
        tile, cache.transpose(0, 2, 3, 1), frames.transpose(0, 2, 3, 1)
    )
    before = before.transpose(0, 2, 1)[:, :, None]
    after = after.transpose(0, 2, 1)[:, :, None]
    means = gathered[:, 0, :local_groups]
    m2s = gathered[:, 1, :local_groups]
    group_mean = jnp.mean(means, axis=0)
    spread = jnp.sum(m2s, axis=0) + local_members * jnp.sum(
        (means - group_mean) ** 2, axis=0
    )
    group_var = spread / (local_members * nspace)
    inv = lax.rsqrt(group_var + epsilon)

    def activate(x):
        shape = x.shape
        v = x.astype(jnp.float32).reshape(shape[:-1] + (local_groups, group_size))
        scaled = (v - group_mean[:, None]) * inv[:, None]
        normed = scaled.reshape(shape) * gamma + beta
        return jax.nn.silu(normed).astype(jnp.bfloat16)

    active = activate(frames)
    joined = jnp.concatenate([cache, active], axis=0)
    left = jnp.concatenate([before[:ncache], activate(before[ncache:])], axis=0)
    right = jnp.concatenate([after[:ncache], activate(after[ncache:])], axis=0)
    left = jnp.where(me == 0, jnp.zeros_like(left), left)
    right = jnp.where(me == nspace - 1, jnp.zeros_like(right), right)
    bordered = jnp.concatenate([left, joined, right], axis=2)
    bordered = jnp.pad(bordered, ((0, 0), (1, 1), (0, 0), (0, 0)))
    cell_count = nframes * row_count * col_count
    bordered = bordered.transpose(0, 2, 1, 3)
    rows_in = jnp.concatenate(
        [bordered[:, :, row_tap : row_tap + row_count, :] for row_tap in range(3)], axis=3
    )
    rows_in = with_layout_constraint(rows_in, Layout(major_to_minor=(0, 1, 2, 3)))
    columns_in = jnp.concatenate(
        [rows_in[:, col_tap : col_tap + col_count] for col_tap in range(3)], axis=3
    )
    columns_in = with_layout_constraint(columns_in, Layout(major_to_minor=(0, 1, 2, 3)))
    tap_width = columns_in.shape[3]
    nchan = lax.axis_size("chan")
    nx = nchan // 4
    flat_kernel = kernel.transpose(0, 2, 1, 3, 4).reshape(3, tap_width, kernel.shape[4])
    running = jnp.zeros((bias.shape[0] * nchan, cell_count), jnp.float32)
    plane = row_count * col_count
    flat_in = columns_in.reshape(columns_in.shape[0] * plane, tap_width)
    for depth in range(3):
        tap_weight = flat_kernel[depth]
        window = flat_in[depth * plane : depth * plane + cell_count]
        running = running + lax.dot_general(
            tap_weight, window, (((0,), (1,)), ((), ())), preferred_element_type=jnp.float32
        )
    summed = scatter_chan(running.reshape(nx, 2, 2, local_ch, cell_count))
    result = summed.T + bias
    result = result.astype(jnp.bfloat16).reshape(nframes, col_count, row_count, -1)
    return result.transpose(0, 2, 1, 3)


def solution(mesh):
    placed = (
        P(None, None, "space", "chan"),
        P(None, None, "space", "chan"),
        P("chan"),
        P("chan"),
        P(None, None, None, "chan", None),
        P("chan"),
    )
    return jax.shard_map(
        local, mesh=mesh, in_specs=placed, out_specs=P(None, None, "space", "chan"), check_vma=False
    )
```

```python
import functools

import jax
import jax.numpy as jnp
from jax import lax
from jax.experimental import pallas as pl
from jax.experimental.pallas import tpu as pltpu
from jax.experimental.layout import Layout, with_layout_constraint
from jax.sharding import PartitionSpec as P

CH = 512
GROUPS = 32
MESH = pl.DeviceIdType.MESH

epsilon = 1e-06


def gather_kernel(n, members, x_ref, cache_ref, frames_ref, o_ref, left_ref, right_ref,
                  buf, left_buf, right_buf, send_sem, recv_sem, edge_send, edge_recv):
    me = lax.axis_index("space")
    ch = lax.axis_index("chan")
    right = lax.rem(me + 1, n)
    left = lax.rem(me + n - 1, n)
    barrier = pltpu.get_barrier_semaphore()

    def signal(k, carry):
        peer = lax.rem(me + k, n)
        pl.semaphore_signal(barrier, 1, device_id=(peer, ch), device_id_type=MESH)
        return carry

    lax.fori_loop(1, n, signal, 0)
    pl.semaphore_wait(barrier, n - 1)

    ncache = cache_ref.shape[0]
    last = cache_ref.shape[1] - 1
    edges = []
    for k, (src, lo_row) in enumerate(((cache_ref, 0), (frames_ref, ncache))):
        rows = pl.ds(lo_row, src.shape[0])
        edges.append(pltpu.make_async_remote_copy(
            src_ref=src.at[:, last], dst_ref=left_buf.at[rows], send_sem=edge_send.at[k],
            recv_sem=edge_recv.at[k], device_id=(right, ch), device_id_type=MESH))
        edges.append(pltpu.make_async_remote_copy(
            src_ref=src.at[:, 0], dst_ref=right_buf.at[rows], send_sem=edge_send.at[2 + k],
            recv_sem=edge_recv.at[2 + k], device_id=(left, ch), device_id_type=MESH))
    for cp in edges:
        cp.start()

    def copy_to(peer):
        return pltpu.make_async_remote_copy(
            src_ref=x_ref,
            dst_ref=buf.at[me],
            send_sem=send_sem.at[peer],
            recv_sem=recv_sem.at[me],
            device_id=(peer, ch),
            device_id_type=MESH,
        )

    def copy_from(peer):
        return pltpu.make_async_remote_copy(
            src_ref=x_ref,
            dst_ref=buf.at[peer],
            send_sem=send_sem.at[peer],
            recv_sem=recv_sem.at[peer],
            device_id=(peer, ch),
            device_id_type=MESH,
        )

    def start(k, carry):
        copy_to(lax.rem(me + k, n)).start()
        return carry

    lax.fori_loop(1, n, start, 0)

    def finish(k, carry):
        peer = lax.rem(me + k, n)
        copy_to(peer).wait_send()
        copy_from(peer).wait_recv()
        return carry

    lax.fori_loop(1, n, finish, 0)
    buf[me] = x_ref[...]
    gathered = buf[...]
    means = gathered[:, 0, :]
    group_mean = jnp.sum(means, axis=0, keepdims=True) / n
    spread = jnp.sum(gathered[:, 1, :], axis=0, keepdims=True) + members * jnp.sum(
        (means - group_mean) ** 2, axis=0, keepdims=True
    )
    inv = lax.rsqrt(spread / (members * n) + epsilon)
    o_ref[...] = jnp.concatenate([group_mean, inv, jnp.zeros((6,) + inv.shape[1:], inv.dtype)], axis=0)
    for cp in edges:
        cp.wait()
    left_ref[...] = left_buf[...]
    right_ref[...] = right_buf[...]


def gather_space(tile, cache_t, frames_t, members):
    n = lax.axis_size("space")
    vmem = pl.BlockSpec(memory_space=pltpu.VMEM)
    hbm = pl.BlockSpec(memory_space=pl.ANY)
    edge = (cache_t.shape[0] + frames_t.shape[0],) + cache_t.shape[2:]
    return pl.pallas_call(
        functools.partial(gather_kernel, n, members),
        out_shape=(
            jax.ShapeDtypeStruct(tile.shape, tile.dtype),
            jax.ShapeDtypeStruct(edge, cache_t.dtype),
            jax.ShapeDtypeStruct(edge, cache_t.dtype),
        ),
        in_specs=[vmem, hbm, hbm],
        out_specs=(vmem, vmem, vmem),
        scratch_shapes=[
            pltpu.VMEM((n,) + tile.shape, tile.dtype),
            pltpu.VMEM(edge, cache_t.dtype),
            pltpu.VMEM(edge, cache_t.dtype),
            pltpu.SemaphoreType.DMA((n,)),
            pltpu.SemaphoreType.DMA((n,)),
            pltpu.SemaphoreType.DMA((4,)),
            pltpu.SemaphoreType.DMA((4,)),
        ],
        compiler_params=pltpu.CompilerParams(collective_id=0, has_side_effects=True),
    )(tile, cache_t, frames_t)


def scatter_kernel(nchunk, x_ref, o_ref, recv1, acc1, own, recv2, acc2, recv3,
                   sem1s, sem1r, sem2s, sem2r, sem3s, sem3r):
    sp = lax.axis_index("space")
    c = lax.axis_index("chan")
    core = c % 2
    yh = (c // 2) % 2
    xx = c // 4
    nx, nyh = x_ref.shape[0], x_ref.shape[1]
    width = x_ref.shape[-1] // nchunk
    f32, bf16 = jnp.float32, jnp.bfloat16

    def dev(x_, yh_, core_):
        return (sp, x_ * 4 + yh_ * 2 + core_)

    peers = [dev(xx, yh, 1 - core)]
    peers += [dev(lax.rem(xx + k, nx), yh, core) for k in range(1, nx)]
    peers += [dev(xx, 1 - yh, core)]
    barrier = pltpu.get_barrier_semaphore()
    for p in peers:
        pl.semaphore_signal(barrier, 1, device_id=p, device_id_type=MESH)
    pl.semaphore_wait(barrier, len(peers))

    def cols(q):
        return pl.ds(q * width, width)

    firsts = []
    for q in range(nchunk):
        for i in range(nx):
            for j in range(nyh):
                n = (q * nx + i) * nyh + j
                cp = pltpu.make_async_remote_copy(
                    src_ref=x_ref.at[i, j, 1 - core, :, cols(q)], dst_ref=recv1.at[q, i, j],
                    send_sem=sem1s.at[n], recv_sem=sem1r.at[n],
                    device_id=peers[0], device_id_type=MESH)
                cp.start()
                firsts.append(cp)

    def second(q):
        for cp in firsts[q * nx * nyh : (q + 1) * nx * nyh]:
            cp.wait()
        sends = []
        for k in range(1, nx):
            dest = lax.rem(xx + k, nx)
            for j in range(nyh):
                acc1[q, dest, j] = (x_ref[dest, j, core, :, cols(q)] + recv1[q, dest, j]).astype(bf16)
            slot = nx - 1 - k
            cp = pltpu.make_async_remote_copy(
                src_ref=acc1.at[q, dest], dst_ref=recv2.at[q, slot],
                send_sem=sem2s.at[q * (nx - 1) + k - 1], recv_sem=sem2r.at[q * (nx - 1) + slot],
                device_id=peers[k], device_id_type=MESH)
            cp.start()
            sends.append(cp)
        for j in range(nyh):
            own[q, j] = x_ref[xx, j, core, :, cols(q)] + recv1[q, xx, j]
        return sends

    def third(q):
        for slot in range(nx - 1):
            pltpu.make_async_remote_copy(
                src_ref=acc1.at[q, xx], dst_ref=recv2.at[q, slot],
                send_sem=sem2s.at[q * (nx - 1) + slot], recv_sem=sem2r.at[q * (nx - 1) + slot],
                device_id=peers[0], device_id_type=MESH).wait_recv()
        other = 1 - yh
        total = own[q, other]
        for slot in range(nx - 1):
            total = total + recv2[q, slot, other].astype(f32)
        acc2[q] = total.astype(bf16)
        cp = pltpu.make_async_remote_copy(
            src_ref=acc2.at[q], dst_ref=recv3.at[q], send_sem=sem3s.at[q],
            recv_sem=sem3r.at[q], device_id=peers[nx], device_id_type=MESH)
        cp.start()
        total = own[q, yh]
        for slot in range(nx - 1):
            total = total + recv2[q, slot, yh].astype(f32)
        own[q, yh] = total
        return cp

    seconds, lasts = [], []
    for q in range(nchunk):
        seconds.append(second(q))
        if q >= 1:
            lasts.append(third(q - 1))
    lasts.append(third(nchunk - 1))
    for sends in seconds:
        for cp in sends:
            cp.wait_send()
    for q, cp in enumerate(lasts):
        cp.wait()
        o_ref[:, cols(q)] = own[q, yh] + recv3[q].astype(f32)


def scatter_chan(parts, nchunk=3):
    nx, nyh, ncore, rows, cells = parts.shape
    width = cells // nchunk
    f32, bf16 = jnp.float32, jnp.bfloat16
    return pl.pallas_call(
        functools.partial(scatter_kernel, nchunk),
        out_shape=jax.ShapeDtypeStruct((rows, cells), f32),
        in_specs=[pl.BlockSpec(memory_space=pltpu.VMEM)],
        out_specs=pl.BlockSpec(memory_space=pltpu.VMEM),
        scratch_shapes=[
            pltpu.VMEM((nchunk, nx, nyh, rows, width), f32),
            pltpu.VMEM((nchunk, nx, nyh, rows, width), bf16),
            pltpu.VMEM((nchunk, nyh, rows, width), f32),
            pltpu.VMEM((nchunk, nx - 1, nyh, rows, width), bf16),
            pltpu.VMEM((nchunk, rows, width), bf16),
            pltpu.VMEM((nchunk, rows, width), bf16),
            pltpu.SemaphoreType.DMA((nchunk * nx * nyh,)),
            pltpu.SemaphoreType.DMA((nchunk * nx * nyh,)),
            pltpu.SemaphoreType.DMA((nchunk * (nx - 1),)),
            pltpu.SemaphoreType.DMA((nchunk * (nx - 1),)),
            pltpu.SemaphoreType.DMA((nchunk,)),
            pltpu.SemaphoreType.DMA((nchunk,)),
        ],
        compiler_params=pltpu.CompilerParams(
            collective_id=1, has_side_effects=True, vmem_limit_bytes=48 * 1024 * 1024),
    )(parts)


def local(frames, cache, gamma, beta, kernel, bias):
    nframes, row_count, col_count, local_ch = frames.shape
    ncache = cache.shape[0]
    group_size = CH // GROUPS
    local_groups = local_ch // group_size
    nspace = lax.axis_size("space")
    me = lax.axis_index("space")
    local_members = float(nframes * row_count * col_count * group_size)


    values = frames.astype(jnp.float32).reshape(
        nframes, row_count, col_count, local_groups, group_size
    )
    local_mean = jnp.sum(values, axis=(0, 1, 2, 4)) / local_members
    local_dev = values - local_mean[:, None]
    local_m2 = jnp.sum(local_dev * local_dev, axis=(0, 1, 2, 4))
    tile = jnp.zeros((8, 128), jnp.float32)
    tile = tile.at[0, :local_groups].set(local_mean).at[1, :local_groups].set(local_m2)
    combined, before, after = gather_space(
        tile, cache.transpose(0, 2, 3, 1), frames.transpose(0, 2, 3, 1), local_members
    )
    before = before.transpose(0, 2, 1)[:, :, None]
    after = after.transpose(0, 2, 1)[:, :, None]
    group_mean = combined[0, :local_groups]
    inv = combined[1, :local_groups]

    def activate(x):
        shape = x.shape
        v = x.astype(jnp.float32).reshape(shape[:-1] + (local_groups, group_size))
        scaled = (v - group_mean[:, None]) * inv[:, None]
        normed = scaled.reshape(shape) * gamma + beta
        return jax.nn.silu(normed).astype(jnp.bfloat16)

    active = activate(frames)
    joined = jnp.concatenate([cache, active], axis=0)
    left = jnp.concatenate([before[:ncache], activate(before[ncache:])], axis=0)
    right = jnp.concatenate([after[:ncache], activate(after[ncache:])], axis=0)
    left = jnp.where(me == 0, jnp.zeros_like(left), left)
    right = jnp.where(me == nspace - 1, jnp.zeros_like(right), right)
    bordered = jnp.concatenate([left, joined, right], axis=2)
    bordered = jnp.pad(bordered, ((0, 0), (1, 1), (0, 0), (0, 0)))
    cell_count = nframes * row_count * col_count
    bordered = bordered.transpose(0, 2, 1, 3)
    rows_in = jnp.concatenate(
        [bordered[:, :, row_tap : row_tap + row_count, :] for row_tap in range(3)], axis=3
    )
    rows_in = with_layout_constraint(rows_in, Layout(major_to_minor=(0, 1, 2, 3)))
    columns_in = jnp.concatenate(
        [rows_in[:, col_tap : col_tap + col_count] for col_tap in range(3)], axis=3
    )
    columns_in = with_layout_constraint(columns_in, Layout(major_to_minor=(0, 1, 2, 3)))
    tap_width = columns_in.shape[3]
    nchan = lax.axis_size("chan")
    nx = nchan // 4
    flat_kernel = kernel.transpose(0, 2, 1, 3, 4).reshape(3, tap_width, kernel.shape[4])
    running = jnp.zeros((bias.shape[0] * nchan, cell_count), jnp.float32)
    plane = row_count * col_count
    flat_in = columns_in.reshape(columns_in.shape[0] * plane, tap_width)
    for depth in range(3):
        tap_weight = flat_kernel[depth]
        window = flat_in[depth * plane : depth * plane + cell_count]
        running = running + lax.dot_general(
            tap_weight, window, (((0,), (1,)), ((), ())), preferred_element_type=jnp.float32
        )
    summed = scatter_chan(running.reshape(nx, 2, 2, local_ch, cell_count))
    result = summed.T + bias
    result = result.astype(jnp.bfloat16).reshape(nframes, col_count, row_count, -1)
    return result.transpose(0, 2, 1, 3)


def solution(mesh):
    placed = (
        P(None, None, "space", "chan"),
        P(None, None, "space", "chan"),
        P("chan"),
        P("chan"),
        P(None, None, None, "chan", None),
        P("chan"),
    )
    return jax.shard_map(
        local, mesh=mesh, in_specs=placed, out_specs=P(None, None, "space", "chan"), check_vma=False
    )
```

```python
import functools

import jax
import jax.numpy as jnp
from jax import lax
from jax.experimental import pallas as pl
from jax.experimental.pallas import tpu as pltpu
from jax.experimental.layout import Layout, with_layout_constraint
from jax.sharding import PartitionSpec as P

CH = 512
GROUPS = 32
MESH = pl.DeviceIdType.MESH

epsilon = 1e-06


def gather_kernel(n, x_ref, cache_ref, frames_ref, o_ref, left_ref, right_ref,
                  buf, left_buf, right_buf, send_sem, recv_sem, edge_send, edge_recv):
    me = lax.axis_index("space")
    ch = lax.axis_index("chan")
    right = lax.rem(me + 1, n)
    left = lax.rem(me + n - 1, n)
    barrier = pltpu.get_barrier_semaphore()

    def signal(k, carry):
        peer = lax.rem(me + k, n)
        pl.semaphore_signal(barrier, 1, device_id=(peer, ch), device_id_type=MESH)
        return carry

    lax.fori_loop(1, n, signal, 0)
    pl.semaphore_wait(barrier, n - 1)

    ncache = cache_ref.shape[0]
    last = cache_ref.shape[1] - 1
    edges = []
    for k, (src, lo_row) in enumerate(((cache_ref, 0), (frames_ref, ncache))):
        rows = pl.ds(lo_row, src.shape[0])
        edges.append(pltpu.make_async_remote_copy(
            src_ref=src.at[:, last], dst_ref=left_buf.at[rows], send_sem=edge_send.at[k],
            recv_sem=edge_recv.at[k], device_id=(right, ch), device_id_type=MESH))
        edges.append(pltpu.make_async_remote_copy(
            src_ref=src.at[:, 0], dst_ref=right_buf.at[rows], send_sem=edge_send.at[2 + k],
            recv_sem=edge_recv.at[2 + k], device_id=(left, ch), device_id_type=MESH))
    for cp in edges:
        cp.start()

    def copy_to(peer):
        return pltpu.make_async_remote_copy(
            src_ref=x_ref,
            dst_ref=buf.at[me],
            send_sem=send_sem.at[peer],
            recv_sem=recv_sem.at[me],
            device_id=(peer, ch),
            device_id_type=MESH,
        )

    def copy_from(peer):
        return pltpu.make_async_remote_copy(
            src_ref=x_ref,
            dst_ref=buf.at[peer],
            send_sem=send_sem.at[peer],
            recv_sem=recv_sem.at[peer],
            device_id=(peer, ch),
            device_id_type=MESH,
        )

    def start(k, carry):
        copy_to(lax.rem(me + k, n)).start()
        return carry

    lax.fori_loop(1, n, start, 0)

    def finish(k, carry):
        peer = lax.rem(me + k, n)
        copy_to(peer).wait_send()
        copy_from(peer).wait_recv()
        return carry

    lax.fori_loop(1, n, finish, 0)
    buf[me] = x_ref[...]
    o_ref[...] = buf[...]
    for cp in edges:
        cp.wait()
    left_ref[...] = left_buf[...]
    right_ref[...] = right_buf[...]


def gather_space(tile, cache_t, frames_t):
    n = lax.axis_size("space")
    vmem = pl.BlockSpec(memory_space=pltpu.VMEM)
    hbm = pl.BlockSpec(memory_space=pl.ANY)
    edge = (cache_t.shape[0] + frames_t.shape[0],) + cache_t.shape[2:]
    return pl.pallas_call(
        functools.partial(gather_kernel, n),
        out_shape=(
            jax.ShapeDtypeStruct((n,) + tile.shape, tile.dtype),
            jax.ShapeDtypeStruct(edge, cache_t.dtype),
            jax.ShapeDtypeStruct(edge, cache_t.dtype),
        ),
        in_specs=[vmem, hbm, hbm],
        out_specs=(vmem, vmem, vmem),
        scratch_shapes=[
            pltpu.VMEM((n,) + tile.shape, tile.dtype),
            pltpu.VMEM(edge, cache_t.dtype),
            pltpu.VMEM(edge, cache_t.dtype),
            pltpu.SemaphoreType.DMA((n,)),
            pltpu.SemaphoreType.DMA((n,)),
            pltpu.SemaphoreType.DMA((4,)),
            pltpu.SemaphoreType.DMA((4,)),
        ],
        compiler_params=pltpu.CompilerParams(collective_id=0, has_side_effects=True),
    )(tile, cache_t, frames_t)


def scatter_kernel(nchunk, x_ref, o_ref, recv1, acc1, own, recv2, acc2, recv3,
                   sem1s, sem1r, sem2s, sem2r, sem3s, sem3r):
    sp = lax.axis_index("space")
    c = lax.axis_index("chan")
    core = c % 2
    yh = (c // 2) % 2
    xx = c // 4
    nx, nyh = x_ref.shape[0], x_ref.shape[1]
    width = x_ref.shape[-1] // nchunk
    f32, bf16 = jnp.float32, jnp.bfloat16

    def dev(x_, yh_, core_):
        return (sp, x_ * 4 + yh_ * 2 + core_)

    peers = [dev(xx, yh, 1 - core)]
    peers += [dev(lax.rem(xx + k, nx), yh, core) for k in range(1, nx)]
    peers += [dev(xx, 1 - yh, core)]
    barrier = pltpu.get_barrier_semaphore()
    for p in peers:
        pl.semaphore_signal(barrier, 1, device_id=p, device_id_type=MESH)
    pl.semaphore_wait(barrier, len(peers))

    def cols(q):
        return pl.ds(q * width, width)

    firsts = []
    for q in range(nchunk):
        for i in range(nx):
            for j in range(nyh):
                n = (q * nx + i) * nyh + j
                cp = pltpu.make_async_remote_copy(
                    src_ref=x_ref.at[i, j, 1 - core, :, cols(q)], dst_ref=recv1.at[q, i, j],
                    send_sem=sem1s.at[n], recv_sem=sem1r.at[n],
                    device_id=peers[0], device_id_type=MESH)
                cp.start()
                firsts.append(cp)

    def second(q):
        for cp in firsts[q * nx * nyh : (q + 1) * nx * nyh]:
            cp.wait()
        sends = []
        for k in range(1, nx):
            dest = lax.rem(xx + k, nx)
            for j in range(nyh):
                acc1[q, dest, j] = (x_ref[dest, j, core, :, cols(q)] + recv1[q, dest, j]).astype(bf16)
            slot = nx - 1 - k
            cp = pltpu.make_async_remote_copy(
                src_ref=acc1.at[q, dest], dst_ref=recv2.at[q, slot],
                send_sem=sem2s.at[q * (nx - 1) + k - 1], recv_sem=sem2r.at[q * (nx - 1) + slot],
                device_id=peers[k], device_id_type=MESH)
            cp.start()
            sends.append(cp)
        for j in range(nyh):
            own[q, j] = x_ref[xx, j, core, :, cols(q)] + recv1[q, xx, j]
        return sends

    def third(q):
        for slot in range(nx - 1):
            pltpu.make_async_remote_copy(
                src_ref=acc1.at[q, xx], dst_ref=recv2.at[q, slot],
                send_sem=sem2s.at[q * (nx - 1) + slot], recv_sem=sem2r.at[q * (nx - 1) + slot],
                device_id=peers[0], device_id_type=MESH).wait_recv()
        other = 1 - yh
        total = own[q, other]
        for slot in range(nx - 1):
            total = total + recv2[q, slot, other].astype(f32)
        acc2[q] = total.astype(bf16)
        cp = pltpu.make_async_remote_copy(
            src_ref=acc2.at[q], dst_ref=recv3.at[q], send_sem=sem3s.at[q],
            recv_sem=sem3r.at[q], device_id=peers[nx], device_id_type=MESH)
        cp.start()
        total = own[q, yh]
        for slot in range(nx - 1):
            total = total + recv2[q, slot, yh].astype(f32)
        own[q, yh] = total
        return cp

    seconds, lasts = [], []
    for q in range(nchunk):
        seconds.append(second(q))
        if q >= 1:
            lasts.append(third(q - 1))
    lasts.append(third(nchunk - 1))
    for sends in seconds:
        for cp in sends:
            cp.wait_send()
    for q, cp in enumerate(lasts):
        cp.wait()
        o_ref[:, cols(q)] = own[q, yh] + recv3[q].astype(f32)


def scatter_chan(parts, nchunk=3):
    nx, nyh, ncore, rows, cells = parts.shape
    width = cells // nchunk
    f32, bf16 = jnp.float32, jnp.bfloat16
    return pl.pallas_call(
        functools.partial(scatter_kernel, nchunk),
        out_shape=jax.ShapeDtypeStruct((rows, cells), f32),
        in_specs=[pl.BlockSpec(memory_space=pltpu.VMEM)],
        out_specs=pl.BlockSpec(memory_space=pltpu.VMEM),
        scratch_shapes=[
            pltpu.VMEM((nchunk, nx, nyh, rows, width), f32),
            pltpu.VMEM((nchunk, nx, nyh, rows, width), bf16),
            pltpu.VMEM((nchunk, nyh, rows, width), f32),
            pltpu.VMEM((nchunk, nx - 1, nyh, rows, width), bf16),
            pltpu.VMEM((nchunk, rows, width), bf16),
            pltpu.VMEM((nchunk, rows, width), bf16),
            pltpu.SemaphoreType.DMA((nchunk * nx * nyh,)),
            pltpu.SemaphoreType.DMA((nchunk * nx * nyh,)),
            pltpu.SemaphoreType.DMA((nchunk * (nx - 1),)),
            pltpu.SemaphoreType.DMA((nchunk * (nx - 1),)),
            pltpu.SemaphoreType.DMA((nchunk,)),
            pltpu.SemaphoreType.DMA((nchunk,)),
        ],
        compiler_params=pltpu.CompilerParams(
            collective_id=1, has_side_effects=True, vmem_limit_bytes=48 * 1024 * 1024),
    )(parts)


def local(frames, cache, gamma, beta, kernel, bias):
    nframes, row_count, col_count, local_ch = frames.shape
    ncache = cache.shape[0]
    group_size = CH // GROUPS
    local_groups = local_ch // group_size
    nspace = lax.axis_size("space")
    me = lax.axis_index("space")
    local_members = float(nframes * row_count * col_count * group_size)


    values = frames.astype(jnp.float32).reshape(
        nframes, row_count, col_count, local_groups, group_size
    )
    local_mean = jnp.sum(values, axis=(0, 1, 2, 4)) / local_members
    local_dev = values - local_mean[:, None]
    local_m2 = jnp.sum(local_dev * local_dev, axis=(0, 1, 2, 4))
    tile = jnp.zeros((8, 128), jnp.float32)
    tile = tile.at[0, :local_groups].set(local_mean).at[1, :local_groups].set(local_m2)
    gathered, before, after = gather_space(
        tile, cache.transpose(0, 2, 3, 1), frames.transpose(0, 2, 3, 1)
    )
    before = before.transpose(0, 2, 1)[:, :, None]
    after = after.transpose(0, 2, 1)[:, :, None]
    means = gathered[:, 0, :local_groups]
    m2s = gathered[:, 1, :local_groups]
    group_mean = jnp.mean(means, axis=0)
    spread = jnp.sum(m2s, axis=0) + local_members * jnp.sum(
        (means - group_mean) ** 2, axis=0
    )
    group_var = spread / (local_members * nspace)
    inv = lax.rsqrt(group_var + epsilon)

    def activate(x):
        shape = x.shape
        v = x.astype(jnp.float32).reshape(shape[:-1] + (local_groups, group_size))
        scaled = (v - group_mean[:, None]) * inv[:, None]
        normed = scaled.reshape(shape) * gamma + beta
        return jax.nn.silu(normed).astype(jnp.bfloat16)

    active = activate(frames)
    joined = jnp.concatenate([cache, active], axis=0)
    left = jnp.concatenate([before[:ncache], activate(before[ncache:])], axis=0)
    right = jnp.concatenate([after[:ncache], activate(after[ncache:])], axis=0)
    left = jnp.where(me == 0, jnp.zeros_like(left), left)
    right = jnp.where(me == nspace - 1, jnp.zeros_like(right), right)
    bordered = jnp.concatenate([left, joined, right], axis=2)
    bordered = jnp.pad(bordered, ((0, 0), (1, 1), (0, 0), (0, 0)))
    cell_count = nframes * row_count * col_count
    bordered = bordered.transpose(0, 2, 1, 3)
    rows_in = jnp.concatenate(
        [bordered[:, :, row_tap : row_tap + row_count, :] for row_tap in range(3)], axis=3
    )
    rows_in = with_layout_constraint(rows_in, Layout(major_to_minor=(0, 1, 2, 3)))
    columns_in = jnp.concatenate(
        [rows_in[:, col_tap : col_tap + col_count] for col_tap in range(3)], axis=3
    )
    columns_in = with_layout_constraint(columns_in, Layout(major_to_minor=(0, 1, 2, 3)))
    tap_width = columns_in.shape[3]
    nchan = lax.axis_size("chan")
    nx = nchan // 4
    flat_kernel = kernel.transpose(0, 2, 1, 3, 4).reshape(3, tap_width, kernel.shape[4])
    running = jnp.zeros((bias.shape[0] * nchan, cell_count), jnp.float32)
    plane = row_count * col_count
    flat_in = columns_in.reshape(columns_in.shape[0] * plane, tap_width)
    for depth in range(3):
        tap_weight = flat_kernel[depth]
        window = flat_in[depth * plane : depth * plane + cell_count]
        running = running + lax.dot_general(
            tap_weight, window, (((0,), (1,)), ((), ())), preferred_element_type=jnp.float32
        )
    summed = scatter_chan(running.reshape(nx, 2, 2, local_ch, cell_count))
    result = (summed + bias[:, None]).astype(jnp.bfloat16)
    result = result.reshape(-1, nframes, col_count, row_count)
    return result.transpose(1, 3, 2, 0)


def solution(mesh):
    placed = (
        P(None, None, "space", "chan"),
        P(None, None, "space", "chan"),
        P("chan"),
        P("chan"),
        P(None, None, None, "chan", None),
        P("chan"),
    )
    return jax.shard_map(
        local, mesh=mesh, in_specs=placed, out_specs=P(None, None, "space", "chan"), check_vma=False
    )
```

```python
import functools

import jax
import jax.numpy as jnp
from jax import lax
from jax.experimental import pallas as pl
from jax.experimental.pallas import tpu as pltpu
from jax.experimental.layout import Layout, with_layout_constraint
from jax.sharding import PartitionSpec as P

CH = 512
GROUPS = 32
MESH = pl.DeviceIdType.MESH

epsilon = 1e-06


def gather_kernel(n, x_ref, cache_ref, frames_ref, o_ref, left_ref, right_ref,
                  buf, left_buf, right_buf, send_sem, recv_sem, edge_send, edge_recv):
    me = lax.axis_index("space")
    ch = lax.axis_index("chan")
    right = lax.rem(me + 1, n)
    left = lax.rem(me + n - 1, n)
    barrier = pltpu.get_barrier_semaphore()

    def signal(k, carry):
        peer = lax.rem(me + k, n)
        pl.semaphore_signal(barrier, 1, device_id=(peer, ch), device_id_type=MESH)
        return carry

    lax.fori_loop(1, n, signal, 0)
    pl.semaphore_wait(barrier, n - 1)

    ncache = cache_ref.shape[0]
    last = cache_ref.shape[1] - 1
    edges = []
    for k, (src, lo_row) in enumerate(((cache_ref, 0), (frames_ref, ncache))):
        rows = pl.ds(lo_row, src.shape[0])
        edges.append(pltpu.make_async_remote_copy(
            src_ref=src.at[:, last], dst_ref=left_buf.at[rows], send_sem=edge_send.at[k],
            recv_sem=edge_recv.at[k], device_id=(right, ch), device_id_type=MESH))
        edges.append(pltpu.make_async_remote_copy(
            src_ref=src.at[:, 0], dst_ref=right_buf.at[rows], send_sem=edge_send.at[2 + k],
            recv_sem=edge_recv.at[2 + k], device_id=(left, ch), device_id_type=MESH))
    for cp in edges:
        cp.start()

    def copy_to(peer):
        return pltpu.make_async_remote_copy(
            src_ref=x_ref,
            dst_ref=buf.at[me],
            send_sem=send_sem.at[peer],
            recv_sem=recv_sem.at[me],
            device_id=(peer, ch),
            device_id_type=MESH,
        )

    def copy_from(peer):
        return pltpu.make_async_remote_copy(
            src_ref=x_ref,
            dst_ref=buf.at[peer],
            send_sem=send_sem.at[peer],
            recv_sem=recv_sem.at[peer],
            device_id=(peer, ch),
            device_id_type=MESH,
        )

    def start(k, carry):
        copy_to(lax.rem(me + k, n)).start()
        return carry

    lax.fori_loop(1, n, start, 0)

    def finish(k, carry):
        peer = lax.rem(me + k, n)
        copy_to(peer).wait_send()
        copy_from(peer).wait_recv()
        return carry

    lax.fori_loop(1, n, finish, 0)
    buf[me] = x_ref[...]
    o_ref[...] = buf[...]
    for cp in edges:
        cp.wait()
    for t in range(left_ref.shape[0]):
        left_ref[t] = left_buf[t].astype(jnp.float32).T.astype(left_ref.dtype)
        right_ref[t] = right_buf[t].astype(jnp.float32).T.astype(right_ref.dtype)


def gather_space(tile, cache_t, frames_t):
    n = lax.axis_size("space")
    vmem = pl.BlockSpec(memory_space=pltpu.VMEM)
    hbm = pl.BlockSpec(memory_space=pl.ANY)
    edge = (cache_t.shape[0] + frames_t.shape[0],) + cache_t.shape[2:]
    edge_t = edge[:1] + edge[:0:-1]
    return pl.pallas_call(
        functools.partial(gather_kernel, n),
        out_shape=(
            jax.ShapeDtypeStruct((n,) + tile.shape, tile.dtype),
            jax.ShapeDtypeStruct(edge_t, cache_t.dtype),
            jax.ShapeDtypeStruct(edge_t, cache_t.dtype),
        ),
        in_specs=[vmem, hbm, hbm],
        out_specs=(vmem, vmem, vmem),
        scratch_shapes=[
            pltpu.VMEM((n,) + tile.shape, tile.dtype),
            pltpu.VMEM(edge, cache_t.dtype),
            pltpu.VMEM(edge, cache_t.dtype),
            pltpu.SemaphoreType.DMA((n,)),
            pltpu.SemaphoreType.DMA((n,)),
            pltpu.SemaphoreType.DMA((4,)),
            pltpu.SemaphoreType.DMA((4,)),
        ],
        compiler_params=pltpu.CompilerParams(collective_id=0, has_side_effects=True),
    )(tile, cache_t, frames_t)


def scatter_kernel(nchunk, x_ref, o_ref, recv1, acc1, own, recv2, acc2, recv3,
                   sem1s, sem1r, sem2s, sem2r, sem3s, sem3r):
    sp = lax.axis_index("space")
    c = lax.axis_index("chan")
    core = c % 2
    yh = (c // 2) % 2
    xx = c // 4
    nx, nyh = x_ref.shape[0], x_ref.shape[1]
    width = x_ref.shape[-1] // nchunk
    f32, bf16 = jnp.float32, jnp.bfloat16

    def dev(x_, yh_, core_):
        return (sp, x_ * 4 + yh_ * 2 + core_)

    peers = [dev(xx, yh, 1 - core)]
    peers += [dev(lax.rem(xx + k, nx), yh, core) for k in range(1, nx)]
    peers += [dev(xx, 1 - yh, core)]
    barrier = pltpu.get_barrier_semaphore()
    for p in peers:
        pl.semaphore_signal(barrier, 1, device_id=p, device_id_type=MESH)
    pl.semaphore_wait(barrier, len(peers))

    def cols(q):
        return pl.ds(q * width, width)

    firsts = []
    for q in range(nchunk):
        for i in range(nx):
            for j in range(nyh):
                n = (q * nx + i) * nyh + j
                cp = pltpu.make_async_remote_copy(
                    src_ref=x_ref.at[i, j, 1 - core, :, cols(q)], dst_ref=recv1.at[q, i, j],
                    send_sem=sem1s.at[n], recv_sem=sem1r.at[n],
                    device_id=peers[0], device_id_type=MESH)
                cp.start()
                firsts.append(cp)

    def second(q):
        for cp in firsts[q * nx * nyh : (q + 1) * nx * nyh]:
            cp.wait()
        sends = []
        for k in range(1, nx):
            dest = lax.rem(xx + k, nx)
            for j in range(nyh):
                acc1[q, dest, j] = (x_ref[dest, j, core, :, cols(q)] + recv1[q, dest, j]).astype(bf16)
            slot = nx - 1 - k
            cp = pltpu.make_async_remote_copy(
                src_ref=acc1.at[q, dest], dst_ref=recv2.at[q, slot],
                send_sem=sem2s.at[q * (nx - 1) + k - 1], recv_sem=sem2r.at[q * (nx - 1) + slot],
                device_id=peers[k], device_id_type=MESH)
            cp.start()
            sends.append(cp)
        for j in range(nyh):
            own[q, j] = x_ref[xx, j, core, :, cols(q)] + recv1[q, xx, j]
        return sends

    def third(q):
        for slot in range(nx - 1):
            pltpu.make_async_remote_copy(
                src_ref=acc1.at[q, xx], dst_ref=recv2.at[q, slot],
                send_sem=sem2s.at[q * (nx - 1) + slot], recv_sem=sem2r.at[q * (nx - 1) + slot],
                device_id=peers[0], device_id_type=MESH).wait_recv()
        other = 1 - yh
        total = own[q, other]
        for slot in range(nx - 1):
            total = total + recv2[q, slot, other].astype(f32)
        acc2[q] = total.astype(bf16)
        cp = pltpu.make_async_remote_copy(
            src_ref=acc2.at[q], dst_ref=recv3.at[q], send_sem=sem3s.at[q],
            recv_sem=sem3r.at[q], device_id=peers[nx], device_id_type=MESH)
        cp.start()
        total = own[q, yh]
        for slot in range(nx - 1):
            total = total + recv2[q, slot, yh].astype(f32)
        own[q, yh] = total
        return cp

    seconds, lasts = [], []
    for q in range(nchunk):
        seconds.append(second(q))
        if q >= 1:
            lasts.append(third(q - 1))
    lasts.append(third(nchunk - 1))
    for sends in seconds:
        for cp in sends:
            cp.wait_send()
    for q, cp in enumerate(lasts):
        cp.wait()
        o_ref[:, cols(q)] = own[q, yh] + recv3[q].astype(f32)


def scatter_chan(parts, nchunk=3):
    nx, nyh, ncore, rows, cells = parts.shape
    width = cells // nchunk
    f32, bf16 = jnp.float32, jnp.bfloat16
    return pl.pallas_call(
        functools.partial(scatter_kernel, nchunk),
        out_shape=jax.ShapeDtypeStruct((rows, cells), f32),
        in_specs=[pl.BlockSpec(memory_space=pltpu.VMEM)],
        out_specs=pl.BlockSpec(memory_space=pltpu.VMEM),
        scratch_shapes=[
            pltpu.VMEM((nchunk, nx, nyh, rows, width), f32),
            pltpu.VMEM((nchunk, nx, nyh, rows, width), bf16),
            pltpu.VMEM((nchunk, nyh, rows, width), f32),
            pltpu.VMEM((nchunk, nx - 1, nyh, rows, width), bf16),
            pltpu.VMEM((nchunk, rows, width), bf16),
            pltpu.VMEM((nchunk, rows, width), bf16),
            pltpu.SemaphoreType.DMA((nchunk * nx * nyh,)),
            pltpu.SemaphoreType.DMA((nchunk * nx * nyh,)),
            pltpu.SemaphoreType.DMA((nchunk * (nx - 1),)),
            pltpu.SemaphoreType.DMA((nchunk * (nx - 1),)),
            pltpu.SemaphoreType.DMA((nchunk,)),
            pltpu.SemaphoreType.DMA((nchunk,)),
        ],
        compiler_params=pltpu.CompilerParams(
            collective_id=1, has_side_effects=True, vmem_limit_bytes=48 * 1024 * 1024),
    )(parts)


def local(frames, cache, gamma, beta, kernel, bias):
    nframes, row_count, col_count, local_ch = frames.shape
    ncache = cache.shape[0]
    group_size = CH // GROUPS
    local_groups = local_ch // group_size
    nspace = lax.axis_size("space")
    me = lax.axis_index("space")
    local_members = float(nframes * row_count * col_count * group_size)


    values = frames.astype(jnp.float32).reshape(
        nframes, row_count, col_count, local_groups, group_size
    )
    local_mean = jnp.sum(values, axis=(0, 1, 2, 4)) / local_members
    local_dev = values - local_mean[:, None]
    local_m2 = jnp.sum(local_dev * local_dev, axis=(0, 1, 2, 4))
    tile = jnp.zeros((8, 128), jnp.float32)
    tile = tile.at[0, :local_groups].set(local_mean).at[1, :local_groups].set(local_m2)
    gathered, before, after = gather_space(
        tile, cache.transpose(0, 2, 3, 1), frames.transpose(0, 2, 3, 1)
    )
    before = before[:, :, None]
    after = after[:, :, None]
    means = gathered[:, 0, :local_groups]
    m2s = gathered[:, 1, :local_groups]
    group_mean = jnp.mean(means, axis=0)
    spread = jnp.sum(m2s, axis=0) + local_members * jnp.sum(
        (means - group_mean) ** 2, axis=0
    )
    group_var = spread / (local_members * nspace)
    inv = lax.rsqrt(group_var + epsilon)

    def activate(x):
        shape = x.shape
        v = x.astype(jnp.float32).reshape(shape[:-1] + (local_groups, group_size))
        scaled = (v - group_mean[:, None]) * inv[:, None]
        normed = scaled.reshape(shape) * gamma + beta
        return jax.nn.silu(normed).astype(jnp.bfloat16)

    active = activate(frames)
    joined = jnp.concatenate([cache, active], axis=0)
    left = jnp.concatenate([before[:ncache], activate(before[ncache:])], axis=0)
    right = jnp.concatenate([after[:ncache], activate(after[ncache:])], axis=0)
    left = jnp.where(me == 0, jnp.zeros_like(left), left)
    right = jnp.where(me == nspace - 1, jnp.zeros_like(right), right)
    bordered = jnp.concatenate([left, joined, right], axis=2)
    bordered = jnp.pad(bordered, ((0, 0), (1, 1), (0, 0), (0, 0)))
    cell_count = nframes * row_count * col_count
    bordered = bordered.transpose(0, 2, 1, 3)
    rows_in = jnp.concatenate(
        [bordered[:, :, row_tap : row_tap + row_count, :] for row_tap in range(3)], axis=3
    )
    rows_in = with_layout_constraint(rows_in, Layout(major_to_minor=(0, 1, 2, 3)))
    columns_in = jnp.concatenate(
        [rows_in[:, col_tap : col_tap + col_count] for col_tap in range(3)], axis=3
    )
    columns_in = with_layout_constraint(columns_in, Layout(major_to_minor=(0, 1, 2, 3)))
    tap_width = columns_in.shape[3]
    nchan = lax.axis_size("chan")
    nx = nchan // 4
    flat_kernel = kernel.transpose(0, 2, 1, 3, 4).reshape(3, tap_width, kernel.shape[4])
    running = jnp.zeros((bias.shape[0] * nchan, cell_count), jnp.float32)
    plane = row_count * col_count
    flat_in = columns_in.reshape(columns_in.shape[0] * plane, tap_width)
    for depth in range(3):
        tap_weight = flat_kernel[depth]
        window = flat_in[depth * plane : depth * plane + cell_count]
        running = running + lax.dot_general(
            tap_weight, window, (((0,), (1,)), ((), ())), preferred_element_type=jnp.float32
        )
    summed = scatter_chan(running.reshape(nx, 2, 2, local_ch, cell_count))
    result = summed.T + bias
    result = result.astype(jnp.bfloat16).reshape(nframes, col_count, row_count, -1)
    return result.transpose(0, 2, 1, 3)


def solution(mesh):
    placed = (
        P(None, None, "space", "chan"),
        P(None, None, "space", "chan"),
        P("chan"),
        P("chan"),
        P(None, None, None, "chan", None),
        P("chan"),
    )
    return jax.shard_map(
        local, mesh=mesh, in_specs=placed, out_specs=P(None, None, "space", "chan"), check_vma=False
    )
```

```python
import functools

import jax
import jax.numpy as jnp
from jax import lax
from jax.experimental import pallas as pl
from jax.experimental.pallas import tpu as pltpu
from jax.experimental.layout import Layout, with_layout_constraint
from jax.sharding import PartitionSpec as P

CH = 512
GROUPS = 32
MESH = pl.DeviceIdType.MESH

epsilon = 1e-06


def gather_kernel(n, x_ref, cache_ref, frames_ref, o_ref, left_ref, right_ref,
                  buf, left_buf, right_buf, send_sem, recv_sem, edge_send, edge_recv):
    me = lax.axis_index("space")
    ch = lax.axis_index("chan")
    right = lax.rem(me + 1, n)
    left = lax.rem(me + n - 1, n)
    barrier = pltpu.get_barrier_semaphore()

    def signal(k, carry):
        peer = lax.rem(me + k, n)
        pl.semaphore_signal(barrier, 1, device_id=(peer, ch), device_id_type=MESH)
        return carry

    lax.fori_loop(1, n, signal, 0)
    pl.semaphore_wait(barrier, n - 1)

    ncache = cache_ref.shape[0]
    last = cache_ref.shape[1] - 1
    edges = []
    for k, (src, lo_row) in enumerate(((cache_ref, 0), (frames_ref, ncache))):
        rows = pl.ds(lo_row, src.shape[0])
        edges.append(pltpu.make_async_remote_copy(
            src_ref=src.at[:, last], dst_ref=left_buf.at[rows], send_sem=edge_send.at[k],
            recv_sem=edge_recv.at[k], device_id=(right, ch), device_id_type=MESH))
        edges.append(pltpu.make_async_remote_copy(
            src_ref=src.at[:, 0], dst_ref=right_buf.at[rows], send_sem=edge_send.at[2 + k],
            recv_sem=edge_recv.at[2 + k], device_id=(left, ch), device_id_type=MESH))
    for cp in edges:
        cp.start()

    def copy_to(peer):
        return pltpu.make_async_remote_copy(
            src_ref=x_ref,
            dst_ref=buf.at[me],
            send_sem=send_sem.at[peer],
            recv_sem=recv_sem.at[me],
            device_id=(peer, ch),
            device_id_type=MESH,
        )

    def copy_from(peer):
        return pltpu.make_async_remote_copy(
            src_ref=x_ref,
            dst_ref=buf.at[peer],
            send_sem=send_sem.at[peer],
            recv_sem=recv_sem.at[peer],
            device_id=(peer, ch),
            device_id_type=MESH,
        )

    def start(k, carry):
        copy_to(lax.rem(me + k, n)).start()
        return carry

    lax.fori_loop(1, n, start, 0)

    def finish(k, carry):
        peer = lax.rem(me + k, n)
        copy_to(peer).wait_send()
        copy_from(peer).wait_recv()
        return carry

    lax.fori_loop(1, n, finish, 0)
    buf[me] = x_ref[...]
    o_ref[...] = buf[...]
    for cp in edges:
        cp.wait()
    left_ref[...] = left_buf[...]
    right_ref[...] = right_buf[...]


def gather_space(tile, cache_t, frames_t):
    n = lax.axis_size("space")
    vmem = pl.BlockSpec(memory_space=pltpu.VMEM)
    hbm = pl.BlockSpec(memory_space=pl.ANY)
    edge = (cache_t.shape[0] + frames_t.shape[0],) + cache_t.shape[2:]
    return pl.pallas_call(
        functools.partial(gather_kernel, n),
        out_shape=(
            jax.ShapeDtypeStruct((n,) + tile.shape, tile.dtype),
            jax.ShapeDtypeStruct(edge, cache_t.dtype),
            jax.ShapeDtypeStruct(edge, cache_t.dtype),
        ),
        in_specs=[vmem, hbm, hbm],
        out_specs=(vmem, vmem, vmem),
        scratch_shapes=[
            pltpu.VMEM((n,) + tile.shape, tile.dtype),
            pltpu.VMEM(edge, cache_t.dtype),
            pltpu.VMEM(edge, cache_t.dtype),
            pltpu.SemaphoreType.DMA((n,)),
            pltpu.SemaphoreType.DMA((n,)),
            pltpu.SemaphoreType.DMA((4,)),
            pltpu.SemaphoreType.DMA((4,)),
        ],
        compiler_params=pltpu.CompilerParams(collective_id=0, has_side_effects=True),
    )(tile, cache_t, frames_t)


def scatter_kernel(widths, x_ref, o_ref, recv1, acc1, own, recv2, acc2, recv3,
                   sem1s, sem1r, sem2s, sem2r, sem3s, sem3r):
    sp = lax.axis_index("space")
    c = lax.axis_index("chan")
    core = c % 2
    yh = (c // 2) % 2
    xx = c // 4
    nx, nyh = x_ref.shape[0], x_ref.shape[1]
    nchunk = len(widths)
    starts = [sum(widths[:q]) for q in range(nchunk)]
    f32, bf16 = jnp.float32, jnp.bfloat16

    def dev(x_, yh_, core_):
        return (sp, x_ * 4 + yh_ * 2 + core_)

    peers = [dev(xx, yh, 1 - core)]
    peers += [dev(lax.rem(xx + k, nx), yh, core) for k in range(1, nx)]
    peers += [dev(xx, 1 - yh, core)]
    barrier = pltpu.get_barrier_semaphore()
    for p in peers:
        pl.semaphore_signal(barrier, 1, device_id=p, device_id_type=MESH)
    pl.semaphore_wait(barrier, len(peers))

    def cols(q):
        return pl.ds(starts[q], widths[q])

    def fit(q):
        return pl.ds(0, widths[q])

    firsts = []
    for q in range(nchunk):
        for i in range(nx):
            for j in range(nyh):
                n = (q * nx + i) * nyh + j
                cp = pltpu.make_async_remote_copy(
                    src_ref=x_ref.at[i, j, 1 - core, :, cols(q)], dst_ref=recv1.at[q, i, j, :, fit(q)],
                    send_sem=sem1s.at[n], recv_sem=sem1r.at[n],
                    device_id=peers[0], device_id_type=MESH)
                cp.start()
                firsts.append(cp)

    def second(q):
        for cp in firsts[q * nx * nyh : (q + 1) * nx * nyh]:
            cp.wait()
        sends = []
        for k in range(1, nx):
            dest = lax.rem(xx + k, nx)
            for j in range(nyh):
                acc1[q, dest, j, :, fit(q)] = (
                    x_ref[dest, j, core, :, cols(q)] + recv1[q, dest, j, :, fit(q)]
                ).astype(bf16)
            slot = nx - 1 - k
            cp = pltpu.make_async_remote_copy(
                src_ref=acc1.at[q, dest, :, :, fit(q)], dst_ref=recv2.at[q, slot, :, :, fit(q)],
                send_sem=sem2s.at[q * (nx - 1) + k - 1], recv_sem=sem2r.at[q * (nx - 1) + slot],
                device_id=peers[k], device_id_type=MESH)
            cp.start()
            sends.append(cp)
        for j in range(nyh):
            own[q, j, :, fit(q)] = x_ref[xx, j, core, :, cols(q)] + recv1[q, xx, j, :, fit(q)]
        return sends

    def third(q):
        for slot in range(nx - 1):
            pltpu.make_async_remote_copy(
                src_ref=acc1.at[q, xx, :, :, fit(q)], dst_ref=recv2.at[q, slot, :, :, fit(q)],
                send_sem=sem2s.at[q * (nx - 1) + slot], recv_sem=sem2r.at[q * (nx - 1) + slot],
                device_id=peers[0], device_id_type=MESH).wait_recv()
        other = 1 - yh
        total = own[q, other, :, fit(q)]
        for slot in range(nx - 1):
            total = total + recv2[q, slot, other, :, fit(q)].astype(f32)
        acc2[q, :, fit(q)] = total.astype(bf16)
        cp = pltpu.make_async_remote_copy(
            src_ref=acc2.at[q, :, fit(q)], dst_ref=recv3.at[q, :, fit(q)], send_sem=sem3s.at[q],
            recv_sem=sem3r.at[q], device_id=peers[nx], device_id_type=MESH)
        cp.start()
        total = own[q, yh, :, fit(q)]
        for slot in range(nx - 1):
            total = total + recv2[q, slot, yh, :, fit(q)].astype(f32)
        own[q, yh, :, fit(q)] = total
        return cp

    seconds, lasts = [], []
    for q in range(nchunk):
        seconds.append(second(q))
        if q >= 1:
            lasts.append(third(q - 1))
    lasts.append(third(nchunk - 1))
    for sends in seconds:
        for cp in sends:
            cp.wait_send()
    for q, cp in enumerate(lasts):
        cp.wait()
        o_ref[:, cols(q)] = own[q, yh, :, fit(q)] + recv3[q, :, fit(q)].astype(f32)


def scatter_chan(parts, widths=(384, 1152, 384)):
    nx, nyh, ncore, rows, cells = parts.shape
    nchunk, width = len(widths), max(widths)
    assert sum(widths) == cells
    f32, bf16 = jnp.float32, jnp.bfloat16
    return pl.pallas_call(
        functools.partial(scatter_kernel, widths),
        out_shape=jax.ShapeDtypeStruct((rows, cells), f32),
        in_specs=[pl.BlockSpec(memory_space=pltpu.VMEM)],
        out_specs=pl.BlockSpec(memory_space=pltpu.VMEM),
        scratch_shapes=[
            pltpu.VMEM((nchunk, nx, nyh, rows, width), f32),
            pltpu.VMEM((nchunk, nx, nyh, rows, width), bf16),
            pltpu.VMEM((nchunk, nyh, rows, width), f32),
            pltpu.VMEM((nchunk, nx - 1, nyh, rows, width), bf16),
            pltpu.VMEM((nchunk, rows, width), bf16),
            pltpu.VMEM((nchunk, rows, width), bf16),
            pltpu.SemaphoreType.DMA((nchunk * nx * nyh,)),
            pltpu.SemaphoreType.DMA((nchunk * nx * nyh,)),
            pltpu.SemaphoreType.DMA((nchunk * (nx - 1),)),
            pltpu.SemaphoreType.DMA((nchunk * (nx - 1),)),
            pltpu.SemaphoreType.DMA((nchunk,)),
            pltpu.SemaphoreType.DMA((nchunk,)),
        ],
        compiler_params=pltpu.CompilerParams(
            collective_id=1, has_side_effects=True, vmem_limit_bytes=48 * 1024 * 1024),
    )(parts)


def local(frames, cache, gamma, beta, kernel, bias):
    nframes, row_count, col_count, local_ch = frames.shape
    ncache = cache.shape[0]
    group_size = CH // GROUPS
    local_groups = local_ch // group_size
    nspace = lax.axis_size("space")
    me = lax.axis_index("space")
    local_members = float(nframes * row_count * col_count * group_size)


    values = frames.astype(jnp.float32).reshape(
        nframes, row_count, col_count, local_groups, group_size
    )
    local_mean = jnp.sum(values, axis=(0, 1, 2, 4)) / local_members
    local_dev = values - local_mean[:, None]
    local_m2 = jnp.sum(local_dev * local_dev, axis=(0, 1, 2, 4))
    tile = jnp.zeros((8, 128), jnp.float32)
    tile = tile.at[0, :local_groups].set(local_mean).at[1, :local_groups].set(local_m2)
    gathered, before, after = gather_space(
        tile, cache.transpose(0, 2, 3, 1), frames.transpose(0, 2, 3, 1)
    )
    before = before.transpose(0, 2, 1)[:, :, None]
    after = after.transpose(0, 2, 1)[:, :, None]
    means = gathered[:, 0, :local_groups]
    m2s = gathered[:, 1, :local_groups]
    group_mean = jnp.mean(means, axis=0)
    spread = jnp.sum(m2s, axis=0) + local_members * jnp.sum(
        (means - group_mean) ** 2, axis=0
    )
    group_var = spread / (local_members * nspace)
    inv = lax.rsqrt(group_var + epsilon)

    def activate(x):
        shape = x.shape
        v = x.astype(jnp.float32).reshape(shape[:-1] + (local_groups, group_size))
        scaled = (v - group_mean[:, None]) * inv[:, None]
        normed = scaled.reshape(shape) * gamma + beta
        return jax.nn.silu(normed).astype(jnp.bfloat16)

    active = activate(frames)
    joined = jnp.concatenate([cache, active], axis=0)
    left = jnp.concatenate([before[:ncache], activate(before[ncache:])], axis=0)
    right = jnp.concatenate([after[:ncache], activate(after[ncache:])], axis=0)
    left = jnp.where(me == 0, jnp.zeros_like(left), left)
    right = jnp.where(me == nspace - 1, jnp.zeros_like(right), right)
    bordered = jnp.concatenate([left, joined, right], axis=2)
    bordered = jnp.pad(bordered, ((0, 0), (1, 1), (0, 0), (0, 0)))
    cell_count = nframes * row_count * col_count
    bordered = bordered.transpose(0, 2, 1, 3)
    rows_in = jnp.concatenate(
        [bordered[:, :, row_tap : row_tap + row_count, :] for row_tap in range(3)], axis=3
    )
    rows_in = with_layout_constraint(rows_in, Layout(major_to_minor=(0, 1, 2, 3)))
    columns_in = jnp.concatenate(
        [rows_in[:, col_tap : col_tap + col_count] for col_tap in range(3)], axis=3
    )
    columns_in = with_layout_constraint(columns_in, Layout(major_to_minor=(0, 1, 2, 3)))
    tap_width = columns_in.shape[3]
    nchan = lax.axis_size("chan")
    nx = nchan // 4
    flat_kernel = kernel.transpose(0, 2, 1, 3, 4).reshape(3, tap_width, kernel.shape[4])
    running = jnp.zeros((bias.shape[0] * nchan, cell_count), jnp.float32)
    plane = row_count * col_count
    flat_in = columns_in.reshape(columns_in.shape[0] * plane, tap_width)
    for depth in range(3):
        tap_weight = flat_kernel[depth]
        window = flat_in[depth * plane : depth * plane + cell_count]
        running = running + lax.dot_general(
            tap_weight, window, (((0,), (1,)), ((), ())), preferred_element_type=jnp.float32
        )
    summed = scatter_chan(running.reshape(nx, 2, 2, local_ch, cell_count))
    result = summed.T + bias
    result = result.astype(jnp.bfloat16).reshape(nframes, col_count, row_count, -1)
    return result.transpose(0, 2, 1, 3)


def solution(mesh):
    placed = (
        P(None, None, "space", "chan"),
        P(None, None, "space", "chan"),
        P("chan"),
        P("chan"),
        P(None, None, None, "chan", None),
        P("chan"),
    )
    return jax.shard_map(
        local, mesh=mesh, in_specs=placed, out_specs=P(None, None, "space", "chan"), check_vma=False
    )
```

```python
import functools

import jax
import jax.numpy as jnp
from jax import lax
from jax.experimental import pallas as pl
from jax.experimental.pallas import tpu as pltpu
from jax.experimental.layout import Layout, with_layout_constraint
from jax.sharding import PartitionSpec as P

CH = 512
GROUPS = 32
MESH = pl.DeviceIdType.MESH

epsilon = 1e-06


def gather_kernel(n, members, x_ref, cache_ref, frames_ref, o_ref, left_ref, right_ref,
                  buf, left_buf, right_buf, send_sem, recv_sem, edge_send, edge_recv):
    me = lax.axis_index("space")
    ch = lax.axis_index("chan")
    right = lax.rem(me + 1, n)
    left = lax.rem(me + n - 1, n)
    barrier = pltpu.get_barrier_semaphore()

    def signal(k, carry):
        peer = lax.rem(me + k, n)
        pl.semaphore_signal(barrier, 1, device_id=(peer, ch), device_id_type=MESH)
        return carry

    lax.fori_loop(1, n, signal, 0)
    pl.semaphore_wait(barrier, n - 1)

    ncache = cache_ref.shape[0]
    last = cache_ref.shape[1] - 1
    edges = []
    for k, (src, lo_row) in enumerate(((cache_ref, 0), (frames_ref, ncache))):
        rows = pl.ds(lo_row, src.shape[0])
        edges.append(pltpu.make_async_remote_copy(
            src_ref=src.at[:, last], dst_ref=left_buf.at[rows], send_sem=edge_send.at[k],
            recv_sem=edge_recv.at[k], device_id=(right, ch), device_id_type=MESH))
        edges.append(pltpu.make_async_remote_copy(
            src_ref=src.at[:, 0], dst_ref=right_buf.at[rows], send_sem=edge_send.at[2 + k],
            recv_sem=edge_recv.at[2 + k], device_id=(left, ch), device_id_type=MESH))
    for cp in edges:
        cp.start()

    def copy_to(peer):
        return pltpu.make_async_remote_copy(
            src_ref=x_ref,
            dst_ref=buf.at[me],
            send_sem=send_sem.at[peer],
            recv_sem=recv_sem.at[me],
            device_id=(peer, ch),
            device_id_type=MESH,
        )

    def copy_from(peer):
        return pltpu.make_async_remote_copy(
            src_ref=x_ref,
            dst_ref=buf.at[peer],
            send_sem=send_sem.at[peer],
            recv_sem=recv_sem.at[peer],
            device_id=(peer, ch),
            device_id_type=MESH,
        )

    def start(k, carry):
        copy_to(lax.rem(me + k, n)).start()
        return carry

    lax.fori_loop(1, n, start, 0)

    def finish(k, carry):
        peer = lax.rem(me + k, n)
        copy_to(peer).wait_send()
        copy_from(peer).wait_recv()
        return carry

    lax.fori_loop(1, n, finish, 0)
    buf[me] = x_ref[...]
    gathered = buf[...]
    means = gathered[:, 0, :]
    group_mean = jnp.sum(means, axis=0, keepdims=True) / n
    spread = jnp.sum(gathered[:, 1, :], axis=0, keepdims=True) + members * jnp.sum(
        (means - group_mean) ** 2, axis=0, keepdims=True
    )
    inv = lax.rsqrt(spread / (members * n) + epsilon)
    o_ref[...] = jnp.concatenate([group_mean, inv, jnp.zeros((6,) + inv.shape[1:], inv.dtype)], axis=0)
    for cp in edges:
        cp.wait()
    for t in range(left_ref.shape[0]):
        left_ref[t] = left_buf[t].astype(jnp.float32).T.astype(left_ref.dtype)
        right_ref[t] = right_buf[t].astype(jnp.float32).T.astype(right_ref.dtype)


def gather_space(tile, cache_t, frames_t, members):
    n = lax.axis_size("space")
    vmem = pl.BlockSpec(memory_space=pltpu.VMEM)
    hbm = pl.BlockSpec(memory_space=pl.ANY)
    edge = (cache_t.shape[0] + frames_t.shape[0],) + cache_t.shape[2:]
    edge_t = edge[:1] + edge[:0:-1]
    return pl.pallas_call(
        functools.partial(gather_kernel, n, members),
        out_shape=(
            jax.ShapeDtypeStruct(tile.shape, tile.dtype),
            jax.ShapeDtypeStruct(edge_t, cache_t.dtype),
            jax.ShapeDtypeStruct(edge_t, cache_t.dtype),
        ),
        in_specs=[vmem, hbm, hbm],
        out_specs=(vmem, vmem, vmem),
        scratch_shapes=[
            pltpu.VMEM((n,) + tile.shape, tile.dtype),
            pltpu.VMEM(edge, cache_t.dtype),
            pltpu.VMEM(edge, cache_t.dtype),
            pltpu.SemaphoreType.DMA((n,)),
            pltpu.SemaphoreType.DMA((n,)),
            pltpu.SemaphoreType.DMA((4,)),
            pltpu.SemaphoreType.DMA((4,)),
        ],
        compiler_params=pltpu.CompilerParams(collective_id=0, has_side_effects=True),
    )(tile, cache_t, frames_t)


def scatter_kernel(widths, x_ref, o_ref, recv1, acc1, own, recv2, acc2, recv3,
                   sem1s, sem1r, sem2s, sem2r, sem3s, sem3r):
    sp = lax.axis_index("space")
    c = lax.axis_index("chan")
    core = c % 2
    yh = (c // 2) % 2
    xx = c // 4
    nx, nyh = x_ref.shape[0], x_ref.shape[1]
    nchunk = len(widths)
    starts = [sum(widths[:q]) for q in range(nchunk)]
    f32, bf16 = jnp.float32, jnp.bfloat16

    def dev(x_, yh_, core_):
        return (sp, x_ * 4 + yh_ * 2 + core_)

    peers = [dev(xx, yh, 1 - core)]
    peers += [dev(lax.rem(xx + k, nx), yh, core) for k in range(1, nx)]
    peers += [dev(xx, 1 - yh, core)]
    barrier = pltpu.get_barrier_semaphore()
    for p in peers:
        pl.semaphore_signal(barrier, 1, device_id=p, device_id_type=MESH)
    pl.semaphore_wait(barrier, len(peers))

    def cols(q):
        return pl.ds(starts[q], widths[q])

    def fit(q):
        return pl.ds(0, widths[q])

    firsts = []
    for q in range(nchunk):
        for i in range(nx):
            for j in range(nyh):
                n = (q * nx + i) * nyh + j
                cp = pltpu.make_async_remote_copy(
                    src_ref=x_ref.at[i, j, 1 - core, :, cols(q)], dst_ref=recv1.at[q, i, j, :, fit(q)],
                    send_sem=sem1s.at[n], recv_sem=sem1r.at[n],
                    device_id=peers[0], device_id_type=MESH)
                cp.start()
                firsts.append(cp)

    def second(q):
        for cp in firsts[q * nx * nyh : (q + 1) * nx * nyh]:
            cp.wait()
        sends = []
        for k in range(1, nx):
            dest = lax.rem(xx + k, nx)
            for j in range(nyh):
                acc1[q, dest, j, :, fit(q)] = (
                    x_ref[dest, j, core, :, cols(q)] + recv1[q, dest, j, :, fit(q)]
                ).astype(bf16)
            slot = nx - 1 - k
            cp = pltpu.make_async_remote_copy(
                src_ref=acc1.at[q, dest, :, :, fit(q)], dst_ref=recv2.at[q, slot, :, :, fit(q)],
                send_sem=sem2s.at[q * (nx - 1) + k - 1], recv_sem=sem2r.at[q * (nx - 1) + slot],
                device_id=peers[k], device_id_type=MESH)
            cp.start()
            sends.append(cp)
        for j in range(nyh):
            own[q, j, :, fit(q)] = x_ref[xx, j, core, :, cols(q)] + recv1[q, xx, j, :, fit(q)]
        return sends

    def third(q):
        for slot in range(nx - 1):
            pltpu.make_async_remote_copy(
                src_ref=acc1.at[q, xx, :, :, fit(q)], dst_ref=recv2.at[q, slot, :, :, fit(q)],
                send_sem=sem2s.at[q * (nx - 1) + slot], recv_sem=sem2r.at[q * (nx - 1) + slot],
                device_id=peers[0], device_id_type=MESH).wait_recv()
        other = 1 - yh
        total = own[q, other, :, fit(q)]
        for slot in range(nx - 1):
            total = total + recv2[q, slot, other, :, fit(q)].astype(f32)
        acc2[q, :, fit(q)] = total.astype(bf16)
        cp = pltpu.make_async_remote_copy(
            src_ref=acc2.at[q, :, fit(q)], dst_ref=recv3.at[q, :, fit(q)], send_sem=sem3s.at[q],
            recv_sem=sem3r.at[q], device_id=peers[nx], device_id_type=MESH)
        cp.start()
        total = own[q, yh, :, fit(q)]
        for slot in range(nx - 1):
            total = total + recv2[q, slot, yh, :, fit(q)].astype(f32)
        own[q, yh, :, fit(q)] = total
        return cp

    seconds, lasts = [], []
    for q in range(nchunk):
        seconds.append(second(q))
        if q >= 1:
            lasts.append(third(q - 1))
    lasts.append(third(nchunk - 1))
    for sends in seconds:
        for cp in sends:
            cp.wait_send()
    for q, cp in enumerate(lasts):
        cp.wait()
        o_ref[:, cols(q)] = own[q, yh, :, fit(q)] + recv3[q, :, fit(q)].astype(f32)


def scatter_chan(parts, widths=(384, 1152, 384)):
    nx, nyh, ncore, rows, cells = parts.shape
    nchunk, width = len(widths), max(widths)
    assert sum(widths) == cells
    f32, bf16 = jnp.float32, jnp.bfloat16
    return pl.pallas_call(
        functools.partial(scatter_kernel, widths),
        out_shape=jax.ShapeDtypeStruct((rows, cells), f32),
        in_specs=[pl.BlockSpec(memory_space=pltpu.VMEM)],
        out_specs=pl.BlockSpec(memory_space=pltpu.VMEM),
        scratch_shapes=[
            pltpu.VMEM((nchunk, nx, nyh, rows, width), f32),
            pltpu.VMEM((nchunk, nx, nyh, rows, width), bf16),
            pltpu.VMEM((nchunk, nyh, rows, width), f32),
            pltpu.VMEM((nchunk, nx - 1, nyh, rows, width), bf16),
            pltpu.VMEM((nchunk, rows, width), bf16),
            pltpu.VMEM((nchunk, rows, width), bf16),
            pltpu.SemaphoreType.DMA((nchunk * nx * nyh,)),
            pltpu.SemaphoreType.DMA((nchunk * nx * nyh,)),
            pltpu.SemaphoreType.DMA((nchunk * (nx - 1),)),
            pltpu.SemaphoreType.DMA((nchunk * (nx - 1),)),
            pltpu.SemaphoreType.DMA((nchunk,)),
            pltpu.SemaphoreType.DMA((nchunk,)),
        ],
        compiler_params=pltpu.CompilerParams(
            collective_id=1, has_side_effects=True, vmem_limit_bytes=48 * 1024 * 1024),
    )(parts)


def local(frames, cache, gamma, beta, kernel, bias):
    nframes, row_count, col_count, local_ch = frames.shape
    ncache = cache.shape[0]
    group_size = CH // GROUPS
    local_groups = local_ch // group_size
    nspace = lax.axis_size("space")
    me = lax.axis_index("space")
    local_members = float(nframes * row_count * col_count * group_size)


    values = frames.astype(jnp.float32).reshape(
        nframes, row_count, col_count, local_groups, group_size
    )
    local_mean = jnp.sum(values, axis=(0, 1, 2, 4)) / local_members
    local_dev = values - local_mean[:, None]
    local_m2 = jnp.sum(local_dev * local_dev, axis=(0, 1, 2, 4))
    tile = jnp.zeros((8, 128), jnp.float32)
    tile = tile.at[0, :local_groups].set(local_mean).at[1, :local_groups].set(local_m2)
    combined, before, after = gather_space(
        tile, cache.transpose(0, 2, 3, 1), frames.transpose(0, 2, 3, 1), local_members
    )
    before = before[:, :, None]
    after = after[:, :, None]
    group_mean = combined[0, :local_groups]
    inv = combined[1, :local_groups]

    def activate(x):
        shape = x.shape
        v = x.astype(jnp.float32).reshape(shape[:-1] + (local_groups, group_size))
        scaled = (v - group_mean[:, None]) * inv[:, None]
        normed = scaled.reshape(shape) * gamma + beta
        return jax.nn.silu(normed).astype(jnp.bfloat16)

    active = activate(frames)
    joined = jnp.concatenate([cache, active], axis=0)
    left = jnp.concatenate([before[:ncache], activate(before[ncache:])], axis=0)
    right = jnp.concatenate([after[:ncache], activate(after[ncache:])], axis=0)
    left = jnp.where(me == 0, jnp.zeros_like(left), left)
    right = jnp.where(me == nspace - 1, jnp.zeros_like(right), right)
    bordered = jnp.concatenate([left, joined, right], axis=2)
    bordered = jnp.pad(bordered, ((0, 0), (1, 1), (0, 0), (0, 0)))
    cell_count = nframes * row_count * col_count
    bordered = bordered.transpose(0, 2, 1, 3)
    rows_in = jnp.concatenate(
        [bordered[:, :, row_tap : row_tap + row_count, :] for row_tap in range(3)], axis=3
    )
    rows_in = with_layout_constraint(rows_in, Layout(major_to_minor=(0, 1, 2, 3)))
    columns_in = jnp.concatenate(
        [rows_in[:, col_tap : col_tap + col_count] for col_tap in range(3)], axis=3
    )
    columns_in = with_layout_constraint(columns_in, Layout(major_to_minor=(0, 1, 2, 3)))
    tap_width = columns_in.shape[3]
    nchan = lax.axis_size("chan")
    nx = nchan // 4
    flat_kernel = kernel.transpose(0, 2, 1, 3, 4).reshape(3, tap_width, kernel.shape[4])
    running = jnp.zeros((bias.shape[0] * nchan, cell_count), jnp.float32)
    plane = row_count * col_count
    flat_in = columns_in.reshape(columns_in.shape[0] * plane, tap_width)
    for depth in range(3):
        tap_weight = flat_kernel[depth]
        window = flat_in[depth * plane : depth * plane + cell_count]
        running = running + lax.dot_general(
            tap_weight, window, (((0,), (1,)), ((), ())), preferred_element_type=jnp.float32
        )
    summed = scatter_chan(running.reshape(nx, 2, 2, local_ch, cell_count))
    result = summed.T + bias
    result = result.astype(jnp.bfloat16).reshape(nframes, col_count, row_count, -1)
    return result.transpose(0, 2, 1, 3)


def solution(mesh):
    placed = (
        P(None, None, "space", "chan"),
        P(None, None, "space", "chan"),
        P("chan"),
        P("chan"),
        P(None, None, None, "chan", None),
        P("chan"),
    )
    return jax.shard_map(
        local, mesh=mesh, in_specs=placed, out_specs=P(None, None, "space", "chan"), check_vma=False
    )
```

```python
import functools

import jax
import jax.numpy as jnp
from jax import lax
from jax.experimental import pallas as pl
from jax.experimental.pallas import tpu as pltpu
from jax.experimental.layout import Layout, with_layout_constraint
from jax.sharding import PartitionSpec as P

CH = 512
GROUPS = 32
MESH = pl.DeviceIdType.MESH

epsilon = 1e-06


def gather_kernel(n, x_ref, cache_ref, frames_ref, o_ref, left_ref, right_ref,
                  buf, left_buf, right_buf, send_sem, recv_sem, edge_send, edge_recv):
    me = lax.axis_index("space")
    ch = lax.axis_index("chan")
    right = lax.rem(me + 1, n)
    left = lax.rem(me + n - 1, n)
    barrier = pltpu.get_barrier_semaphore()

    def signal(k, carry):
        peer = lax.rem(me + k, n)
        pl.semaphore_signal(barrier, 1, device_id=(peer, ch), device_id_type=MESH)
        return carry

    lax.fori_loop(1, n, signal, 0)
    pl.semaphore_wait(barrier, n - 1)

    ncache = cache_ref.shape[0]
    last = cache_ref.shape[1] - 1
    edges = []
    for k, (src, lo_row) in enumerate(((cache_ref, 0), (frames_ref, ncache))):
        rows = pl.ds(lo_row, src.shape[0])
        edges.append(pltpu.make_async_remote_copy(
            src_ref=src.at[:, last], dst_ref=left_buf.at[rows], send_sem=edge_send.at[k],
            recv_sem=edge_recv.at[k], device_id=(right, ch), device_id_type=MESH))
        edges.append(pltpu.make_async_remote_copy(
            src_ref=src.at[:, 0], dst_ref=right_buf.at[rows], send_sem=edge_send.at[2 + k],
            recv_sem=edge_recv.at[2 + k], device_id=(left, ch), device_id_type=MESH))
    for cp in edges:
        cp.start()

    def copy_to(peer):
        return pltpu.make_async_remote_copy(
            src_ref=x_ref,
            dst_ref=buf.at[me],
            send_sem=send_sem.at[peer],
            recv_sem=recv_sem.at[me],
            device_id=(peer, ch),
            device_id_type=MESH,
        )

    def copy_from(peer):
        return pltpu.make_async_remote_copy(
            src_ref=x_ref,
            dst_ref=buf.at[peer],
            send_sem=send_sem.at[peer],
            recv_sem=recv_sem.at[peer],
            device_id=(peer, ch),
            device_id_type=MESH,
        )

    def start(k, carry):
        copy_to(lax.rem(me + k, n)).start()
        return carry

    lax.fori_loop(1, n, start, 0)

    def finish(k, carry):
        peer = lax.rem(me + k, n)
        copy_to(peer).wait_send()
        copy_from(peer).wait_recv()
        return carry

    lax.fori_loop(1, n, finish, 0)
    buf[me] = x_ref[...]
    o_ref[...] = buf[...]
    for cp in edges:
        cp.wait()
    left_ref[...] = left_buf[...]
    right_ref[...] = right_buf[...]


def gather_space(tile, cache_t, frames_t):
    n = lax.axis_size("space")
    vmem = pl.BlockSpec(memory_space=pltpu.VMEM)
    hbm = pl.BlockSpec(memory_space=pl.ANY)
    edge = (cache_t.shape[0] + frames_t.shape[0],) + cache_t.shape[2:]
    return pl.pallas_call(
        functools.partial(gather_kernel, n),
        out_shape=(
            jax.ShapeDtypeStruct((n,) + tile.shape, tile.dtype),
            jax.ShapeDtypeStruct(edge, cache_t.dtype),
            jax.ShapeDtypeStruct(edge, cache_t.dtype),
        ),
        in_specs=[vmem, hbm, hbm],
        out_specs=(vmem, vmem, vmem),
        scratch_shapes=[
            pltpu.VMEM((n,) + tile.shape, tile.dtype),
            pltpu.VMEM(edge, cache_t.dtype),
            pltpu.VMEM(edge, cache_t.dtype),
            pltpu.SemaphoreType.DMA((n,)),
            pltpu.SemaphoreType.DMA((n,)),
            pltpu.SemaphoreType.DMA((4,)),
            pltpu.SemaphoreType.DMA((4,)),
        ],
        compiler_params=pltpu.CompilerParams(collective_id=0, has_side_effects=True),
    )(tile, cache_t, frames_t)


def scatter_kernel(widths, x_ref, bias_ref, o_ref, recv1, acc1, own, recv2, acc2, recv3,
                   sem1s, sem1r, sem2s, sem2r, sem3s, sem3r):
    sp = lax.axis_index("space")
    c = lax.axis_index("chan")
    core = c % 2
    yh = (c // 2) % 2
    xx = c // 4
    nx, nyh = x_ref.shape[0], x_ref.shape[1]
    nchunk = len(widths)
    starts = [sum(widths[:q]) for q in range(nchunk)]
    f32, bf16 = jnp.float32, jnp.bfloat16

    def dev(x_, yh_, core_):
        return (sp, x_ * 4 + yh_ * 2 + core_)

    peers = [dev(xx, yh, 1 - core)]
    peers += [dev(lax.rem(xx + k, nx), yh, core) for k in range(1, nx)]
    peers += [dev(xx, 1 - yh, core)]
    barrier = pltpu.get_barrier_semaphore()
    for p in peers:
        pl.semaphore_signal(barrier, 1, device_id=p, device_id_type=MESH)
    pl.semaphore_wait(barrier, len(peers))

    def cols(q):
        return pl.ds(starts[q], widths[q])

    def fit(q):
        return pl.ds(0, widths[q])

    firsts = []
    for q in range(nchunk):
        for i in range(nx):
            for j in range(nyh):
                n = (q * nx + i) * nyh + j
                cp = pltpu.make_async_remote_copy(
                    src_ref=x_ref.at[i, j, 1 - core, :, cols(q)], dst_ref=recv1.at[q, i, j, :, fit(q)],
                    send_sem=sem1s.at[n], recv_sem=sem1r.at[n],
                    device_id=peers[0], device_id_type=MESH)
                cp.start()
                firsts.append(cp)

    def second(q):
        for cp in firsts[q * nx * nyh : (q + 1) * nx * nyh]:
            cp.wait()
        sends = []
        for k in range(1, nx):
            dest = lax.rem(xx + k, nx)
            for j in range(nyh):
                acc1[q, dest, j, :, fit(q)] = (
                    x_ref[dest, j, core, :, cols(q)] + recv1[q, dest, j, :, fit(q)]
                ).astype(bf16)
            slot = nx - 1 - k
            cp = pltpu.make_async_remote_copy(
                src_ref=acc1.at[q, dest, :, :, fit(q)], dst_ref=recv2.at[q, slot, :, :, fit(q)],
                send_sem=sem2s.at[q * (nx - 1) + k - 1], recv_sem=sem2r.at[q * (nx - 1) + slot],
                device_id=peers[k], device_id_type=MESH)
            cp.start()
            sends.append(cp)
        for j in range(nyh):
            own[q, j, :, fit(q)] = x_ref[xx, j, core, :, cols(q)] + recv1[q, xx, j, :, fit(q)]
        return sends

    def third(q):
        for slot in range(nx - 1):
            pltpu.make_async_remote_copy(
                src_ref=acc1.at[q, xx, :, :, fit(q)], dst_ref=recv2.at[q, slot, :, :, fit(q)],
                send_sem=sem2s.at[q * (nx - 1) + slot], recv_sem=sem2r.at[q * (nx - 1) + slot],
                device_id=peers[0], device_id_type=MESH).wait_recv()
        other = 1 - yh
        total = own[q, other, :, fit(q)]
        for slot in range(nx - 1):
            total = total + recv2[q, slot, other, :, fit(q)].astype(f32)
        acc2[q, :, fit(q)] = total.astype(bf16)
        cp = pltpu.make_async_remote_copy(
            src_ref=acc2.at[q, :, fit(q)], dst_ref=recv3.at[q, :, fit(q)], send_sem=sem3s.at[q],
            recv_sem=sem3r.at[q], device_id=peers[nx], device_id_type=MESH)
        cp.start()
        total = own[q, yh, :, fit(q)]
        for slot in range(nx - 1):
            total = total + recv2[q, slot, yh, :, fit(q)].astype(f32)
        own[q, yh, :, fit(q)] = total
        return cp

    seconds, lasts = [], []
    for q in range(nchunk):
        seconds.append(second(q))
        if q >= 1:
            lasts.append(third(q - 1))
    lasts.append(third(nchunk - 1))
    for sends in seconds:
        for cp in sends:
            cp.wait_send()
    for q, cp in enumerate(lasts):
        cp.wait()
        total = own[q, yh, :, fit(q)] + recv3[q, :, fit(q)].astype(f32)
        o_ref[:, cols(q)] = (total + bias_ref[...]).astype(o_ref.dtype)


def scatter_chan(parts, bias, widths=(384, 1152, 384)):
    nx, nyh, ncore, rows, cells = parts.shape
    nchunk, width = len(widths), max(widths)
    assert sum(widths) == cells
    f32, bf16 = jnp.float32, jnp.bfloat16
    return pl.pallas_call(
        functools.partial(scatter_kernel, widths),
        out_shape=jax.ShapeDtypeStruct((rows, cells), bf16),
        in_specs=[pl.BlockSpec(memory_space=pltpu.VMEM)] * 2,
        out_specs=pl.BlockSpec(memory_space=pltpu.VMEM),
        scratch_shapes=[
            pltpu.VMEM((nchunk, nx, nyh, rows, width), f32),
            pltpu.VMEM((nchunk, nx, nyh, rows, width), bf16),
            pltpu.VMEM((nchunk, nyh, rows, width), f32),
            pltpu.VMEM((nchunk, nx - 1, nyh, rows, width), bf16),
            pltpu.VMEM((nchunk, rows, width), bf16),
            pltpu.VMEM((nchunk, rows, width), bf16),
            pltpu.SemaphoreType.DMA((nchunk * nx * nyh,)),
            pltpu.SemaphoreType.DMA((nchunk * nx * nyh,)),
            pltpu.SemaphoreType.DMA((nchunk * (nx - 1),)),
            pltpu.SemaphoreType.DMA((nchunk * (nx - 1),)),
            pltpu.SemaphoreType.DMA((nchunk,)),
            pltpu.SemaphoreType.DMA((nchunk,)),
        ],
        compiler_params=pltpu.CompilerParams(
            collective_id=1, has_side_effects=True, vmem_limit_bytes=48 * 1024 * 1024),
    )(parts, bias)


def local(frames, cache, gamma, beta, kernel, bias):
    nframes, row_count, col_count, local_ch = frames.shape
    ncache = cache.shape[0]
    group_size = CH // GROUPS
    local_groups = local_ch // group_size
    nspace = lax.axis_size("space")
    me = lax.axis_index("space")
    local_members = float(nframes * row_count * col_count * group_size)


    values = frames.astype(jnp.float32).reshape(
        nframes, row_count, col_count, local_groups, group_size
    )
    local_mean = jnp.sum(values, axis=(0, 1, 2, 4)) / local_members
    local_dev = values - local_mean[:, None]
    local_m2 = jnp.sum(local_dev * local_dev, axis=(0, 1, 2, 4))
    tile = jnp.zeros((8, 128), jnp.float32)
    tile = tile.at[0, :local_groups].set(local_mean).at[1, :local_groups].set(local_m2)
    gathered, before, after = gather_space(
        tile, cache.transpose(0, 2, 3, 1), frames.transpose(0, 2, 3, 1)
    )
    before = before.transpose(0, 2, 1)[:, :, None]
    after = after.transpose(0, 2, 1)[:, :, None]
    means = gathered[:, 0, :local_groups]
    m2s = gathered[:, 1, :local_groups]
    group_mean = jnp.mean(means, axis=0)
    spread = jnp.sum(m2s, axis=0) + local_members * jnp.sum(
        (means - group_mean) ** 2, axis=0
    )
    group_var = spread / (local_members * nspace)
    inv = lax.rsqrt(group_var + epsilon)

    def activate(x):
        shape = x.shape
        v = x.astype(jnp.float32).reshape(shape[:-1] + (local_groups, group_size))
        scaled = (v - group_mean[:, None]) * inv[:, None]
        normed = scaled.reshape(shape) * gamma + beta
        return jax.nn.silu(normed).astype(jnp.bfloat16)

    active = activate(frames)
    joined = jnp.concatenate([cache, active], axis=0)
    left = jnp.concatenate([before[:ncache], activate(before[ncache:])], axis=0)
    right = jnp.concatenate([after[:ncache], activate(after[ncache:])], axis=0)
    left = jnp.where(me == 0, jnp.zeros_like(left), left)
    right = jnp.where(me == nspace - 1, jnp.zeros_like(right), right)
    bordered = jnp.concatenate([left, joined, right], axis=2)
    bordered = jnp.pad(bordered, ((0, 0), (1, 1), (0, 0), (0, 0)))
    cell_count = nframes * row_count * col_count
    bordered = bordered.transpose(0, 2, 1, 3)
    rows_in = jnp.concatenate(
        [bordered[:, :, row_tap : row_tap + row_count, :] for row_tap in range(3)], axis=3
    )
    rows_in = with_layout_constraint(rows_in, Layout(major_to_minor=(0, 1, 2, 3)))
    columns_in = jnp.concatenate(
        [rows_in[:, col_tap : col_tap + col_count] for col_tap in range(3)], axis=3
    )
    columns_in = with_layout_constraint(columns_in, Layout(major_to_minor=(0, 1, 2, 3)))
    tap_width = columns_in.shape[3]
    nchan = lax.axis_size("chan")
    nx = nchan // 4
    flat_kernel = kernel.transpose(0, 2, 1, 3, 4).reshape(3, tap_width, kernel.shape[4])
    running = jnp.zeros((bias.shape[0] * nchan, cell_count), jnp.float32)
    plane = row_count * col_count
    flat_in = columns_in.reshape(columns_in.shape[0] * plane, tap_width)
    for depth in range(3):
        tap_weight = flat_kernel[depth]
        window = flat_in[depth * plane : depth * plane + cell_count]
        running = running + lax.dot_general(
            tap_weight, window, (((0,), (1,)), ((), ())), preferred_element_type=jnp.float32
        )
    summed = scatter_chan(running.reshape(nx, 2, 2, local_ch, cell_count), bias[:, None])
    result = summed.T.reshape(nframes, col_count, row_count, -1)
    return result.transpose(0, 2, 1, 3)


def solution(mesh):
    placed = (
        P(None, None, "space", "chan"),
        P(None, None, "space", "chan"),
        P("chan"),
        P("chan"),
        P(None, None, None, "chan", None),
        P("chan"),
    )
    return jax.shard_map(
        local, mesh=mesh, in_specs=placed, out_specs=P(None, None, "space", "chan"), check_vma=False
    )
```

```python
import functools

import jax
import jax.numpy as jnp
from jax import lax
from jax.experimental import pallas as pl
from jax.experimental.pallas import tpu as pltpu
from jax.experimental.layout import Layout, with_layout_constraint
from jax.sharding import PartitionSpec as P

CH = 512
GROUPS = 32
MESH = pl.DeviceIdType.MESH

epsilon = 1e-06


def gather_kernel(n, x_ref, cache_ref, frames_ref, o_ref, left_ref, right_ref,
                  buf, left_buf, right_buf, send_sem, recv_sem, edge_send, edge_recv):
    me = lax.axis_index("space")
    ch = lax.axis_index("chan")
    right = lax.rem(me + 1, n)
    left = lax.rem(me + n - 1, n)
    barrier = pltpu.get_barrier_semaphore()

    def signal(k, carry):
        peer = lax.rem(me + k, n)
        pl.semaphore_signal(barrier, 1, device_id=(peer, ch), device_id_type=MESH)
        return carry

    lax.fori_loop(1, n, signal, 0)
    pl.semaphore_wait(barrier, n - 1)

    ncache = cache_ref.shape[0]
    last = cache_ref.shape[1] - 1
    edges = []
    for k, (src, lo_row) in enumerate(((cache_ref, 0), (frames_ref, ncache))):
        rows = pl.ds(lo_row, src.shape[0])
        edges.append(pltpu.make_async_remote_copy(
            src_ref=src.at[:, last], dst_ref=left_buf.at[rows], send_sem=edge_send.at[k],
            recv_sem=edge_recv.at[k], device_id=(right, ch), device_id_type=MESH))
        edges.append(pltpu.make_async_remote_copy(
            src_ref=src.at[:, 0], dst_ref=right_buf.at[rows], send_sem=edge_send.at[2 + k],
            recv_sem=edge_recv.at[2 + k], device_id=(left, ch), device_id_type=MESH))
    for cp in edges:
        cp.start()

    def copy_to(peer):
        return pltpu.make_async_remote_copy(
            src_ref=x_ref,
            dst_ref=buf.at[me],
            send_sem=send_sem.at[peer],
            recv_sem=recv_sem.at[me],
            device_id=(peer, ch),
            device_id_type=MESH,
        )

    def copy_from(peer):
        return pltpu.make_async_remote_copy(
            src_ref=x_ref,
            dst_ref=buf.at[peer],
            send_sem=send_sem.at[peer],
            recv_sem=recv_sem.at[peer],
            device_id=(peer, ch),
            device_id_type=MESH,
        )

    def start(k, carry):
        copy_to(lax.rem(me + k, n)).start()
        return carry

    lax.fori_loop(1, n, start, 0)

    def finish(k, carry):
        peer = lax.rem(me + k, n)
        copy_to(peer).wait_send()
        copy_from(peer).wait_recv()
        return carry

    lax.fori_loop(1, n, finish, 0)
    buf[me] = x_ref[...]
    o_ref[...] = buf[...]
    for cp in edges:
        cp.wait()
    left_ref[...] = left_buf[...]
    right_ref[...] = right_buf[...]


def gather_space(tile, cache_t, frames_t):
    n = lax.axis_size("space")
    vmem = pl.BlockSpec(memory_space=pltpu.VMEM)
    hbm = pl.BlockSpec(memory_space=pl.ANY)
    edge = (cache_t.shape[0] + frames_t.shape[0],) + cache_t.shape[2:]
    return pl.pallas_call(
        functools.partial(gather_kernel, n),
        out_shape=(
            jax.ShapeDtypeStruct((n,) + tile.shape, tile.dtype),
            jax.ShapeDtypeStruct(edge, cache_t.dtype),
            jax.ShapeDtypeStruct(edge, cache_t.dtype),
        ),
        in_specs=[vmem, hbm, hbm],
        out_specs=(vmem, vmem, vmem),
        scratch_shapes=[
            pltpu.VMEM((n,) + tile.shape, tile.dtype),
            pltpu.VMEM(edge, cache_t.dtype),
            pltpu.VMEM(edge, cache_t.dtype),
            pltpu.SemaphoreType.DMA((n,)),
            pltpu.SemaphoreType.DMA((n,)),
            pltpu.SemaphoreType.DMA((4,)),
            pltpu.SemaphoreType.DMA((4,)),
        ],
        compiler_params=pltpu.CompilerParams(collective_id=0, has_side_effects=True),
    )(tile, cache_t, frames_t)


def scatter_kernel(widths, x_ref, o_ref, recv1, acc1, own, recv2, acc2, recv3,
                   sem1s, sem1r, sem2s, sem2r, sem3s, sem3r):
    sp = lax.axis_index("space")
    c = lax.axis_index("chan")
    core = c % 2
    yh = (c // 2) % 2
    xx = c // 4
    nx, nyh = x_ref.shape[0], x_ref.shape[1]
    nchunk = len(widths)
    starts = [sum(widths[:q]) for q in range(nchunk)]
    f32, bf16 = jnp.float32, jnp.bfloat16

    def dev(x_, yh_, core_):
        return (sp, x_ * 4 + yh_ * 2 + core_)

    peers = [dev(xx, yh, 1 - core)]
    peers += [dev(lax.rem(xx + k, nx), yh, core) for k in range(1, nx)]
    peers += [dev(xx, 1 - yh, core)]
    barrier = pltpu.get_barrier_semaphore()
    for p in peers:
        pl.semaphore_signal(barrier, 1, device_id=p, device_id_type=MESH)
    pl.semaphore_wait(barrier, len(peers))

    def cols(q):
        return pl.ds(starts[q], widths[q])

    def fit(q):
        return pl.ds(0, widths[q])

    firsts = []
    for q in range(nchunk):
        for i in range(nx):
            for j in range(nyh):
                n = (q * nx + i) * nyh + j
                cp = pltpu.make_async_remote_copy(
                    src_ref=x_ref.at[i, j, 1 - core, :, cols(q)], dst_ref=recv1.at[q, i, j, :, fit(q)],
                    send_sem=sem1s.at[n], recv_sem=sem1r.at[n],
                    device_id=peers[0], device_id_type=MESH)
                cp.start()
                firsts.append(cp)

    def second(q):
        for cp in firsts[q * nx * nyh : (q + 1) * nx * nyh]:
            cp.wait()
        sends = []
        for k in range(1, nx):
            dest = lax.rem(xx + k, nx)
            for j in range(nyh):
                acc1[q, dest, j, :, fit(q)] = (
                    x_ref[dest, j, core, :, cols(q)] + recv1[q, dest, j, :, fit(q)]
                ).astype(bf16)
            slot = nx - 1 - k
            cp = pltpu.make_async_remote_copy(
                src_ref=acc1.at[q, dest, :, :, fit(q)], dst_ref=recv2.at[q, slot, :, :, fit(q)],
                send_sem=sem2s.at[q * (nx - 1) + k - 1], recv_sem=sem2r.at[q * (nx - 1) + slot],
                device_id=peers[k], device_id_type=MESH)
            cp.start()
            sends.append(cp)
        for j in range(nyh):
            own[q, j, :, fit(q)] = x_ref[xx, j, core, :, cols(q)] + recv1[q, xx, j, :, fit(q)]
        return sends

    def third(q):
        for slot in range(nx - 1):
            pltpu.make_async_remote_copy(
                src_ref=acc1.at[q, xx, :, :, fit(q)], dst_ref=recv2.at[q, slot, :, :, fit(q)],
                send_sem=sem2s.at[q * (nx - 1) + slot], recv_sem=sem2r.at[q * (nx - 1) + slot],
                device_id=peers[0], device_id_type=MESH).wait_recv()
        other = 1 - yh
        total = own[q, other, :, fit(q)]
        for slot in range(nx - 1):
            total = total + recv2[q, slot, other, :, fit(q)].astype(f32)
        acc2[q, :, fit(q)] = total.astype(bf16)
        cp = pltpu.make_async_remote_copy(
            src_ref=acc2.at[q, :, fit(q)], dst_ref=recv3.at[q, :, fit(q)], send_sem=sem3s.at[q],
            recv_sem=sem3r.at[q], device_id=peers[nx], device_id_type=MESH)
        cp.start()
        total = own[q, yh, :, fit(q)]
        for slot in range(nx - 1):
            total = total + recv2[q, slot, yh, :, fit(q)].astype(f32)
        own[q, yh, :, fit(q)] = total
        return cp

    seconds, lasts = [], []
    for q in range(nchunk):
        seconds.append(second(q))
        if q >= 1:
            lasts.append(third(q - 1))
    lasts.append(third(nchunk - 1))
    for sends in seconds:
        for cp in sends:
            cp.wait_send()
    for q, cp in enumerate(lasts):
        cp.wait()
        o_ref[:, cols(q)] = own[q, yh, :, fit(q)] + recv3[q, :, fit(q)].astype(f32)


def scatter_chan(parts, widths=(384, 1152, 384)):
    nx, nyh, ncore, rows, cells = parts.shape
    nchunk, width = len(widths), max(widths)
    assert sum(widths) == cells
    f32, bf16 = jnp.float32, jnp.bfloat16
    return pl.pallas_call(
        functools.partial(scatter_kernel, widths),
        out_shape=jax.ShapeDtypeStruct((rows, cells), f32),
        in_specs=[pl.BlockSpec(memory_space=pltpu.VMEM)],
        out_specs=pl.BlockSpec(memory_space=pltpu.VMEM),
        scratch_shapes=[
            pltpu.VMEM((nchunk, nx, nyh, rows, width), f32),
            pltpu.VMEM((nchunk, nx, nyh, rows, width), bf16),
            pltpu.VMEM((nchunk, nyh, rows, width), f32),
            pltpu.VMEM((nchunk, nx - 1, nyh, rows, width), bf16),
            pltpu.VMEM((nchunk, rows, width), bf16),
            pltpu.VMEM((nchunk, rows, width), bf16),
            pltpu.SemaphoreType.DMA((nchunk * nx * nyh,)),
            pltpu.SemaphoreType.DMA((nchunk * nx * nyh,)),
            pltpu.SemaphoreType.DMA((nchunk * (nx - 1),)),
            pltpu.SemaphoreType.DMA((nchunk * (nx - 1),)),
            pltpu.SemaphoreType.DMA((nchunk,)),
            pltpu.SemaphoreType.DMA((nchunk,)),
        ],
        compiler_params=pltpu.CompilerParams(
            collective_id=1, has_side_effects=True, vmem_limit_bytes=48 * 1024 * 1024),
    )(parts)


def local(frames, cache, gamma, beta, kernel, bias):
    nframes, row_count, col_count, local_ch = frames.shape
    ncache = cache.shape[0]
    group_size = CH // GROUPS
    local_groups = local_ch // group_size
    nspace = lax.axis_size("space")
    me = lax.axis_index("space")
    local_members = float(nframes * row_count * col_count * group_size)


    values = frames.astype(jnp.float32).reshape(
        nframes, row_count, col_count, local_groups, group_size
    )
    local_mean = jnp.sum(values, axis=(0, 1, 2, 4)) / local_members
    local_dev = values - local_mean[:, None]
    local_m2 = jnp.sum(local_dev * local_dev, axis=(0, 1, 2, 4))
    tile = jnp.zeros((8, 128), jnp.float32)
    tile = tile.at[0, :local_groups].set(local_mean).at[1, :local_groups].set(local_m2)
    gathered, before, after = gather_space(
        tile, cache.transpose(0, 2, 3, 1), frames.transpose(0, 2, 3, 1)
    )
    before = before.transpose(0, 2, 1)[:, :, None]
    after = after.transpose(0, 2, 1)[:, :, None]
    means = gathered[:, 0, :local_groups]
    m2s = gathered[:, 1, :local_groups]
    group_mean = jnp.mean(means, axis=0)
    spread = jnp.sum(m2s, axis=0) + local_members * jnp.sum(
        (means - group_mean) ** 2, axis=0
    )
    group_var = spread / (local_members * nspace)
    inv = lax.rsqrt(group_var + epsilon)

    def activate(x):
        shape = x.shape
        v = x.astype(jnp.float32).reshape(shape[:-1] + (local_groups, group_size))
        scaled = (v - group_mean[:, None]) * inv[:, None]
        normed = scaled.reshape(shape) * gamma + beta
        return jax.nn.silu(normed).astype(jnp.bfloat16)

    active = activate(frames)
    joined = jnp.concatenate([cache, active], axis=0)
    left = jnp.concatenate([before[:ncache], activate(before[ncache:])], axis=0)
    right = jnp.concatenate([after[:ncache], activate(after[ncache:])], axis=0)
    left = jnp.where(me == 0, jnp.zeros_like(left), left)
    right = jnp.where(me == nspace - 1, jnp.zeros_like(right), right)
    bordered = jnp.concatenate([left, joined, right], axis=2)
    bordered = jnp.pad(bordered, ((0, 0), (1, 1), (0, 0), (0, 0)))
    cell_count = nframes * row_count * col_count
    bordered = bordered.transpose(0, 2, 1, 3)
    rows_in = jnp.concatenate(
        [bordered[:, :, row_tap : row_tap + row_count, :] for row_tap in range(3)], axis=3
    )
    rows_in = with_layout_constraint(rows_in, Layout(major_to_minor=(0, 1, 2, 3)))
    columns_in = jnp.concatenate(
        [rows_in[:, col_tap : col_tap + col_count] for col_tap in range(3)], axis=3
    )
    columns_in = with_layout_constraint(columns_in, Layout(major_to_minor=(0, 1, 2, 3)))
    tap_width = columns_in.shape[3]
    nchan = lax.axis_size("chan")
    nx = nchan // 4
    full_kernel = kernel.transpose(0, 2, 1, 3, 4).reshape(3 * tap_width, kernel.shape[4])
    depth_in = jnp.concatenate(
        [columns_in[depth : depth + nframes] for depth in range(3)], axis=3
    )
    depth_in = with_layout_constraint(depth_in, Layout(major_to_minor=(0, 1, 2, 3)))
    window = depth_in.reshape(cell_count, 3 * tap_width)
    running = lax.dot_general(
        full_kernel, window, (((0,), (1,)), ((), ())), preferred_element_type=jnp.float32
    )
    summed = scatter_chan(running.reshape(nx, 2, 2, local_ch, cell_count))
    result = summed.T + bias
    result = result.astype(jnp.bfloat16).reshape(nframes, col_count, row_count, -1)
    return result.transpose(0, 2, 1, 3)


def solution(mesh):
    placed = (
        P(None, None, "space", "chan"),
        P(None, None, "space", "chan"),
        P("chan"),
        P("chan"),
        P(None, None, None, "chan", None),
        P("chan"),
    )
    return jax.shard_map(
        local, mesh=mesh, in_specs=placed, out_specs=P(None, None, "space", "chan"), check_vma=False
    )
```

```python
import functools

import jax
import jax.numpy as jnp
from jax import lax
from jax.experimental import pallas as pl
from jax.experimental.pallas import tpu as pltpu
from jax.experimental.layout import Layout, with_layout_constraint
from jax.sharding import PartitionSpec as P

CH = 512
GROUPS = 32
MESH = pl.DeviceIdType.MESH

epsilon = 1e-06


def gather_kernel(n, x_ref, cache_ref, frames_ref, o_ref, left_ref, right_ref,
                  buf, left_buf, right_buf, send_sem, recv_sem, edge_send, edge_recv):
    me = lax.axis_index("space")
    ch = lax.axis_index("chan")
    right = lax.rem(me + 1, n)
    left = lax.rem(me + n - 1, n)
    barrier = pltpu.get_barrier_semaphore()

    def signal(k, carry):
        peer = lax.rem(me + k, n)
        pl.semaphore_signal(barrier, 1, device_id=(peer, ch), device_id_type=MESH)
        return carry

    lax.fori_loop(1, n, signal, 0)
    pl.semaphore_wait(barrier, n - 1)

    ncache = cache_ref.shape[0]
    last = cache_ref.shape[1] - 1
    edges = []
    for k, (src, lo_row) in enumerate(((cache_ref, 0), (frames_ref, ncache))):
        rows = pl.ds(lo_row, src.shape[0])
        edges.append(pltpu.make_async_remote_copy(
            src_ref=src.at[:, last], dst_ref=left_buf.at[rows], send_sem=edge_send.at[k],
            recv_sem=edge_recv.at[k], device_id=(right, ch), device_id_type=MESH))
        edges.append(pltpu.make_async_remote_copy(
            src_ref=src.at[:, 0], dst_ref=right_buf.at[rows], send_sem=edge_send.at[2 + k],
            recv_sem=edge_recv.at[2 + k], device_id=(left, ch), device_id_type=MESH))
    for cp in edges:
        cp.start()

    def copy_to(peer):
        return pltpu.make_async_remote_copy(
            src_ref=x_ref,
            dst_ref=buf.at[me],
            send_sem=send_sem.at[peer],
            recv_sem=recv_sem.at[me],
            device_id=(peer, ch),
            device_id_type=MESH,
        )

    def copy_from(peer):
        return pltpu.make_async_remote_copy(
            src_ref=x_ref,
            dst_ref=buf.at[peer],
            send_sem=send_sem.at[peer],
            recv_sem=recv_sem.at[peer],
            device_id=(peer, ch),
            device_id_type=MESH,
        )

    def start(k, carry):
        copy_to(lax.rem(me + k, n)).start()
        return carry

    lax.fori_loop(1, n, start, 0)

    def finish(k, carry):
        peer = lax.rem(me + k, n)
        copy_to(peer).wait_send()
        copy_from(peer).wait_recv()
        return carry

    lax.fori_loop(1, n, finish, 0)
    buf[me] = x_ref[...]
    o_ref[...] = buf[...]
    for cp in edges:
        cp.wait()
    left_ref[...] = left_buf[...]
    right_ref[...] = right_buf[...]


def gather_space(tile, cache_t, frames_t):
    n = lax.axis_size("space")
    vmem = pl.BlockSpec(memory_space=pltpu.VMEM)
    hbm = pl.BlockSpec(memory_space=pl.ANY)
    edge = (cache_t.shape[0] + frames_t.shape[0],) + cache_t.shape[2:]
    return pl.pallas_call(
        functools.partial(gather_kernel, n),
        out_shape=(
            jax.ShapeDtypeStruct((n,) + tile.shape, tile.dtype),
            jax.ShapeDtypeStruct(edge, cache_t.dtype),
            jax.ShapeDtypeStruct(edge, cache_t.dtype),
        ),
        in_specs=[vmem, hbm, hbm],
        out_specs=(vmem, vmem, vmem),
        scratch_shapes=[
            pltpu.VMEM((n,) + tile.shape, tile.dtype),
            pltpu.VMEM(edge, cache_t.dtype),
            pltpu.VMEM(edge, cache_t.dtype),
            pltpu.SemaphoreType.DMA((n,)),
            pltpu.SemaphoreType.DMA((n,)),
            pltpu.SemaphoreType.DMA((4,)),
            pltpu.SemaphoreType.DMA((4,)),
        ],
        compiler_params=pltpu.CompilerParams(collective_id=0, has_side_effects=True),
    )(tile, cache_t, frames_t)


def scatter_kernel(widths, x_ref, o_ref, recv1, acc1, own, recv2, acc2, recv3,
                   sem1s, sem1r, sem2s, sem2r, sem3s, sem3r):
    sp = lax.axis_index("space")
    c = lax.axis_index("chan")
    core = c % 2
    yh = (c // 2) % 2
    xx = c // 4
    nx, nyh = x_ref.shape[0], x_ref.shape[1]
    nchunk = len(widths)
    starts = [sum(widths[:q]) for q in range(nchunk)]
    f32, bf16 = jnp.float32, jnp.bfloat16

    def dev(x_, yh_, core_):
        return (sp, x_ * 4 + yh_ * 2 + core_)

    peers = [dev(xx, yh, 1 - core)]
    peers += [dev(lax.rem(xx + k, nx), yh, core) for k in range(1, nx)]
    peers += [dev(xx, 1 - yh, core)]
    barrier = pltpu.get_barrier_semaphore()
    for p in peers:
        pl.semaphore_signal(barrier, 1, device_id=p, device_id_type=MESH)
    pl.semaphore_wait(barrier, len(peers))

    def cols(q):
        return pl.ds(starts[q], widths[q])

    def fit(q):
        return pl.ds(0, widths[q])

    firsts = []
    for q in range(nchunk):
        for i in range(nx):
            for j in range(nyh):
                n = (q * nx + i) * nyh + j
                cp = pltpu.make_async_remote_copy(
                    src_ref=x_ref.at[i, j, 1 - core, :, cols(q)], dst_ref=recv1.at[q, i, j, :, fit(q)],
                    send_sem=sem1s.at[n], recv_sem=sem1r.at[n],
                    device_id=peers[0], device_id_type=MESH)
                cp.start()
                firsts.append(cp)

    def second(q):
        for cp in firsts[q * nx * nyh : (q + 1) * nx * nyh]:
            cp.wait()
        sends = []
        for k in range(1, nx):
            dest = lax.rem(xx + k, nx)
            for j in range(nyh):
                acc1[q, dest, j, :, fit(q)] = (
                    x_ref[dest, j, core, :, cols(q)] + recv1[q, dest, j, :, fit(q)]
                ).astype(bf16)
            slot = nx - 1 - k
            cp = pltpu.make_async_remote_copy(
                src_ref=acc1.at[q, dest, :, :, fit(q)], dst_ref=recv2.at[q, slot, :, :, fit(q)],
                send_sem=sem2s.at[q * (nx - 1) + k - 1], recv_sem=sem2r.at[q * (nx - 1) + slot],
                device_id=peers[k], device_id_type=MESH)
            cp.start()
            sends.append(cp)
        for j in range(nyh):
            own[q, j, :, fit(q)] = x_ref[xx, j, core, :, cols(q)] + recv1[q, xx, j, :, fit(q)]
        return sends

    def third(q):
        for slot in range(nx - 1):
            pltpu.make_async_remote_copy(
                src_ref=acc1.at[q, xx, :, :, fit(q)], dst_ref=recv2.at[q, slot, :, :, fit(q)],
                send_sem=sem2s.at[q * (nx - 1) + slot], recv_sem=sem2r.at[q * (nx - 1) + slot],
                device_id=peers[0], device_id_type=MESH).wait_recv()
        other = 1 - yh
        total = own[q, other, :, fit(q)]
        for slot in range(nx - 1):
            total = total + recv2[q, slot, other, :, fit(q)].astype(f32)
        acc2[q, :, fit(q)] = total.astype(bf16)
        cp = pltpu.make_async_remote_copy(
            src_ref=acc2.at[q, :, fit(q)], dst_ref=recv3.at[q, :, fit(q)], send_sem=sem3s.at[q],
            recv_sem=sem3r.at[q], device_id=peers[nx], device_id_type=MESH)
        cp.start()
        total = own[q, yh, :, fit(q)]
        for slot in range(nx - 1):
            total = total + recv2[q, slot, yh, :, fit(q)].astype(f32)
        own[q, yh, :, fit(q)] = total
        return cp

    seconds, lasts = [], []
    for q in range(nchunk):
        seconds.append(second(q))
        if q >= 1:
            lasts.append(third(q - 1))
    lasts.append(third(nchunk - 1))
    for sends in seconds:
        for cp in sends:
            cp.wait_send()
    for q, cp in enumerate(lasts):
        cp.wait()
        o_ref[:, cols(q)] = own[q, yh, :, fit(q)] + recv3[q, :, fit(q)].astype(f32)


def scatter_chan(parts, widths=(256, 1408, 256)):
    nx, nyh, ncore, rows, cells = parts.shape
    nchunk, width = len(widths), max(widths)
    assert sum(widths) == cells
    f32, bf16 = jnp.float32, jnp.bfloat16
    return pl.pallas_call(
        functools.partial(scatter_kernel, widths),
        out_shape=jax.ShapeDtypeStruct((rows, cells), f32),
        in_specs=[pl.BlockSpec(memory_space=pltpu.VMEM)],
        out_specs=pl.BlockSpec(memory_space=pltpu.VMEM),
        scratch_shapes=[
            pltpu.VMEM((nchunk, nx, nyh, rows, width), f32),
            pltpu.VMEM((nchunk, nx, nyh, rows, width), bf16),
            pltpu.VMEM((nchunk, nyh, rows, width), f32),
            pltpu.VMEM((nchunk, nx - 1, nyh, rows, width), bf16),
            pltpu.VMEM((nchunk, rows, width), bf16),
            pltpu.VMEM((nchunk, rows, width), bf16),
            pltpu.SemaphoreType.DMA((nchunk * nx * nyh,)),
            pltpu.SemaphoreType.DMA((nchunk * nx * nyh,)),
            pltpu.SemaphoreType.DMA((nchunk * (nx - 1),)),
            pltpu.SemaphoreType.DMA((nchunk * (nx - 1),)),
            pltpu.SemaphoreType.DMA((nchunk,)),
            pltpu.SemaphoreType.DMA((nchunk,)),
        ],
        compiler_params=pltpu.CompilerParams(
            collective_id=1, has_side_effects=True, vmem_limit_bytes=48 * 1024 * 1024),
    )(parts)


def local(frames, cache, gamma, beta, kernel, bias):
    nframes, row_count, col_count, local_ch = frames.shape
    ncache = cache.shape[0]
    group_size = CH // GROUPS
    local_groups = local_ch // group_size
    nspace = lax.axis_size("space")
    me = lax.axis_index("space")
    local_members = float(nframes * row_count * col_count * group_size)


    values = frames.astype(jnp.float32).reshape(
        nframes, row_count, col_count, local_groups, group_size
    )
    local_mean = jnp.sum(values, axis=(0, 1, 2, 4)) / local_members
    local_dev = values - local_mean[:, None]
    local_m2 = jnp.sum(local_dev * local_dev, axis=(0, 1, 2, 4))
    tile = jnp.zeros((8, 128), jnp.float32)
    tile = tile.at[0, :local_groups].set(local_mean).at[1, :local_groups].set(local_m2)
    gathered, before, after = gather_space(
        tile, cache.transpose(0, 2, 3, 1), frames.transpose(0, 2, 3, 1)
    )
    before = before.transpose(0, 2, 1)[:, :, None]
    after = after.transpose(0, 2, 1)[:, :, None]
    means = gathered[:, 0, :local_groups]
    m2s = gathered[:, 1, :local_groups]
    group_mean = jnp.mean(means, axis=0)
    spread = jnp.sum(m2s, axis=0) + local_members * jnp.sum(
        (means - group_mean) ** 2, axis=0
    )
    group_var = spread / (local_members * nspace)
    inv = lax.rsqrt(group_var + epsilon)

    def activate(x):
        shape = x.shape
        v = x.astype(jnp.float32).reshape(shape[:-1] + (local_groups, group_size))
        scaled = (v - group_mean[:, None]) * inv[:, None]
        normed = scaled.reshape(shape) * gamma + beta
        return jax.nn.silu(normed).astype(jnp.bfloat16)

    active = activate(frames)
    joined = jnp.concatenate([cache, active], axis=0)
    left = jnp.concatenate([before[:ncache], activate(before[ncache:])], axis=0)
    right = jnp.concatenate([after[:ncache], activate(after[ncache:])], axis=0)
    left = jnp.where(me == 0, jnp.zeros_like(left), left)
    right = jnp.where(me == nspace - 1, jnp.zeros_like(right), right)
    bordered = jnp.concatenate([left, joined, right], axis=2)
    bordered = jnp.pad(bordered, ((0, 0), (1, 1), (0, 0), (0, 0)))
    cell_count = nframes * row_count * col_count
    bordered = bordered.transpose(0, 2, 1, 3)
    rows_in = jnp.concatenate(
        [bordered[:, :, row_tap : row_tap + row_count, :] for row_tap in range(3)], axis=3
    )
    rows_in = with_layout_constraint(rows_in, Layout(major_to_minor=(0, 1, 2, 3)))
    columns_in = jnp.concatenate(
        [rows_in[:, col_tap : col_tap + col_count] for col_tap in range(3)], axis=3
    )
    columns_in = with_layout_constraint(columns_in, Layout(major_to_minor=(0, 1, 2, 3)))
    tap_width = columns_in.shape[3]
    nchan = lax.axis_size("chan")
    nx = nchan // 4
    flat_kernel = kernel.transpose(0, 2, 1, 3, 4).reshape(3, tap_width, kernel.shape[4])
    running = jnp.zeros((bias.shape[0] * nchan, cell_count), jnp.float32)
    plane = row_count * col_count
    flat_in = columns_in.reshape(columns_in.shape[0] * plane, tap_width)
    for depth in range(3):
        tap_weight = flat_kernel[depth]
        window = flat_in[depth * plane : depth * plane + cell_count]
        running = running + lax.dot_general(
            tap_weight, window, (((0,), (1,)), ((), ())), preferred_element_type=jnp.float32
        )
    summed = scatter_chan(running.reshape(nx, 2, 2, local_ch, cell_count))
    result = summed.T + bias
    result = result.astype(jnp.bfloat16).reshape(nframes, col_count, row_count, -1)
    return result.transpose(0, 2, 1, 3)


def solution(mesh):
    placed = (
        P(None, None, "space", "chan"),
        P(None, None, "space", "chan"),
        P("chan"),
        P("chan"),
        P(None, None, None, "chan", None),
        P("chan"),
    )
    return jax.shard_map(
        local, mesh=mesh, in_specs=placed, out_specs=P(None, None, "space", "chan"), check_vma=False
    )
```

```python
import functools

import jax
import jax.numpy as jnp
from jax import lax
from jax.experimental import pallas as pl
from jax.experimental.pallas import tpu as pltpu
from jax.experimental.layout import Layout, with_layout_constraint
from jax.sharding import PartitionSpec as P

CH = 512
GROUPS = 32
MESH = pl.DeviceIdType.MESH

epsilon = 1e-06


def gather_kernel(n, x_ref, cache_ref, frames_ref, o_ref, left_ref, right_ref,
                  buf, left_buf, right_buf, send_sem, recv_sem, edge_send, edge_recv):
    me = lax.axis_index("space")
    ch = lax.axis_index("chan")
    right = lax.rem(me + 1, n)
    left = lax.rem(me + n - 1, n)
    barrier = pltpu.get_barrier_semaphore()

    def signal(k, carry):
        peer = lax.rem(me + k, n)
        pl.semaphore_signal(barrier, 1, device_id=(peer, ch), device_id_type=MESH)
        return carry

    lax.fori_loop(1, n, signal, 0)
    pl.semaphore_wait(barrier, n - 1)

    ncache = cache_ref.shape[0]
    last = cache_ref.shape[1] - 1
    edges = []
    for k, (src, lo_row) in enumerate(((cache_ref, 0), (frames_ref, ncache))):
        rows = pl.ds(lo_row, src.shape[0])
        edges.append(pltpu.make_async_remote_copy(
            src_ref=src.at[:, last], dst_ref=left_buf.at[rows], send_sem=edge_send.at[k],
            recv_sem=edge_recv.at[k], device_id=(right, ch), device_id_type=MESH))
        edges.append(pltpu.make_async_remote_copy(
            src_ref=src.at[:, 0], dst_ref=right_buf.at[rows], send_sem=edge_send.at[2 + k],
            recv_sem=edge_recv.at[2 + k], device_id=(left, ch), device_id_type=MESH))
    for cp in edges:
        cp.start()

    def copy_to(peer):
        return pltpu.make_async_remote_copy(
            src_ref=x_ref,
            dst_ref=buf.at[me],
            send_sem=send_sem.at[peer],
            recv_sem=recv_sem.at[me],
            device_id=(peer, ch),
            device_id_type=MESH,
        )

    def copy_from(peer):
        return pltpu.make_async_remote_copy(
            src_ref=x_ref,
            dst_ref=buf.at[peer],
            send_sem=send_sem.at[peer],
            recv_sem=recv_sem.at[peer],
            device_id=(peer, ch),
            device_id_type=MESH,
        )

    def start(k, carry):
        copy_to(lax.rem(me + k, n)).start()
        return carry

    lax.fori_loop(1, n, start, 0)

    def finish(k, carry):
        peer = lax.rem(me + k, n)
        copy_to(peer).wait_send()
        copy_from(peer).wait_recv()
        return carry

    lax.fori_loop(1, n, finish, 0)
    buf[me] = x_ref[...]
    o_ref[...] = buf[...]
    for cp in edges:
        cp.wait()
    left_ref[...] = left_buf[...]
    right_ref[...] = right_buf[...]


def gather_space(tile, cache_t, frames_t):
    n = lax.axis_size("space")
    vmem = pl.BlockSpec(memory_space=pltpu.VMEM)
    hbm = pl.BlockSpec(memory_space=pl.ANY)
    edge = (cache_t.shape[0] + frames_t.shape[0],) + cache_t.shape[2:]
    return pl.pallas_call(
        functools.partial(gather_kernel, n),
        out_shape=(
            jax.ShapeDtypeStruct((n,) + tile.shape, tile.dtype),
            jax.ShapeDtypeStruct(edge, cache_t.dtype),
            jax.ShapeDtypeStruct(edge, cache_t.dtype),
        ),
        in_specs=[vmem, hbm, hbm],
        out_specs=(vmem, vmem, vmem),
        scratch_shapes=[
            pltpu.VMEM((n,) + tile.shape, tile.dtype),
            pltpu.VMEM(edge, cache_t.dtype),
            pltpu.VMEM(edge, cache_t.dtype),
            pltpu.SemaphoreType.DMA((n,)),
            pltpu.SemaphoreType.DMA((n,)),
            pltpu.SemaphoreType.DMA((4,)),
            pltpu.SemaphoreType.DMA((4,)),
        ],
        compiler_params=pltpu.CompilerParams(collective_id=0, has_side_effects=True),
    )(tile, cache_t, frames_t)


def scatter_kernel(widths, x_ref, o_ref, recv1, acc1, own, recv2, acc2, recv3,
                   sem1s, sem1r, sem2s, sem2r, sem3s, sem3r):
    sp = lax.axis_index("space")
    c = lax.axis_index("chan")
    core = c % 2
    yh = (c // 2) % 2
    xx = c // 4
    nx, nyh = x_ref.shape[0], x_ref.shape[1]
    nchunk = len(widths)
    starts = [sum(widths[:q]) for q in range(nchunk)]
    f32, bf16 = jnp.float32, jnp.bfloat16

    def dev(x_, yh_, core_):
        return (sp, x_ * 4 + yh_ * 2 + core_)

    peers = [dev(xx, yh, 1 - core)]
    peers += [dev(lax.rem(xx + k, nx), yh, core) for k in range(1, nx)]
    peers += [dev(xx, 1 - yh, core)]
    barrier = pltpu.get_barrier_semaphore()
    for p in peers:
        pl.semaphore_signal(barrier, 1, device_id=p, device_id_type=MESH)
    pl.semaphore_wait(barrier, len(peers))

    def cols(q):
        return pl.ds(starts[q], widths[q])

    def fit(q):
        return pl.ds(0, widths[q])

    firsts = []
    for q in range(nchunk):
        for i in range(nx):
            for j in range(nyh):
                n = (q * nx + i) * nyh + j
                cp = pltpu.make_async_remote_copy(
                    src_ref=x_ref.at[i, j, 1 - core, :, cols(q)], dst_ref=recv1.at[q, i, j, :, fit(q)],
                    send_sem=sem1s.at[n], recv_sem=sem1r.at[n],
                    device_id=peers[0], device_id_type=MESH)
                cp.start()
                firsts.append(cp)

    def second(q):
        for cp in firsts[q * nx * nyh : (q + 1) * nx * nyh]:
            cp.wait()
        sends = []
        for k in range(1, nx):
            dest = lax.rem(xx + k, nx)
            for j in range(nyh):
                acc1[q, dest, j, :, fit(q)] = (
                    x_ref[dest, j, core, :, cols(q)] + recv1[q, dest, j, :, fit(q)]
                ).astype(bf16)
            slot = nx - 1 - k
            cp = pltpu.make_async_remote_copy(
                src_ref=acc1.at[q, dest, :, :, fit(q)], dst_ref=recv2.at[q, slot, :, :, fit(q)],
                send_sem=sem2s.at[q * (nx - 1) + k - 1], recv_sem=sem2r.at[q * (nx - 1) + slot],
                device_id=peers[k], device_id_type=MESH)
            cp.start()
            sends.append(cp)
        for j in range(nyh):
            own[q, j, :, fit(q)] = x_ref[xx, j, core, :, cols(q)] + recv1[q, xx, j, :, fit(q)]
        return sends

    def third(q):
        for slot in range(nx - 1):
            pltpu.make_async_remote_copy(
                src_ref=acc1.at[q, xx, :, :, fit(q)], dst_ref=recv2.at[q, slot, :, :, fit(q)],
                send_sem=sem2s.at[q * (nx - 1) + slot], recv_sem=sem2r.at[q * (nx - 1) + slot],
                device_id=peers[0], device_id_type=MESH).wait_recv()
        other = 1 - yh
        total = own[q, other, :, fit(q)]
        for slot in range(nx - 1):
            total = total + recv2[q, slot, other, :, fit(q)].astype(f32)
        acc2[q, :, fit(q)] = total.astype(bf16)
        cp = pltpu.make_async_remote_copy(
            src_ref=acc2.at[q, :, fit(q)], dst_ref=recv3.at[q, :, fit(q)], send_sem=sem3s.at[q],
            recv_sem=sem3r.at[q], device_id=peers[nx], device_id_type=MESH)
        cp.start()
        total = own[q, yh, :, fit(q)]
        for slot in range(nx - 1):
            total = total + recv2[q, slot, yh, :, fit(q)].astype(f32)
        own[q, yh, :, fit(q)] = total
        return cp

    seconds, lasts = [], []
    for q in range(nchunk):
        seconds.append(second(q))
        if q >= 1:
            lasts.append(third(q - 1))
    lasts.append(third(nchunk - 1))
    for sends in seconds:
        for cp in sends:
            cp.wait_send()
    for q, cp in enumerate(lasts):
        cp.wait()
        o_ref[:, cols(q)] = own[q, yh, :, fit(q)] + recv3[q, :, fit(q)].astype(f32)


def scatter_chan(parts, widths=(512, 896, 512)):
    nx, nyh, ncore, rows, cells = parts.shape
    nchunk, width = len(widths), max(widths)
    assert sum(widths) == cells
    f32, bf16 = jnp.float32, jnp.bfloat16
    return pl.pallas_call(
        functools.partial(scatter_kernel, widths),
        out_shape=jax.ShapeDtypeStruct((rows, cells), f32),
        in_specs=[pl.BlockSpec(memory_space=pltpu.VMEM)],
        out_specs=pl.BlockSpec(memory_space=pltpu.VMEM),
        scratch_shapes=[
            pltpu.VMEM((nchunk, nx, nyh, rows, width), f32),
            pltpu.VMEM((nchunk, nx, nyh, rows, width), bf16),
            pltpu.VMEM((nchunk, nyh, rows, width), f32),
            pltpu.VMEM((nchunk, nx - 1, nyh, rows, width), bf16),
            pltpu.VMEM((nchunk, rows, width), bf16),
            pltpu.VMEM((nchunk, rows, width), bf16),
            pltpu.SemaphoreType.DMA((nchunk * nx * nyh,)),
            pltpu.SemaphoreType.DMA((nchunk * nx * nyh,)),
            pltpu.SemaphoreType.DMA((nchunk * (nx - 1),)),
            pltpu.SemaphoreType.DMA((nchunk * (nx - 1),)),
            pltpu.SemaphoreType.DMA((nchunk,)),
            pltpu.SemaphoreType.DMA((nchunk,)),
        ],
        compiler_params=pltpu.CompilerParams(
            collective_id=1, has_side_effects=True, vmem_limit_bytes=48 * 1024 * 1024),
    )(parts)


def local(frames, cache, gamma, beta, kernel, bias):
    nframes, row_count, col_count, local_ch = frames.shape
    ncache = cache.shape[0]
    group_size = CH // GROUPS
    local_groups = local_ch // group_size
    nspace = lax.axis_size("space")
    me = lax.axis_index("space")
    local_members = float(nframes * row_count * col_count * group_size)


    values = frames.astype(jnp.float32).reshape(
        nframes, row_count, col_count, local_groups, group_size
    )
    local_mean = jnp.sum(values, axis=(0, 1, 2, 4)) / local_members
    local_dev = values - local_mean[:, None]
    local_m2 = jnp.sum(local_dev * local_dev, axis=(0, 1, 2, 4))
    tile = jnp.zeros((8, 128), jnp.float32)
    tile = tile.at[0, :local_groups].set(local_mean).at[1, :local_groups].set(local_m2)
    gathered, before, after = gather_space(
        tile, cache.transpose(0, 2, 3, 1), frames.transpose(0, 2, 3, 1)
    )
    before = before.transpose(0, 2, 1)[:, :, None]
    after = after.transpose(0, 2, 1)[:, :, None]
    means = gathered[:, 0, :local_groups]
    m2s = gathered[:, 1, :local_groups]
    group_mean = jnp.mean(means, axis=0)
    spread = jnp.sum(m2s, axis=0) + local_members * jnp.sum(
        (means - group_mean) ** 2, axis=0
    )
    group_var = spread / (local_members * nspace)
    inv = lax.rsqrt(group_var + epsilon)

    def activate(x):
        shape = x.shape
        v = x.astype(jnp.float32).reshape(shape[:-1] + (local_groups, group_size))
        scaled = (v - group_mean[:, None]) * inv[:, None]
        normed = scaled.reshape(shape) * gamma + beta
        return jax.nn.silu(normed).astype(jnp.bfloat16)

    active = activate(frames)
    joined = jnp.concatenate([cache, active], axis=0)
    left = jnp.concatenate([before[:ncache], activate(before[ncache:])], axis=0)
    right = jnp.concatenate([after[:ncache], activate(after[ncache:])], axis=0)
    left = jnp.where(me == 0, jnp.zeros_like(left), left)
    right = jnp.where(me == nspace - 1, jnp.zeros_like(right), right)
    bordered = jnp.concatenate([left, joined, right], axis=2)
    bordered = jnp.pad(bordered, ((0, 0), (1, 1), (0, 0), (0, 0)))
    cell_count = nframes * row_count * col_count
    bordered = bordered.transpose(0, 2, 1, 3)
    rows_in = jnp.concatenate(
        [bordered[:, :, row_tap : row_tap + row_count, :] for row_tap in range(3)], axis=3
    )
    rows_in = with_layout_constraint(rows_in, Layout(major_to_minor=(0, 1, 2, 3)))
    columns_in = jnp.concatenate(
        [rows_in[:, col_tap : col_tap + col_count] for col_tap in range(3)], axis=3
    )
    columns_in = with_layout_constraint(columns_in, Layout(major_to_minor=(0, 1, 2, 3)))
    tap_width = columns_in.shape[3]
    nchan = lax.axis_size("chan")
    nx = nchan // 4
    flat_kernel = kernel.transpose(0, 2, 1, 3, 4).reshape(3, tap_width, kernel.shape[4])
    running = jnp.zeros((bias.shape[0] * nchan, cell_count), jnp.float32)
    plane = row_count * col_count
    flat_in = columns_in.reshape(columns_in.shape[0] * plane, tap_width)
    for depth in range(3):
        tap_weight = flat_kernel[depth]
        window = flat_in[depth * plane : depth * plane + cell_count]
        running = running + lax.dot_general(
            tap_weight, window, (((0,), (1,)), ((), ())), preferred_element_type=jnp.float32
        )
    summed = scatter_chan(running.reshape(nx, 2, 2, local_ch, cell_count))
    result = summed.T + bias
    result = result.astype(jnp.bfloat16).reshape(nframes, col_count, row_count, -1)
    return result.transpose(0, 2, 1, 3)


def solution(mesh):
    placed = (
        P(None, None, "space", "chan"),
        P(None, None, "space", "chan"),
        P("chan"),
        P("chan"),
        P(None, None, None, "chan", None),
        P("chan"),
    )
    return jax.shard_map(
        local, mesh=mesh, in_specs=placed, out_specs=P(None, None, "space", "chan"), check_vma=False
    )
```
